256 devices in a mesh: seq: 32 (over z, x), head: 2 (over y_hi), batch: 4 (over y_lo, core).
Axes of the slice: x: 4, y: 4 (y_hi: 2, y_lo: 2; y = y_hi * 2 + y_lo), z: 8, core: 2. Of those that a mesh axis runs over, the one named last changes fastest.
Arguments:
- query: bfloat16 [8, 32, 128, 32, 128], P('batch', 'seq', None, 'head'), parts along dimension 0, may hold values from -6 to 6
- keys: bfloat16 [8, 32, 128, 8, 128], P('batch', 'seq', None, 'head'), parts along dimension 0, may hold values from -6 to 6
- values: bfloat16 [8, 32, 128, 8, 128], P('batch', 'seq', None, 'head'), parts along dimension 0, may hold values from -6 to 6
- grad_out: bfloat16 [8, 32, 128, 32, 128], P('batch', 'seq', None, 'head'), parts along dimension 0, may hold values from -6 to 6
- doc_starts: int32 [16384], P('batch'), parts along dimension 0, may hold values from 0 to 8192, as said below
Outputs:
- attended: bfloat16 [8, 32, 128, 32, 128], P('batch', 'seq', None, 'head'), parts along dimension 0
- grad_query: bfloat16 [8, 32, 128, 32, 128], P('batch', 'seq', None, 'head'), parts along dimension 0
- grad_keys: bfloat16 [8, 32, 128, 8, 128], P('batch', 'seq', None, 'head'), parts along dimension 0
- grad_values: bfloat16 [8, 32, 128, 8, 128], P('batch', 'seq', None, 'head'), parts along dimension 0
The draws below stay inside these ranges and needn't reach their ends.
There are 4 independent parts, one for each index of `batch`. The reference program is written for one: setup_inputs(seed, part) draws one part's arguments, and reference() takes and returns one part's arrays. A program takes and returns all parts, laid end to end along the dimension named above; each array names one. Nothing has to cross between parts.
Inputs may be any that keep to these rules, and one draw needn't show every extreme that they name: `doc_starts`: entry 0 is 0; entries rise with differences of 2 to 2048 until an entry reaches 8192, and every later entry equals 8192; one difference is exactly 2048. So every document has at most 2048 tokens.
All inputs are finite; a program needn't handle non-finite values.
Results may differ from the reference program's by a relative error of at most 0.0065.
Values may be sent and summed in bfloat16 or wider, within the bound.
A program may use at most 128 MiB of HBM per device.

```python
import jax
import jax.numpy as jnp
from jax import lax

QUERY_HEADS = 32
KEY_VALUE_HEADS = 8
HEAD_WIDTH = 128
SPAN_TOKENS = 128
WINDOW = 16
N_SEQ = 32


def doc_bounds(key):
    sequence_length = 2 * SPAN_TOKENS * N_SEQ
    longest = WINDOW * SPAN_TOKENS
    count = sequence_length // 2
    bits = jax.random.randint(jax.random.fold_in(key, 15), (count,), 1, longest.bit_length())
    limits = jnp.minimum(jnp.left_shift(jnp.ones((count,), jnp.int32), bits), longest)
    lengths = jax.random.randint(jax.random.fold_in(key, 11), (count,), 2, limits + 1)
    chosen = jax.random.randint(jax.random.fold_in(key, 12), (), 0, 4)
    lengths = jnp.where(jnp.arange(count) == chosen, longest, lengths).astype(jnp.int32)
    ends = jnp.cumsum(lengths).astype(jnp.int32)
    starts = jnp.concatenate([jnp.zeros((1,), jnp.int32), ends[:-1]])
    return jnp.minimum(starts, sequence_length).astype(jnp.int32)


def mirror_layout(full):
    spans = full.reshape((2 * N_SEQ, SPAN_TOKENS) + full.shape[1:])
    return jnp.stack([spans[:N_SEQ], spans[N_SEQ:][::-1]], axis=0)


def draw_query(key, part):
    sequence_length = 2 * SPAN_TOKENS * N_SEQ
    base_offset = jnp.clip(jax.random.normal(jax.random.fold_in(key, 21), (sequence_length, QUERY_HEADS, HEAD_WIDTH), jnp.float32), -6.0, 6.0)
    return mirror_layout(base_offset).astype(jnp.bfloat16)


def draw_keys(key, part):
    sequence_length = 2 * SPAN_TOKENS * N_SEQ
    base_offset = jnp.clip(jax.random.normal(jax.random.fold_in(key, 22), (sequence_length, KEY_VALUE_HEADS, HEAD_WIDTH), jnp.float32), -6.0, 6.0)
    return mirror_layout(base_offset).astype(jnp.bfloat16)


def draw_doc_starts(key, part):
    return doc_bounds(key)


def level_of(own_key, dims, cuts, smallest, largest):
    def one(position, blocks):
        steps = jax.random.uniform(jax.random.fold_in(jax.random.fold_in(own_key, 6), position), (blocks,), jnp.float32, smallest / len(cuts), largest / len(cuts))
        return jnp.repeat(jnp.exp(steps), dims[position] // blocks).reshape((-1,) + (1,) * (len(dims) - position - 1))

    gain = one(*cuts[0])
    for cut in cuts[1:]:
        gain = gain * one(*cut)
    return gain


def centred(own_key, shape, spread, most, cuts=(), kind=jnp.bfloat16):
    result = spread * jax.random.normal(own_key, shape, jnp.float32)
    if cuts:
        result = result * level_of(own_key, shape, cuts, -0.22, 0.18)
    return jnp.clip(result, -most, most).astype(kind)


def setup_inputs(seed: int = 0, part: int = 0) -> dict:
    seeds = jax.random.split(jax.random.key(seed), 6)
    part_splits = jax.random.split(jax.random.fold_in(seeds[5], part), 6)
    return {
        "query": draw_query(jax.random.fold_in(jax.random.fold_in(seeds[5], part), 71), part),
        "keys": draw_keys(jax.random.fold_in(jax.random.fold_in(seeds[5], part), 71), part),
        "values": centred(part_splits[2], (2, N_SEQ, SPAN_TOKENS, KEY_VALUE_HEADS, HEAD_WIDTH), 1.0, 6.0, ((1, 32), (3, 2))),
        "grad_out": centred(part_splits[3], (2, N_SEQ, SPAN_TOKENS, QUERY_HEADS, HEAD_WIDTH), 1.0, 6.0, ((1, 32), (3, 2))),
        "doc_starts": draw_doc_starts(jax.random.fold_in(jax.random.fold_in(seeds[5], part), 71), part),
    }


def in_order(array):
    return jnp.concatenate([array[0], array[1][::-1]], axis=0)


def mirrored(array):
    half_count = array.shape[0] // 2
    return jnp.stack([array[:half_count], array[half_count:][::-1]], axis=0)


def doc_index(doc_starts, positions):
    return jnp.searchsorted(doc_starts, positions, side="right").astype(jnp.int32) - 1


def head_terms(pieces, allowed, score_scale):
    query_wide = pieces[0].astype(jnp.float32)
    key_wide = pieces[1].astype(jnp.float32)
    value_wide = pieces[2].astype(jnp.float32)
    grad_wide = pieces[3].astype(jnp.float32)
    scores = jnp.einsum("rgd,jd->grj", query_wide, key_wide) * score_scale
    scores = jnp.where(allowed[None], scores, -jnp.inf)
    top_score = jnp.max(scores, axis=-1, keepdims=True)
    expons = jnp.exp(scores - top_score)
    weights = expons / jnp.sum(expons, axis=-1, keepdims=True)
    weights_low = weights.astype(jnp.bfloat16)
    weights_wide = weights_low.astype(jnp.float32)
    attended = jnp.einsum("grj,jd->rgd", weights_wide, value_wide).astype(jnp.bfloat16)
    grad_weights = jnp.einsum("rgd,jd->grj", grad_wide, value_wide)
    delta = jnp.transpose(jnp.sum(grad_wide * attended.astype(jnp.float32), axis=-1), (1, 0))
    grad_scores = (weights * (grad_weights - delta[..., None]) * score_scale).astype(jnp.bfloat16)
    grad_scores_wide = grad_scores.astype(jnp.float32)
    grad_query = jnp.einsum("grj,jd->rgd", grad_scores_wide, key_wide).astype(jnp.bfloat16)
    grad_keys = jnp.einsum("grj,rgd->jd", grad_scores_wide, query_wide)
    grad_values = jnp.einsum("grj,rgd->jd", weights_wide, grad_wide)
    return attended, grad_query, grad_keys, grad_values


def reference(query, keys, values, grad_out, doc_starts):
    query_ord = in_order(query)
    keys_ord = in_order(keys)
    values_ord = in_order(values)
    grad_ord = in_order(grad_out)
    span_count, span_len, head_count, head_dim = query_ord.shape
    kv_heads = keys_ord.shape[2]
    group_size = head_count // kv_heads
    score_scale = head_dim ** -0.5
    window = WINDOW
    key_count = (window + 1) * span_len
    keys_pad = jnp.concatenate([jnp.zeros((window,) + keys_ord.shape[1:], keys_ord.dtype), keys_ord], axis=0)
    values_pad = jnp.concatenate([jnp.zeros((window,) + values_ord.shape[1:], values_ord.dtype), values_ord], axis=0)

    def one_span(totals, pieces):
        key_total, value_total = totals
        queries, grad_output, span_idx = pieces
        token_pos = span_idx * span_len + jnp.arange(span_len, dtype=jnp.int32)
        key_pos = (span_idx - window) * span_len + jnp.arange(key_count, dtype=jnp.int32)
        query_doc = doc_index(doc_starts, token_pos)
        key_doc = doc_index(doc_starts, key_pos)
        allowed = (query_doc[:, None] == key_doc[None, :]) & (key_pos[None, :] <= token_pos[:, None])
        key_window = lax.dynamic_slice_in_dim(keys_pad, span_idx, window + 1, 0).reshape(key_count, kv_heads, head_dim)
        value_window = lax.dynamic_slice_in_dim(values_pad, span_idx, window + 1, 0).reshape(key_count, kv_heads, head_dim)
        query_heads = jnp.transpose(queries.reshape(span_len, kv_heads, group_size, head_dim), (1, 0, 2, 3))
        grad_heads = jnp.transpose(grad_output.reshape(span_len, kv_heads, group_size, head_dim), (1, 0, 2, 3))
        attended, grad_query, grad_keys, grad_values = lax.map(
            lambda parts: head_terms(parts, allowed, score_scale),
            (query_heads, jnp.transpose(key_window, (1, 0, 2)), jnp.transpose(value_window, (1, 0, 2)), grad_heads))
        key_terms = jnp.transpose(grad_keys, (1, 0, 2)).reshape(window + 1, span_len, kv_heads, head_dim)
        value_terms = jnp.transpose(grad_values, (1, 0, 2)).reshape(window + 1, span_len, kv_heads, head_dim)
        key_total = lax.dynamic_update_slice_in_dim(
            key_total, lax.dynamic_slice_in_dim(key_total, span_idx, window + 1, 0) + key_terms, span_idx, 0)
        value_total = lax.dynamic_update_slice_in_dim(
            value_total, lax.dynamic_slice_in_dim(value_total, span_idx, window + 1, 0) + value_terms, span_idx, 0)
        attended = jnp.transpose(attended, (1, 0, 2, 3)).reshape(span_len, head_count, head_dim)
        grad_query = jnp.transpose(grad_query, (1, 0, 2, 3)).reshape(span_len, head_count, head_dim)
        return (key_total, value_total), (attended, grad_query)

    zero_total = jnp.zeros((window + span_count, span_len, kv_heads, head_dim), jnp.float32)
    totals, outputs = lax.scan(one_span, (zero_total, zero_total),
                               (query_ord, grad_ord, jnp.arange(span_count, dtype=jnp.int32)))
    grad_keys = totals[0][window:].astype(jnp.bfloat16)
    grad_values = totals[1][window:].astype(jnp.bfloat16)
    return (mirrored(outputs[0]), mirrored(outputs[1]), mirrored(grad_keys), mirrored(grad_values))
```

```python
import functools

import jax
import jax.numpy as jnp
from jax import lax
from jax.sharding import PartitionSpec as P

from jax.experimental import pallas as pl
from jax.experimental.pallas import tpu as pltpu

ROUNDS = 16


def greet_neighbours(me, count):
    barrier = pltpu.get_barrier_semaphore()

    @pl.when(me > 0)
    def _():
        pl.semaphore_signal(barrier, 1, device_id={"seq": me - 1})

    @pl.when(me < count - 1)
    def _():
        pl.semaphore_signal(barrier, 1, device_id={"seq": me + 1})

    @pl.when(jnp.logical_and(me > 0, me < count - 1))
    def _():
        pl.semaphore_wait(barrier, 2)

    @pl.when(jnp.logical_or(me == 0, me == count - 1))
    def _():
        pl.semaphore_wait(barrier, 1)


def forward_chain_kernel(count, cur, hist, send_sem, recv_sem, local_sem):
    me = lax.axis_index("seq")
    greet_neighbours(me, count)
    for k in range(1, ROUNDS + 1):
        slot = ROUNDS - k
        src_a = cur.at[0] if k == 1 else hist.at[slot + 1, 0]
        src_b = cur.at[1] if k == 1 else hist.at[slot + 1, 1]
        send_a = pltpu.make_async_remote_copy(
            src_a, hist.at[slot, 0], send_sem.at[slot, 0], recv_sem.at[slot, 0],
            device_id={"seq": me + 1})
        send_b = pltpu.make_async_remote_copy(
            src_b, hist.at[slot, 1], send_sem.at[slot, 1], recv_sem.at[slot, 1],
            device_id={"seq": me - 1})
        local_b = pltpu.make_async_copy(src_a, hist.at[slot, 1], local_sem.at[slot])
        a_sends = jnp.logical_and(me < count - 1, me >= k - 1)
        a_gets = me >= k
        b_sends = me > 0
        b_gets = me < count - 1
        pl.when(a_sends)(send_a.start)
        pl.when(b_sends)(send_b.start)
        pl.when(me == count - 1)(local_b.start)

        @pl.when(jnp.logical_not(a_gets))
        def _():
            hist[slot, 0] = jnp.zeros(hist.shape[2:], hist.dtype)

        pl.when(a_gets)(send_a.wait_recv)
        pl.when(b_gets)(send_b.wait_recv)
        pl.when(me == count - 1)(local_b.wait)
        pl.when(a_sends)(send_a.wait_send)
        pl.when(b_sends)(send_b.wait_send)


def backward_chain_kernel(count, terms, out, send_buf, recv_buf, send_sem, recv_sem, local_sem):
    me = lax.axis_index("seq")
    greet_neighbours(me, count)
    send_buf[0] = terms[0].astype(send_buf.dtype)
    for t in range(1, ROUNDS + 1):
        slot = t - 1
        send_a = pltpu.make_async_remote_copy(
            send_buf.at[slot, 0], recv_buf.at[slot, 0], send_sem.at[slot, 0], recv_sem.at[slot, 0],
            device_id={"seq": me - 1})
        send_b = pltpu.make_async_remote_copy(
            send_buf.at[slot, 1], recv_buf.at[slot, 1], send_sem.at[slot, 1], recv_sem.at[slot, 1],
            device_id={"seq": me + 1})
        local_b = pltpu.make_async_copy(send_buf.at[slot, 1], recv_buf.at[slot, 0], local_sem.at[slot])
        pl.when(me > 0)(send_a.start)
        pl.when(me < count - 1)(send_b.start)
        pl.when(me == count - 1)(local_b.start)
        pl.when(me < count - 1)(send_a.wait_recv)
        pl.when(me == count - 1)(local_b.wait)
        pl.when(me > 0)(send_b.wait_recv)
        pl.when(me > 0)(send_a.wait_send)
        pl.when(me < count - 1)(send_b.wait_send)
        total_a = recv_buf[slot, 0].astype(jnp.float32) + terms[t, 0]

        @pl.when(me > 0)
        def _():
            total_b = recv_buf[slot, 1].astype(jnp.float32) + terms[t, 1]
            if t < ROUNDS:
                send_buf[t, 1] = total_b.astype(send_buf.dtype)
            else:
                out[1] = total_b.astype(out.dtype)

        @pl.when(me == 0)
        def _():
            total_b = terms[t, 1]
            if t < ROUNDS:
                send_buf[t, 1] = total_b.astype(send_buf.dtype)
            else:
                out[1] = total_b.astype(out.dtype)

        if t < ROUNDS:
            send_buf[t, 0] = total_a.astype(send_buf.dtype)
        else:
            out[0] = total_a.astype(out.dtype)


def forward_chain(current, count):
    shape = current.shape
    return pl.pallas_call(
        functools.partial(forward_chain_kernel, count),
        out_shape=jax.ShapeDtypeStruct((ROUNDS,) + shape, current.dtype),
        in_specs=[pl.BlockSpec(memory_space=pltpu.VMEM)],
        out_specs=pl.BlockSpec(memory_space=pltpu.VMEM),
        scratch_shapes=[
            pltpu.SemaphoreType.DMA((ROUNDS, 2)),
            pltpu.SemaphoreType.DMA((ROUNDS, 2)),
            pltpu.SemaphoreType.DMA((ROUNDS,)),
        ],
        compiler_params=pltpu.CompilerParams(
            collective_id=0, has_side_effects=True, vmem_limit_bytes=48 * 1024 * 1024),
    )(current)


def backward_chain(terms, count):
    shape = terms.shape[1:]
    return pl.pallas_call(
        functools.partial(backward_chain_kernel, count),
        out_shape=jax.ShapeDtypeStruct(shape, jnp.bfloat16),
        in_specs=[pl.BlockSpec(memory_space=pltpu.VMEM)],
        out_specs=pl.BlockSpec(memory_space=pltpu.VMEM),
        scratch_shapes=[
            pltpu.VMEM((ROUNDS,) + shape, jnp.bfloat16),
            pltpu.VMEM((ROUNDS,) + shape, jnp.bfloat16),
            pltpu.SemaphoreType.DMA((ROUNDS, 2)),
            pltpu.SemaphoreType.DMA((ROUNDS, 2)),
            pltpu.SemaphoreType.DMA((ROUNDS,)),
        ],
        compiler_params=pltpu.CompilerParams(
            collective_id=1, has_side_effects=True, vmem_limit_bytes=60 * 1024 * 1024),
    )(terms)


def shifted(value, axis, steps):
    count = lax.axis_size(axis)
    initial, last = (max(0, -steps), min(count, count - steps))
    return lax.ppermute(value, axis, [(source, source + steps) for source in range(initial, last)])


def doc_index(doc_starts, positions, span_len):
    blocks = positions.reshape(-1, span_len)

    def count_block(block_pos):
        below = (doc_starts[None, :] <= block_pos[:, None]).astype(jnp.int32)
        return jnp.sum(below, axis=1) - 1

    return lax.map(count_block, blocks).reshape(-1)


def softmax_rows(scores, allowed):
    scores = jnp.where(allowed[None], scores, -jnp.inf)
    top_score = jnp.max(scores, axis=-1, keepdims=True)
    expons = jnp.exp(scores - top_score)
    return expons / jnp.sum(expons, axis=-1, keepdims=True)


def grad_of_scores(weights, grad_weights, grad_output, attended, score_scale):
    delta = jnp.sum(grad_output.astype(jnp.float32) * attended.astype(jnp.float32), axis=-1)
    delta = jnp.transpose(delta, (1, 0))
    return (weights * (grad_weights - delta[..., None]) * score_scale).astype(jnp.bfloat16)


def head_dense(pieces, allowed, score_scale):
    queries, key_window, value_window, grad_output = pieces
    scores = (
        jnp.einsum("rgd,jd->grj", queries, key_window, preferred_element_type=jnp.float32)
        * score_scale
    )
    weights = softmax_rows(scores, allowed)
    weights_low = weights.astype(jnp.bfloat16)
    attended = jnp.einsum(
        "grj,jd->rgd", weights_low, value_window, preferred_element_type=jnp.float32
    ).astype(jnp.bfloat16)
    grad_weights = jnp.einsum(
        "rgd,jd->grj", grad_output, value_window, preferred_element_type=jnp.float32
    )
    grad_scores = grad_of_scores(weights, grad_weights, grad_output, attended, score_scale)
    grad_query = jnp.einsum(
        "grj,jd->rgd", grad_scores, key_window, preferred_element_type=jnp.float32
    )
    grad_keys = jnp.einsum("grj,rgd->jd", grad_scores, queries, preferred_element_type=jnp.float32)
    grad_values = jnp.einsum(
        "grj,rgd->jd", weights_low, grad_output, preferred_element_type=jnp.float32
    )
    return (attended, grad_query.astype(jnp.bfloat16), grad_keys, grad_values)


def body(query, keys, values, grad_out, doc_starts):
    shard_count = lax.axis_size("seq")
    device_index = lax.axis_index("seq")
    window = min(16, shard_count // 2)
    span_len = query.shape[2]
    head_count = query.shape[3]
    kv_heads = keys.shape[3]
    head_dim = query.shape[4]
    group_size = head_count // kv_heads
    score_scale = head_dim ** (-0.5)
    current = jnp.stack([keys[:, 0], values[:, 0]], axis=1)

    flat = current.reshape(2, 2, span_len * kv_heads, head_dim)
    history = forward_chain(flat, shard_count).reshape((window,) + current.shape)
    row_ids = jnp.arange(span_len, dtype=jnp.int32)
    key_count = (window + 1) * span_len
    span_firsts = [device_index, 2 * shard_count - 1 - device_index]
    outputs = []
    query_grads = []
    term_list = []
    for half_idx in range(2):
        token_pos = span_firsts[half_idx] * span_len + row_ids
        key_pos = (span_firsts[half_idx] - window) * span_len + jnp.arange(
            key_count, dtype=jnp.int32
        )
        key_doc = doc_index(doc_starts, key_pos, span_len)
        query_doc = key_doc[window * span_len :]
        allowed = (query_doc[:, None] == key_doc[None, :]) & (
            key_pos[None, :] <= token_pos[:, None]
        )
        windows = jnp.concatenate([history[:, half_idx], current[half_idx][None]], axis=0)
        key_window = jnp.transpose(windows[:, 0].reshape(key_count, kv_heads, head_dim), (1, 0, 2))
        value_window = jnp.transpose(
            windows[:, 1].reshape(key_count, kv_heads, head_dim), (1, 0, 2)
        )
        queries = jnp.transpose(
            query[half_idx, 0].reshape(span_len, kv_heads, group_size, head_dim), (1, 0, 2, 3)
        )
        grad_output = jnp.transpose(
            grad_out[half_idx, 0].reshape(span_len, kv_heads, group_size, head_dim), (1, 0, 2, 3)
        )
        attended, grad_query, grad_keys, grad_values = lax.map(
            lambda parts: head_dense(parts, allowed, score_scale),
            (queries, key_window, value_window, grad_output),
        )
        outputs.append(
            jnp.transpose(attended, (1, 0, 2, 3)).reshape(span_len, head_count, head_dim)
        )
        query_grads.append(
            jnp.transpose(grad_query, (1, 0, 2, 3)).reshape(span_len, head_count, head_dim)
        )
        paired = jnp.stack([grad_keys, grad_values], axis=0).reshape(
            2, kv_heads, window + 1, span_len, head_dim
        )
        term_list.append(jnp.transpose(paired, (2, 0, 3, 1, 4)))
    term_all = jnp.stack(term_list, axis=1)

    term_flat = term_all.reshape(window + 1, 2, 2, span_len * kv_heads, head_dim)
    totals = backward_chain(term_flat, shard_count).reshape(term_all.shape[1:])
    grad_keys_out = totals[:, 0][:, None].astype(jnp.bfloat16)
    grad_values_out = totals[:, 1][:, None].astype(jnp.bfloat16)
    return (
        jnp.stack(outputs, axis=0)[:, None],
        jnp.stack(query_grads, axis=0)[:, None],
        grad_keys_out,
        grad_values_out,
    )


def solution(mesh):
    placed = (
        P("batch", "seq", None, "head", None),
        P("batch", "seq", None, "head", None),
        P("batch", "seq", None, "head", None),
        P("batch", "seq", None, "head", None),
        P("batch"),
    )
    return jax.shard_map(
        body,
        mesh=mesh,
        in_specs=placed,
        out_specs=(
            P("batch", "seq", None, "head", None),
            P("batch", "seq", None, "head", None),
            P("batch", "seq", None, "head", None),
            P("batch", "seq", None, "head", None),
        ),
        check_vma=False,
    )
```

```python
import functools

import jax
import jax.numpy as jnp
from jax import lax
from jax.sharding import PartitionSpec as P

from jax.experimental import pallas as pl
from jax.experimental.pallas import tpu as pltpu

ROUNDS = 16


def greet_neighbours(me, count):
    barrier = pltpu.get_barrier_semaphore()

    @pl.when(me > 0)
    def _():
        pl.semaphore_signal(barrier, 1, device_id={"seq": me - 1})

    @pl.when(me < count - 1)
    def _():
        pl.semaphore_signal(barrier, 1, device_id={"seq": me + 1})

    @pl.when(jnp.logical_and(me > 0, me < count - 1))
    def _():
        pl.semaphore_wait(barrier, 2)

    @pl.when(jnp.logical_or(me == 0, me == count - 1))
    def _():
        pl.semaphore_wait(barrier, 1)


def forward_chain_kernel(count, cur, hist, send_sem, recv_sem, local_sem):
    me = lax.axis_index("seq")
    own = pltpu.make_async_copy(cur, hist.at[ROUNDS], local_sem.at[ROUNDS])
    own.start()
    greet_neighbours(me, count)
    for k in range(1, ROUNDS + 1):
        slot = ROUNDS - k
        src_a = cur.at[0] if k == 1 else hist.at[slot + 1, 0]
        src_b = cur.at[1] if k == 1 else hist.at[slot + 1, 1]
        send_a = pltpu.make_async_remote_copy(
            src_a, hist.at[slot, 0], send_sem.at[slot, 0], recv_sem.at[slot, 0],
            device_id={"seq": me + 1})
        send_b = pltpu.make_async_remote_copy(
            src_b, hist.at[slot, 1], send_sem.at[slot, 1], recv_sem.at[slot, 1],
            device_id={"seq": me - 1})
        local_b = pltpu.make_async_copy(src_a, hist.at[slot, 1], local_sem.at[slot])
        a_sends = jnp.logical_and(me < count - 1, me >= k - 1)
        a_gets = me >= k
        b_sends = me > 0
        b_gets = me < count - 1
        pl.when(a_sends)(send_a.start)
        pl.when(b_sends)(send_b.start)
        pl.when(me == count - 1)(local_b.start)

        @pl.when(jnp.logical_not(a_gets))
        def _():
            hist[slot, 0] = jnp.zeros(hist.shape[2:], hist.dtype)

        pl.when(a_gets)(send_a.wait_recv)
        pl.when(b_gets)(send_b.wait_recv)
        pl.when(me == count - 1)(local_b.wait)
        pl.when(a_sends)(send_a.wait_send)
        pl.when(b_sends)(send_b.wait_send)
    own.wait()


def backward_chain_kernel(count, terms, out, send_buf, recv_buf, send_sem, recv_sem, local_sem):
    me = lax.axis_index("seq")
    greet_neighbours(me, count)
    send_buf[0] = terms[0].astype(send_buf.dtype)
    for t in range(1, ROUNDS + 1):
        slot = t - 1
        send_a = pltpu.make_async_remote_copy(
            send_buf.at[slot, 0], recv_buf.at[slot, 0], send_sem.at[slot, 0], recv_sem.at[slot, 0],
            device_id={"seq": me - 1})
        send_b = pltpu.make_async_remote_copy(
            send_buf.at[slot, 1], recv_buf.at[slot, 1], send_sem.at[slot, 1], recv_sem.at[slot, 1],
            device_id={"seq": me + 1})
        local_b = pltpu.make_async_copy(send_buf.at[slot, 1], recv_buf.at[slot, 0], local_sem.at[slot])
        pl.when(me > 0)(send_a.start)
        pl.when(me < count - 1)(send_b.start)
        pl.when(me == count - 1)(local_b.start)
        pl.when(me < count - 1)(send_a.wait_recv)
        pl.when(me == count - 1)(local_b.wait)
        pl.when(me > 0)(send_b.wait_recv)
        pl.when(me > 0)(send_a.wait_send)
        pl.when(me < count - 1)(send_b.wait_send)
        total_a = recv_buf[slot, 0].astype(jnp.float32) + terms[t, 0]

        @pl.when(me > 0)
        def _():
            total_b = recv_buf[slot, 1].astype(jnp.float32) + terms[t, 1]
            if t < ROUNDS:
                send_buf[t, 1] = total_b.astype(send_buf.dtype)
            else:
                out[1] = total_b.astype(out.dtype)

        @pl.when(me == 0)
        def _():
            total_b = terms[t, 1]
            if t < ROUNDS:
                send_buf[t, 1] = total_b.astype(send_buf.dtype)
            else:
                out[1] = total_b.astype(out.dtype)

        if t < ROUNDS:
            send_buf[t, 0] = total_a.astype(send_buf.dtype)
        else:
            out[0] = total_a.astype(out.dtype)


def forward_chain(current, count):
    shape = current.shape
    return pl.pallas_call(
        functools.partial(forward_chain_kernel, count),
        out_shape=jax.ShapeDtypeStruct((ROUNDS + 1,) + shape, current.dtype),
        in_specs=[pl.BlockSpec(memory_space=pltpu.VMEM)],
        out_specs=pl.BlockSpec(memory_space=pltpu.VMEM),
        scratch_shapes=[
            pltpu.SemaphoreType.DMA((ROUNDS, 2)),
            pltpu.SemaphoreType.DMA((ROUNDS, 2)),
            pltpu.SemaphoreType.DMA((ROUNDS + 1,)),
        ],
        compiler_params=pltpu.CompilerParams(
            collective_id=0, has_side_effects=True, vmem_limit_bytes=48 * 1024 * 1024),
    )(current)


def backward_chain(terms, count):
    shape = terms.shape[1:]
    return pl.pallas_call(
        functools.partial(backward_chain_kernel, count),
        out_shape=jax.ShapeDtypeStruct(shape, jnp.bfloat16),
        in_specs=[pl.BlockSpec(memory_space=pltpu.VMEM)],
        out_specs=pl.BlockSpec(memory_space=pltpu.VMEM),
        scratch_shapes=[
            pltpu.VMEM((ROUNDS,) + shape, jnp.bfloat16),
            pltpu.VMEM((ROUNDS,) + shape, jnp.bfloat16),
            pltpu.SemaphoreType.DMA((ROUNDS, 2)),
            pltpu.SemaphoreType.DMA((ROUNDS, 2)),
            pltpu.SemaphoreType.DMA((ROUNDS,)),
        ],
        compiler_params=pltpu.CompilerParams(
            collective_id=1, has_side_effects=True, vmem_limit_bytes=60 * 1024 * 1024),
    )(terms)


def attention_kernel(skip_ref, q_ref, do_ref, win_ref, qdoc_ref, kdoc_ref,
                     o_ref, dq_ref, terms_ref):
    stream = pl.program_id(0)
    first = skip_ref[stream]
    group, span_len, head_dim = q_ref.shape[1:]
    rows = group * span_len
    last = win_ref.shape[0] - 1
    scale = head_dim ** (-0.5)
    q = q_ref[0].reshape(rows, head_dim)
    grad_output = do_ref[0].reshape(rows, head_dim)
    query_doc = qdoc_ref[0]
    later = lax.broadcasted_iota(jnp.int32, (span_len, span_len), 1) > lax.broadcasted_iota(
        jnp.int32, (span_len, span_len), 0)
    contract_last = (((1,), (1,)), ((), ()))
    contract_first = (((0,), (0,)), ((), ()))

    def scores(j, causal):
        sc = lax.dot_general(q, win_ref[j, 0, 0, 0], contract_last,
                             preferred_element_type=jnp.float32) * scale
        allowed = query_doc == kdoc_ref[0, j]
        if causal:
            allowed = jnp.logical_and(allowed, jnp.logical_not(later))
        sc = jnp.where(allowed[None], sc.reshape(group, span_len, span_len), -jnp.inf)
        return sc.reshape(rows, span_len)

    sc = scores(last, True)
    top = jnp.max(sc, axis=1, keepdims=True)
    total = jnp.sum(jnp.exp(sc - top), axis=1, keepdims=True)

    def stat_step(j, carry):
        top, total = carry
        sc = scores(j, False)
        new_top = jnp.maximum(top, jnp.max(sc, axis=1, keepdims=True))
        total = total * jnp.exp(top - new_top) + jnp.sum(jnp.exp(sc - new_top), axis=1, keepdims=True)
        return new_top, total

    top, total = lax.fori_loop(first, last, stat_step, (top, total))
    inverse = 1.0 / total

    def weights(j, causal):
        return jnp.exp(scores(j, causal) - top) * inverse

    def out_step(j, acc, causal=False):
        low = weights(j, causal).astype(jnp.bfloat16)
        return acc + jnp.dot(low, win_ref[j, 0, 1, 0], preferred_element_type=jnp.float32)

    acc = out_step(last, jnp.zeros((rows, head_dim), jnp.float32), True)
    acc = lax.fori_loop(first, last, out_step, acc)
    attended = acc.astype(jnp.bfloat16)
    o_ref[0] = attended.reshape(group, span_len, head_dim)
    delta = jnp.sum(grad_output.astype(jnp.float32) * attended.astype(jnp.float32), axis=1, keepdims=True)

    def grad_step(j, dq, causal=False):
        prob = weights(j, causal)
        low = prob.astype(jnp.bfloat16)
        key_j = win_ref[j, 0, 0, 0]
        grad_w = lax.dot_general(grad_output, win_ref[j, 0, 1, 0], contract_last,
                                 preferred_element_type=jnp.float32)
        grad_s = (prob * (grad_w - delta) * scale).astype(jnp.bfloat16)
        terms_ref[j, 0, 0, 0] = lax.dot_general(grad_s, q, contract_first,
                                                preferred_element_type=jnp.float32)
        terms_ref[j, 0, 1, 0] = lax.dot_general(low, grad_output, contract_first,
                                                preferred_element_type=jnp.float32)
        return dq + jnp.dot(grad_s, key_j, preferred_element_type=jnp.float32)

    dq = grad_step(last, jnp.zeros((rows, head_dim), jnp.float32), True)
    dq = lax.fori_loop(first, last, grad_step, dq)
    dq_ref[0] = dq.astype(jnp.bfloat16).reshape(group, span_len, head_dim)

    def clear(j, carry):
        terms_ref[j] = jnp.zeros(terms_ref.shape[1:], terms_ref.dtype)
        return carry

    lax.fori_loop(0, first, clear, 0)


def attention(skip, q, grad_out, window, query_doc, key_doc, group):
    streams, heads, span_len, head_dim = q.shape
    kv_heads = heads // group
    spans = window.shape[0]
    head_block = pl.BlockSpec((1, group, span_len, head_dim), lambda s, h, sk: (s, h, 0, 0))
    return pl.pallas_call(
        attention_kernel,
        out_shape=(
            jax.ShapeDtypeStruct(q.shape, jnp.bfloat16),
            jax.ShapeDtypeStruct(q.shape, jnp.bfloat16),
            jax.ShapeDtypeStruct((spans, streams, 2, kv_heads, span_len, head_dim), jnp.float32),
        ),
        grid_spec=pltpu.PrefetchScalarGridSpec(
            num_scalar_prefetch=1,
            grid=(streams, kv_heads),
            in_specs=[
                head_block,
                head_block,
                pl.BlockSpec((spans, 1, 2, 1, span_len, head_dim), lambda s, h, sk: (0, s, 0, h, 0, 0)),
                pl.BlockSpec((1, span_len, 1), lambda s, h, sk: (s, 0, 0)),
                pl.BlockSpec((1, spans, 1, span_len), lambda s, h, sk: (s, 0, 0, 0)),
            ],
            out_specs=[
                head_block,
                head_block,
                pl.BlockSpec((spans, 1, 2, 1, span_len, head_dim), lambda s, h, sk: (0, s, 0, h, 0, 0)),
            ],
        ),
        compiler_params=pltpu.CompilerParams(vmem_limit_bytes=48 * 1024 * 1024),
    )(skip, q, grad_out, window, query_doc, key_doc)


def body(query, keys, values, grad_out, doc_starts):
    shard_count = lax.axis_size("seq")
    device_index = lax.axis_index("seq")
    window = ROUNDS
    span_len = query.shape[2]
    kv_heads = keys.shape[3]
    head_dim = query.shape[4]
    group = query.shape[3] // kv_heads
    q = jnp.transpose(query[:, 0], (0, 2, 1, 3))
    grad_o = jnp.transpose(grad_out[:, 0], (0, 2, 1, 3))
    current = jnp.stack([jnp.transpose(keys[:, 0], (0, 2, 1, 3)),
                         jnp.transpose(values[:, 0], (0, 2, 1, 3))], axis=1)
    flat = current.reshape(2, 2, kv_heads * span_len, head_dim)
    spans = forward_chain(flat, shard_count).reshape((window + 1,) + current.shape)
    span_firsts = jnp.stack([device_index, 2 * shard_count - 1 - device_index])
    key_pos = (span_firsts[:, None] - window) * span_len + jnp.arange(
        (window + 1) * span_len, dtype=jnp.int32)[None]
    key_doc = (jnp.searchsorted(doc_starts, key_pos, side="right") - 1).astype(jnp.int32)
    key_doc = key_doc.reshape(2, window + 1, span_len)
    query_doc = key_doc[:, window]
    skip = jnp.sum(key_doc[:, :window, span_len - 1] < query_doc[:, :1], axis=1).astype(jnp.int32)
    attended, grad_q, terms = attention(
        skip, q, grad_o, spans, query_doc[:, :, None], key_doc[:, :, None, :], group)
    term_flat = terms.reshape(window + 1, 2, 2, kv_heads * span_len, head_dim)
    totals = backward_chain(term_flat, shard_count).reshape(current.shape)
    grad_kv = jnp.transpose(totals, (1, 0, 3, 2, 4))[:, :, None]
    return (
        jnp.transpose(attended, (0, 2, 1, 3))[:, None],
        jnp.transpose(grad_q, (0, 2, 1, 3))[:, None],
        grad_kv[0],
        grad_kv[1],
    )


def solution(mesh):
    placed = (
        P("batch", "seq", None, "head", None),
        P("batch", "seq", None, "head", None),
        P("batch", "seq", None, "head", None),
        P("batch", "seq", None, "head", None),
        P("batch"),
    )
    return jax.shard_map(
        body,
        mesh=mesh,
        in_specs=placed,
        out_specs=(
            P("batch", "seq", None, "head", None),
            P("batch", "seq", None, "head", None),
            P("batch", "seq", None, "head", None),
            P("batch", "seq", None, "head", None),
        ),
        check_vma=False,
    )
```

```python
import functools

import jax
import jax.numpy as jnp
from jax import lax
from jax.sharding import PartitionSpec as P

from jax.experimental import pallas as pl
from jax.experimental.pallas import tpu as pltpu

ROUNDS = 16


def greet_neighbours(me, count):
    barrier = pltpu.get_barrier_semaphore()

    @pl.when(me > 0)
    def _():
        pl.semaphore_signal(barrier, 1, device_id={"seq": me - 1})

    @pl.when(me < count - 1)
    def _():
        pl.semaphore_signal(barrier, 1, device_id={"seq": me + 1})

    @pl.when(jnp.logical_and(me > 0, me < count - 1))
    def _():
        pl.semaphore_wait(barrier, 2)

    @pl.when(jnp.logical_or(me == 0, me == count - 1))
    def _():
        pl.semaphore_wait(barrier, 1)


def forward_chain_kernel(count, cur, hist, send_sem, recv_sem, local_sem):
    me = lax.axis_index("seq")
    own = pltpu.make_async_copy(cur, hist.at[ROUNDS], local_sem.at[ROUNDS])
    own.start()
    greet_neighbours(me, count)
    for k in range(1, ROUNDS + 1):
        slot = ROUNDS - k
        src_a = cur.at[0] if k == 1 else hist.at[slot + 1, 0]
        src_b = cur.at[1] if k == 1 else hist.at[slot + 1, 1]
        send_a = pltpu.make_async_remote_copy(
            src_a, hist.at[slot, 0], send_sem.at[slot, 0], recv_sem.at[slot, 0],
            device_id={"seq": me + 1})
        send_b = pltpu.make_async_remote_copy(
            src_b, hist.at[slot, 1], send_sem.at[slot, 1], recv_sem.at[slot, 1],
            device_id={"seq": me - 1})
        local_b = pltpu.make_async_copy(src_a, hist.at[slot, 1], local_sem.at[slot])
        a_sends = jnp.logical_and(me < count - 1, me >= k - 1)
        a_gets = me >= k
        b_sends = me > 0
        b_gets = me < count - 1
        pl.when(a_sends)(send_a.start)
        pl.when(b_sends)(send_b.start)
        pl.when(me == count - 1)(local_b.start)

        @pl.when(jnp.logical_not(a_gets))
        def _():
            hist[slot, 0] = jnp.zeros(hist.shape[2:], hist.dtype)

        pl.when(a_gets)(send_a.wait_recv)
        pl.when(b_gets)(send_b.wait_recv)
        pl.when(me == count - 1)(local_b.wait)
        pl.when(a_sends)(send_a.wait_send)
        pl.when(b_sends)(send_b.wait_send)
    own.wait()


def backward_chain_kernel(count, terms, out, send_buf, recv_buf, send_sem, recv_sem, local_sem):
    me = lax.axis_index("seq")
    greet_neighbours(me, count)
    send_buf[0] = terms[0].astype(send_buf.dtype)
    for t in range(1, ROUNDS + 1):
        slot = t - 1
        send_a = pltpu.make_async_remote_copy(
            send_buf.at[slot, 0], recv_buf.at[slot, 0], send_sem.at[slot, 0], recv_sem.at[slot, 0],
            device_id={"seq": me - 1})
        send_b = pltpu.make_async_remote_copy(
            send_buf.at[slot, 1], recv_buf.at[slot, 1], send_sem.at[slot, 1], recv_sem.at[slot, 1],
            device_id={"seq": me + 1})
        local_b = pltpu.make_async_copy(send_buf.at[slot, 1], recv_buf.at[slot, 0], local_sem.at[slot])
        pl.when(me > 0)(send_a.start)
        pl.when(me < count - 1)(send_b.start)
        pl.when(me == count - 1)(local_b.start)
        pl.when(me < count - 1)(send_a.wait_recv)
        pl.when(me == count - 1)(local_b.wait)
        pl.when(me > 0)(send_b.wait_recv)
        pl.when(me > 0)(send_a.wait_send)
        pl.when(me < count - 1)(send_b.wait_send)
        total_a = recv_buf[slot, 0].astype(jnp.float32) + terms[t, 0]

        @pl.when(me > 0)
        def _():
            total_b = recv_buf[slot, 1].astype(jnp.float32) + terms[t, 1]
            if t < ROUNDS:
                send_buf[t, 1] = total_b.astype(send_buf.dtype)
            else:
                out[1] = total_b.astype(out.dtype)

        @pl.when(me == 0)
        def _():
            total_b = terms[t, 1]
            if t < ROUNDS:
                send_buf[t, 1] = total_b.astype(send_buf.dtype)
            else:
                out[1] = total_b.astype(out.dtype)

        if t < ROUNDS:
            send_buf[t, 0] = total_a.astype(send_buf.dtype)
        else:
            out[0] = total_a.astype(out.dtype)


def forward_chain(current, count):
    shape = current.shape
    return pl.pallas_call(
        functools.partial(forward_chain_kernel, count),
        out_shape=jax.ShapeDtypeStruct((ROUNDS + 1,) + shape, current.dtype),
        in_specs=[pl.BlockSpec(memory_space=pltpu.VMEM)],
        out_specs=pl.BlockSpec(memory_space=pltpu.VMEM),
        scratch_shapes=[
            pltpu.SemaphoreType.DMA((ROUNDS, 2)),
            pltpu.SemaphoreType.DMA((ROUNDS, 2)),
            pltpu.SemaphoreType.DMA((ROUNDS + 1,)),
        ],
        compiler_params=pltpu.CompilerParams(
            collective_id=0, has_side_effects=True, vmem_limit_bytes=48 * 1024 * 1024),
    )(current)


def backward_chain(terms, count):
    shape = terms.shape[1:]
    return pl.pallas_call(
        functools.partial(backward_chain_kernel, count),
        out_shape=jax.ShapeDtypeStruct(shape, jnp.bfloat16),
        in_specs=[pl.BlockSpec(memory_space=pltpu.VMEM)],
        out_specs=pl.BlockSpec(memory_space=pltpu.VMEM),
        scratch_shapes=[
            pltpu.VMEM((ROUNDS,) + shape, jnp.bfloat16),
            pltpu.VMEM((ROUNDS,) + shape, jnp.bfloat16),
            pltpu.SemaphoreType.DMA((ROUNDS, 2)),
            pltpu.SemaphoreType.DMA((ROUNDS, 2)),
            pltpu.SemaphoreType.DMA((ROUNDS,)),
        ],
        compiler_params=pltpu.CompilerParams(
            collective_id=1, has_side_effects=True, vmem_limit_bytes=60 * 1024 * 1024),
    )(terms)


def attention_kernel(skip_ref, q_ref, do_ref, win_ref, qdoc_ref, kdoc_ref,
                     o_ref, dq_ref, terms_ref):
    stream = pl.program_id(0)
    first = skip_ref[stream]
    group, span_len, head_dim = q_ref.shape[1:]
    rows = group * span_len
    last = win_ref.shape[0] - 1
    scale = head_dim ** (-0.5)
    q = q_ref[0].reshape(rows, head_dim)
    grad_output = do_ref[0].reshape(rows, head_dim)
    query_doc = qdoc_ref[0]
    later = lax.broadcasted_iota(jnp.int32, (span_len, span_len), 1) > lax.broadcasted_iota(
        jnp.int32, (span_len, span_len), 0)
    contract_last = (((1,), (1,)), ((), ()))
    contract_first = (((0,), (0,)), ((), ()))

    def scores(j, causal):
        sc = lax.dot_general(q, win_ref[j, 0, 0, 0], contract_last,
                             preferred_element_type=jnp.float32) * scale
        allowed = query_doc == kdoc_ref[0, j]
        if causal:
            allowed = jnp.logical_and(allowed, jnp.logical_not(later))
        sc = jnp.where(allowed[None], sc.reshape(group, span_len, span_len), -jnp.inf)
        return sc.reshape(rows, span_len)

    sc = scores(last, True)
    top = jnp.max(sc, axis=1, keepdims=True)
    total = jnp.sum(jnp.exp(sc - top), axis=1, keepdims=True)

    def stat_step(j, carry):
        top, total = carry
        sc = scores(j, False)
        new_top = jnp.maximum(top, jnp.max(sc, axis=1, keepdims=True))
        total = total * jnp.exp(top - new_top) + jnp.sum(jnp.exp(sc - new_top), axis=1, keepdims=True)
        return new_top, total

    top, total = lax.fori_loop(first, last, stat_step, (top, total))
    inverse = 1.0 / total

    def weights(j, causal):
        return jnp.exp(scores(j, causal) - top) * inverse

    def out_step(j, acc, causal=False):
        low = weights(j, causal).astype(jnp.bfloat16)
        return acc + jnp.dot(low, win_ref[j, 0, 1, 0], preferred_element_type=jnp.float32)

    acc = out_step(last, jnp.zeros((rows, head_dim), jnp.float32), True)
    acc = lax.fori_loop(first, last, out_step, acc)
    attended = acc.astype(jnp.bfloat16)
    o_ref[0] = attended.reshape(group, span_len, head_dim)
    delta = jnp.sum(grad_output.astype(jnp.float32) * attended.astype(jnp.float32), axis=1, keepdims=True)

    def grad_step(j, dq, causal=False):
        prob = weights(j, causal)
        low = prob.astype(jnp.bfloat16)
        key_j = win_ref[j, 0, 0, 0]
        grad_w = lax.dot_general(grad_output, win_ref[j, 0, 1, 0], contract_last,
                                 preferred_element_type=jnp.float32)
        grad_s = (prob * (grad_w - delta) * scale).astype(jnp.bfloat16)
        terms_ref[j, 0, 0, 0] = lax.dot_general(grad_s, q, contract_first,
                                                preferred_element_type=jnp.float32)
        terms_ref[j, 0, 1, 0] = lax.dot_general(low, grad_output, contract_first,
                                                preferred_element_type=jnp.float32)
        return dq + jnp.dot(grad_s, key_j, preferred_element_type=jnp.float32)

    dq = grad_step(last, jnp.zeros((rows, head_dim), jnp.float32), True)
    dq = lax.fori_loop(first, last, grad_step, dq)
    dq_ref[0] = dq.astype(jnp.bfloat16).reshape(group, span_len, head_dim)

    def clear(j, carry):
        terms_ref[j] = jnp.zeros(terms_ref.shape[1:], terms_ref.dtype)
        return carry

    lax.fori_loop(0, first, clear, 0)


def attention(skip, q, grad_out, window, query_doc, key_doc, group):
    streams, heads, span_len, head_dim = q.shape
    kv_heads = heads // group
    spans = window.shape[0]
    head_block = pl.BlockSpec((1, group, span_len, head_dim), lambda s, h, sk: (s, h, 0, 0))
    return pl.pallas_call(
        attention_kernel,
        out_shape=(
            jax.ShapeDtypeStruct(q.shape, jnp.bfloat16),
            jax.ShapeDtypeStruct(q.shape, jnp.bfloat16),
            jax.ShapeDtypeStruct((spans, streams, 2, kv_heads, span_len, head_dim), jnp.float32),
        ),
        grid_spec=pltpu.PrefetchScalarGridSpec(
            num_scalar_prefetch=1,
            grid=(streams, kv_heads),
            in_specs=[
                head_block,
                head_block,
                pl.BlockSpec((spans, 1, 2, 1, span_len, head_dim), lambda s, h, sk: (0, s, 0, h, 0, 0)),
                pl.BlockSpec((1, span_len, 1), lambda s, h, sk: (s, 0, 0)),
                pl.BlockSpec((1, spans, 1, span_len), lambda s, h, sk: (s, 0, 0, 0)),
            ],
            out_specs=[
                head_block,
                head_block,
                pl.BlockSpec((spans, 1, 2, 1, span_len, head_dim), lambda s, h, sk: (0, s, 0, h, 0, 0)),
            ],
        ),
        compiler_params=pltpu.CompilerParams(vmem_limit_bytes=48 * 1024 * 1024),
    )(skip, q, grad_out, window, query_doc, key_doc)


def window_docs(doc_starts, key_pos):
    width = key_pos.shape[1]
    before = jnp.sum((doc_starts[None, :] < key_pos[:, :1]).astype(jnp.int32), axis=1)
    padded = jnp.concatenate(
        [doc_starts, jnp.full((width // 2,), jnp.iinfo(jnp.int32).max, doc_starts.dtype)])
    local = jnp.stack([lax.dynamic_slice_in_dim(padded, before[i], width // 2) for i in range(2)])
    inside = jnp.sum((local[:, None, :] <= key_pos[:, :, None]).astype(jnp.int32), axis=2)
    return before[:, None] + inside - 1


def body(query, keys, values, grad_out, doc_starts):
    shard_count = lax.axis_size("seq")
    device_index = lax.axis_index("seq")
    window = ROUNDS
    span_len = query.shape[2]
    kv_heads = keys.shape[3]
    head_dim = query.shape[4]
    group = query.shape[3] // kv_heads
    q = jnp.transpose(query[:, 0], (0, 2, 1, 3))
    grad_o = jnp.transpose(grad_out[:, 0], (0, 2, 1, 3))
    current = jnp.stack([jnp.transpose(keys[:, 0], (0, 2, 1, 3)),
                         jnp.transpose(values[:, 0], (0, 2, 1, 3))], axis=1)
    flat = current.reshape(2, 2, kv_heads * span_len, head_dim)
    spans = forward_chain(flat, shard_count).reshape((window + 1,) + current.shape)
    span_firsts = jnp.stack([device_index, 2 * shard_count - 1 - device_index])
    key_pos = (span_firsts[:, None] - window) * span_len + jnp.arange(
        (window + 1) * span_len, dtype=jnp.int32)[None]
    key_doc = window_docs(doc_starts, key_pos)
    key_doc = key_doc.reshape(2, window + 1, span_len)
    query_doc = key_doc[:, window]
    skip = jnp.sum(key_doc[:, :window, span_len - 1] < query_doc[:, :1], axis=1).astype(jnp.int32)
    attended, grad_q, terms = attention(
        skip, q, grad_o, spans, query_doc[:, :, None], key_doc[:, :, None, :], group)
    term_flat = terms.reshape(window + 1, 2, 2, kv_heads * span_len, head_dim)
    totals = backward_chain(term_flat, shard_count).reshape(current.shape)
    grad_kv = jnp.transpose(totals, (1, 0, 3, 2, 4))[:, :, None]
    return (
        jnp.transpose(attended, (0, 2, 1, 3))[:, None],
        jnp.transpose(grad_q, (0, 2, 1, 3))[:, None],
        grad_kv[0],
        grad_kv[1],
    )


def solution(mesh):
    placed = (
        P("batch", "seq", None, "head", None),
        P("batch", "seq", None, "head", None),
        P("batch", "seq", None, "head", None),
        P("batch", "seq", None, "head", None),
        P("batch"),
    )
    return jax.shard_map(
        body,
        mesh=mesh,
        in_specs=placed,
        out_specs=(
            P("batch", "seq", None, "head", None),
            P("batch", "seq", None, "head", None),
            P("batch", "seq", None, "head", None),
            P("batch", "seq", None, "head", None),
        ),
        check_vma=False,
    )
```

```python
import functools

import jax
import jax.numpy as jnp
from jax import lax
from jax.sharding import PartitionSpec as P

from jax.experimental import pallas as pl
from jax.experimental.pallas import tpu as pltpu

ROUNDS = 16


def greet_neighbours(me, count):
    barrier = pltpu.get_barrier_semaphore()

    @pl.when(me > 0)
    def _():
        pl.semaphore_signal(barrier, 1, device_id={"seq": me - 1})

    @pl.when(me < count - 1)
    def _():
        pl.semaphore_signal(barrier, 1, device_id={"seq": me + 1})

    @pl.when(jnp.logical_and(me > 0, me < count - 1))
    def _():
        pl.semaphore_wait(barrier, 2)

    @pl.when(jnp.logical_or(me == 0, me == count - 1))
    def _():
        pl.semaphore_wait(barrier, 1)


def forward_chain_kernel(count, cur, hist, send_sem, recv_sem, local_sem):
    me = lax.axis_index("seq")
    own = pltpu.make_async_copy(cur, hist.at[ROUNDS], local_sem.at[ROUNDS])
    own.start()
    greet_neighbours(me, count)
    for k in range(1, ROUNDS + 1):
        slot = ROUNDS - k
        src_a = cur.at[0] if k == 1 else hist.at[slot + 1, 0]
        src_b = cur.at[1] if k == 1 else hist.at[slot + 1, 1]
        send_a = pltpu.make_async_remote_copy(
            src_a, hist.at[slot, 0], send_sem.at[slot, 0], recv_sem.at[slot, 0],
            device_id={"seq": me + 1})
        send_b = pltpu.make_async_remote_copy(
            src_b, hist.at[slot, 1], send_sem.at[slot, 1], recv_sem.at[slot, 1],
            device_id={"seq": me - 1})
        local_b = pltpu.make_async_copy(src_a, hist.at[slot, 1], local_sem.at[slot])
        a_sends = jnp.logical_and(me < count - 1, me >= k - 1)
        a_gets = me >= k
        b_sends = me > 0
        b_gets = me < count - 1
        pl.when(a_sends)(send_a.start)
        pl.when(b_sends)(send_b.start)
        pl.when(me == count - 1)(local_b.start)

        @pl.when(jnp.logical_not(a_gets))
        def _():
            hist[slot, 0] = jnp.zeros(hist.shape[2:], hist.dtype)

        pl.when(a_gets)(send_a.wait_recv)
        pl.when(b_gets)(send_b.wait_recv)
        pl.when(me == count - 1)(local_b.wait)
        pl.when(a_sends)(send_a.wait_send)
        pl.when(b_sends)(send_b.wait_send)
    own.wait()


def backward_chain_kernel(count, terms, out, send_buf, recv_buf, send_sem, recv_sem, local_sem):
    me = lax.axis_index("seq")
    greet_neighbours(me, count)
    send_buf[0] = terms[0].astype(send_buf.dtype)
    for t in range(1, ROUNDS + 1):
        slot = t - 1
        send_a = pltpu.make_async_remote_copy(
            send_buf.at[slot, 0], recv_buf.at[slot, 0], send_sem.at[slot, 0], recv_sem.at[slot, 0],
            device_id={"seq": me - 1})
        send_b = pltpu.make_async_remote_copy(
            send_buf.at[slot, 1], recv_buf.at[slot, 1], send_sem.at[slot, 1], recv_sem.at[slot, 1],
            device_id={"seq": me + 1})
        local_b = pltpu.make_async_copy(send_buf.at[slot, 1], recv_buf.at[slot, 0], local_sem.at[slot])
        pl.when(me > 0)(send_a.start)
        pl.when(me < count - 1)(send_b.start)
        pl.when(me == count - 1)(local_b.start)
        pl.when(me < count - 1)(send_a.wait_recv)
        pl.when(me == count - 1)(local_b.wait)
        pl.when(me > 0)(send_b.wait_recv)
        pl.when(me > 0)(send_a.wait_send)
        pl.when(me < count - 1)(send_b.wait_send)
        total_a = recv_buf[slot, 0].astype(jnp.float32) + terms[t, 0]

        @pl.when(me > 0)
        def _():
            total_b = recv_buf[slot, 1].astype(jnp.float32) + terms[t, 1]
            if t < ROUNDS:
                send_buf[t, 1] = total_b.astype(send_buf.dtype)
            else:
                out[1] = total_b.astype(out.dtype)

        @pl.when(me == 0)
        def _():
            total_b = terms[t, 1]
            if t < ROUNDS:
                send_buf[t, 1] = total_b.astype(send_buf.dtype)
            else:
                out[1] = total_b.astype(out.dtype)

        if t < ROUNDS:
            send_buf[t, 0] = total_a.astype(send_buf.dtype)
        else:
            out[0] = total_a.astype(out.dtype)


def forward_chain(current, count):
    shape = current.shape
    return pl.pallas_call(
        functools.partial(forward_chain_kernel, count),
        out_shape=jax.ShapeDtypeStruct((ROUNDS + 1,) + shape, current.dtype),
        in_specs=[pl.BlockSpec(memory_space=pltpu.VMEM)],
        out_specs=pl.BlockSpec(memory_space=pltpu.VMEM),
        scratch_shapes=[
            pltpu.SemaphoreType.DMA((ROUNDS, 2)),
            pltpu.SemaphoreType.DMA((ROUNDS, 2)),
            pltpu.SemaphoreType.DMA((ROUNDS + 1,)),
        ],
        compiler_params=pltpu.CompilerParams(
            collective_id=0, has_side_effects=True, vmem_limit_bytes=48 * 1024 * 1024),
    )(current)


def backward_chain(terms, count):
    shape = terms.shape[1:]
    return pl.pallas_call(
        functools.partial(backward_chain_kernel, count),
        out_shape=jax.ShapeDtypeStruct(shape, jnp.bfloat16),
        in_specs=[pl.BlockSpec(memory_space=pltpu.VMEM)],
        out_specs=pl.BlockSpec(memory_space=pltpu.VMEM),
        scratch_shapes=[
            pltpu.VMEM((ROUNDS,) + shape, jnp.bfloat16),
            pltpu.VMEM((ROUNDS,) + shape, jnp.bfloat16),
            pltpu.SemaphoreType.DMA((ROUNDS, 2)),
            pltpu.SemaphoreType.DMA((ROUNDS, 2)),
            pltpu.SemaphoreType.DMA((ROUNDS,)),
        ],
        compiler_params=pltpu.CompilerParams(
            collective_id=1, has_side_effects=True, vmem_limit_bytes=60 * 1024 * 1024),
    )(terms)


def attention_kernel(skip_ref, q_ref, do_ref, win_ref, qdoc_ref, kdoc_ref,
                     o_ref, dq_ref, terms_ref, cache):
    stream = pl.program_id(0)
    first = skip_ref[stream]
    group, span_len, head_dim = q_ref.shape[1:]
    rows = group * span_len
    last = win_ref.shape[0] - 1
    scale = head_dim ** (-0.5)
    q = q_ref[0].reshape(rows, head_dim)
    grad_output = do_ref[0].reshape(rows, head_dim)
    query_doc = qdoc_ref[0]
    later = lax.broadcasted_iota(jnp.int32, (span_len, span_len), 0) > lax.broadcasted_iota(
        jnp.int32, (span_len, span_len), 1)
    contract_last = (((1,), (1,)), ((), ()))

    def scores(j, causal):
        sc = lax.dot_general(win_ref[j, 0, 0, 0], q, contract_last,
                             preferred_element_type=jnp.float32) * scale
        allowed = kdoc_ref[0, j] == query_doc
        if causal:
            allowed = jnp.logical_and(allowed, jnp.logical_not(later))
        allowed = jnp.tile(allowed, (1, group))
        sc = jnp.where(allowed, sc, -jnp.inf)
        cache[j] = sc
        return sc

    sc = scores(last, True)
    top = jnp.max(sc, axis=0, keepdims=True)
    total = jnp.sum(jnp.exp(sc - top), axis=0, keepdims=True)

    def stat_step(j, carry):
        top, total = carry
        sc = scores(j, False)
        new_top = jnp.maximum(top, jnp.max(sc, axis=0, keepdims=True))
        total = total * jnp.exp(top - new_top) + jnp.sum(jnp.exp(sc - new_top), axis=0, keepdims=True)
        return new_top, total

    top, total = lax.fori_loop(first, last, stat_step, (top, total))
    inverse = 1.0 / total

    def out_step(j, acc):
        prob = jnp.exp(cache[j] - top) * inverse
        cache[j] = prob
        value_t = win_ref[j, 0, 1, 0].astype(jnp.float32).T.astype(jnp.bfloat16)
        return acc + jnp.dot(value_t, prob.astype(jnp.bfloat16), preferred_element_type=jnp.float32)

    acc = out_step(last, jnp.zeros((head_dim, rows), jnp.float32))
    acc = lax.fori_loop(first, last, out_step, acc)
    attended_t = acc.astype(jnp.bfloat16)
    o_ref[0] = attended_t.astype(jnp.float32).T.astype(jnp.bfloat16).reshape(group, span_len, head_dim)
    grad_t = grad_output.astype(jnp.float32).T
    delta = jnp.sum(grad_t * attended_t.astype(jnp.float32), axis=0, keepdims=True)

    def grad_step(j, dq):
        prob = cache[j]
        low = prob.astype(jnp.bfloat16)
        grad_w = lax.dot_general(win_ref[j, 0, 1, 0], grad_output, contract_last,
                                 preferred_element_type=jnp.float32)
        grad_s = (prob * (grad_w - delta) * scale).astype(jnp.bfloat16)
        terms_ref[j, 0, 0, 0] = jnp.dot(grad_s, q, preferred_element_type=jnp.float32)
        terms_ref[j, 0, 1, 0] = jnp.dot(low, grad_output, preferred_element_type=jnp.float32)
        key_t = win_ref[j, 0, 0, 0].astype(jnp.float32).T.astype(jnp.bfloat16)
        return dq + jnp.dot(key_t, grad_s, preferred_element_type=jnp.float32)

    dq = grad_step(last, jnp.zeros((head_dim, rows), jnp.float32))
    dq = lax.fori_loop(first, last, grad_step, dq)
    dq_ref[0] = dq.T.astype(jnp.bfloat16).reshape(group, span_len, head_dim)

    def clear(j, carry):
        terms_ref[j] = jnp.zeros(terms_ref.shape[1:], terms_ref.dtype)
        return carry

    lax.fori_loop(0, first, clear, 0)


def attention(skip, q, grad_out, window, query_doc, key_doc, group):
    streams, heads, span_len, head_dim = q.shape
    kv_heads = heads // group
    spans = window.shape[0]
    head_block = pl.BlockSpec((1, group, span_len, head_dim), lambda s, h, sk: (s, h, 0, 0))
    return pl.pallas_call(
        attention_kernel,
        out_shape=(
            jax.ShapeDtypeStruct(q.shape, jnp.bfloat16),
            jax.ShapeDtypeStruct(q.shape, jnp.bfloat16),
            jax.ShapeDtypeStruct((spans, streams, 2, kv_heads, span_len, head_dim), jnp.float32),
        ),
        grid_spec=pltpu.PrefetchScalarGridSpec(
            num_scalar_prefetch=1,
            grid=(streams, kv_heads),
            in_specs=[
                head_block,
                head_block,
                pl.BlockSpec((spans, 1, 2, 1, span_len, head_dim), lambda s, h, sk: (0, s, 0, h, 0, 0)),
                pl.BlockSpec((1, 1, span_len), lambda s, h, sk: (s, 0, 0)),
                pl.BlockSpec((1, spans, span_len, 1), lambda s, h, sk: (s, 0, 0, 0)),
            ],
            out_specs=[
                head_block,
                head_block,
                pl.BlockSpec((spans, 1, 2, 1, span_len, head_dim), lambda s, h, sk: (0, s, 0, h, 0, 0)),
            ],
            scratch_shapes=[pltpu.VMEM((spans, span_len, group * span_len), jnp.float32)],
        ),
        compiler_params=pltpu.CompilerParams(vmem_limit_bytes=48 * 1024 * 1024),
    )(skip, q, grad_out, window, query_doc, key_doc)


def window_docs(doc_starts, key_pos):
    width = key_pos.shape[1]
    before = jnp.sum((doc_starts[None, :] < key_pos[:, :1]).astype(jnp.int32), axis=1)
    padded = jnp.concatenate(
        [doc_starts, jnp.full((width // 2,), jnp.iinfo(jnp.int32).max, doc_starts.dtype)])
    local = jnp.stack([lax.dynamic_slice_in_dim(padded, before[i], width // 2) for i in range(2)])
    inside = jnp.sum((local[:, None, :] <= key_pos[:, :, None]).astype(jnp.int32), axis=2)
    return before[:, None] + inside - 1


def body(query, keys, values, grad_out, doc_starts):
    shard_count = lax.axis_size("seq")
    device_index = lax.axis_index("seq")
    window = ROUNDS
    span_len = query.shape[2]
    kv_heads = keys.shape[3]
    head_dim = query.shape[4]
    group = query.shape[3] // kv_heads
    q = jnp.transpose(query[:, 0], (0, 2, 1, 3))
    grad_o = jnp.transpose(grad_out[:, 0], (0, 2, 1, 3))
    current = jnp.stack([jnp.transpose(keys[:, 0], (0, 2, 1, 3)),
                         jnp.transpose(values[:, 0], (0, 2, 1, 3))], axis=1)
    flat = current.reshape(2, 2, kv_heads * span_len, head_dim)
    spans = forward_chain(flat, shard_count).reshape((window + 1,) + current.shape)
    span_firsts = jnp.stack([device_index, 2 * shard_count - 1 - device_index])
    key_pos = (span_firsts[:, None] - window) * span_len + jnp.arange(
        (window + 1) * span_len, dtype=jnp.int32)[None]
    key_doc = window_docs(doc_starts, key_pos)
    key_doc = key_doc.reshape(2, window + 1, span_len)
    query_doc = key_doc[:, window]
    skip = jnp.sum(key_doc[:, :window, span_len - 1] < query_doc[:, :1], axis=1).astype(jnp.int32)
    attended, grad_q, terms = attention(
        skip, q, grad_o, spans, query_doc[:, None, :], key_doc[:, :, :, None], group)
    term_flat = terms.reshape(window + 1, 2, 2, kv_heads * span_len, head_dim)
    totals = backward_chain(term_flat, shard_count).reshape(current.shape)
    grad_kv = jnp.transpose(totals, (1, 0, 3, 2, 4))[:, :, None]
    return (
        jnp.transpose(attended, (0, 2, 1, 3))[:, None],
        jnp.transpose(grad_q, (0, 2, 1, 3))[:, None],
        grad_kv[0],
        grad_kv[1],
    )


def solution(mesh):
    placed = (
        P("batch", "seq", None, "head", None),
        P("batch", "seq", None, "head", None),
        P("batch", "seq", None, "head", None),
        P("batch", "seq", None, "head", None),
        P("batch"),
    )
    return jax.shard_map(
        body,
        mesh=mesh,
        in_specs=placed,
        out_specs=(
            P("batch", "seq", None, "head", None),
            P("batch", "seq", None, "head", None),
            P("batch", "seq", None, "head", None),
            P("batch", "seq", None, "head", None),
        ),
        check_vma=False,
    )
```

```python
import functools

import jax
import jax.numpy as jnp
from jax import lax
from jax.sharding import PartitionSpec as P

from jax.experimental import pallas as pl
from jax.experimental.pallas import tpu as pltpu

ROUNDS = 16


def greet_neighbours(me, count):
    barrier = pltpu.get_barrier_semaphore()

    @pl.when(me > 0)
    def _():
        pl.semaphore_signal(barrier, 1, device_id={"seq": me - 1})

    @pl.when(me < count - 1)
    def _():
        pl.semaphore_signal(barrier, 1, device_id={"seq": me + 1})

    @pl.when(jnp.logical_and(me > 0, me < count - 1))
    def _():
        pl.semaphore_wait(barrier, 2)

    @pl.when(jnp.logical_or(me == 0, me == count - 1))
    def _():
        pl.semaphore_wait(barrier, 1)


PIECES = 4


def piece_rows(i, total):
    size = total // (PIECES // 2)
    return i // (PIECES // 2), pl.ds((i % (PIECES // 2)) * size, size)


def forward_chain_kernel(count, cur, hist, send_sem, recv_sem, local_sem):
    me = lax.axis_index("seq")
    own = pltpu.make_async_copy(cur, hist.at[ROUNDS], local_sem.at[ROUNDS, 0])
    own.start()
    greet_neighbours(me, count)
    total = cur.shape[2]

    def copies(k, i):
        slot = ROUNDS - k
        kv, rows = piece_rows(i, total)
        src_a = cur.at[0, kv, rows] if k == 1 else hist.at[slot + 1, 0, kv, rows]
        src_b = cur.at[1, kv, rows] if k == 1 else hist.at[slot + 1, 1, kv, rows]
        send_a = pltpu.make_async_remote_copy(
            src_a, hist.at[slot, 0, kv, rows], send_sem.at[slot, 0, i], recv_sem.at[slot, 0, i],
            device_id={"seq": me + 1})
        send_b = pltpu.make_async_remote_copy(
            src_b, hist.at[slot, 1, kv, rows], send_sem.at[slot, 1, i], recv_sem.at[slot, 1, i],
            device_id={"seq": me - 1})
        local_b = pltpu.make_async_copy(src_a, hist.at[slot, 1, kv, rows], local_sem.at[slot, i])
        return send_a, send_b, local_b

    def a_sends(k):
        return jnp.logical_and(me < count - 1, me >= k - 1)

    def receive(k, i):
        send_a, send_b, local_b = copies(k, i)
        pl.when(me >= k)(send_a.wait_recv)
        pl.when(me < count - 1)(send_b.wait_recv)
        pl.when(me == count - 1)(local_b.wait)

    for k in range(1, ROUNDS + 1):
        for i in range(PIECES):
            if k > 1:
                receive(k - 1, i)
            send_a, send_b, local_b = copies(k, i)
            pl.when(a_sends(k))(send_a.start)
            pl.when(me > 0)(send_b.start)
            pl.when(me == count - 1)(local_b.start)

        @pl.when(me < k)
        def _():
            hist[ROUNDS - k, 0] = jnp.zeros(hist.shape[2:], hist.dtype)

    for i in range(PIECES):
        receive(ROUNDS, i)
    for k in range(1, ROUNDS + 1):
        for i in range(PIECES):
            send_a, send_b, _ = copies(k, i)
            pl.when(a_sends(k))(send_a.wait_send)
            pl.when(me > 0)(send_b.wait_send)
    own.wait()


def backward_chain_kernel(count, terms, out, send_buf, recv_buf, send_sem, recv_sem, local_sem):
    me = lax.axis_index("seq")
    greet_neighbours(me, count)
    total = terms.shape[3]

    def copies(t, i):
        slot = t - 1
        kv, rows = piece_rows(i, total)
        send_a = pltpu.make_async_remote_copy(
            send_buf.at[slot, 0, kv, rows], recv_buf.at[slot, 0, kv, rows],
            send_sem.at[slot, 0, i], recv_sem.at[slot, 0, i], device_id={"seq": me - 1})
        send_b = pltpu.make_async_remote_copy(
            send_buf.at[slot, 1, kv, rows], recv_buf.at[slot, 1, kv, rows],
            send_sem.at[slot, 1, i], recv_sem.at[slot, 1, i], device_id={"seq": me + 1})
        local_b = pltpu.make_async_copy(
            send_buf.at[slot, 1, kv, rows], recv_buf.at[slot, 0, kv, rows], local_sem.at[slot, i])
        return send_a, send_b, local_b

    def start(t, i):
        send_a, send_b, local_b = copies(t, i)
        pl.when(me > 0)(send_a.start)
        pl.when(me < count - 1)(send_b.start)
        pl.when(me == count - 1)(local_b.start)

    for i in range(PIECES):
        kv, rows = piece_rows(i, total)
        send_buf[0, :, kv, rows] = terms[0, :, kv, rows].astype(send_buf.dtype)
        start(1, i)
    for t in range(1, ROUNDS + 1):
        slot = t - 1
        for i in range(PIECES):
            kv, rows = piece_rows(i, total)
            send_a, send_b, local_b = copies(t, i)
            pl.when(me < count - 1)(send_a.wait_recv)
            pl.when(me == count - 1)(local_b.wait)
            pl.when(me > 0)(send_b.wait_recv)
            total_a = recv_buf[slot, 0, kv, rows].astype(jnp.float32) + terms[t, 0, kv, rows]
            if t < ROUNDS:
                send_buf[t, 0, kv, rows] = total_a.astype(send_buf.dtype)
            else:
                out[0, kv, rows] = total_a.astype(out.dtype)

            @pl.when(me > 0)
            def _():
                total_b = recv_buf[slot, 1, kv, rows].astype(jnp.float32) + terms[t, 1, kv, rows]
                if t < ROUNDS:
                    send_buf[t, 1, kv, rows] = total_b.astype(send_buf.dtype)
                else:
                    out[1, kv, rows] = total_b.astype(out.dtype)

            @pl.when(me == 0)
            def _():
                total_b = terms[t, 1, kv, rows]
                if t < ROUNDS:
                    send_buf[t, 1, kv, rows] = total_b.astype(send_buf.dtype)
                else:
                    out[1, kv, rows] = total_b.astype(out.dtype)

            if t < ROUNDS:
                start(t + 1, i)
    for t in range(1, ROUNDS + 1):
        for i in range(PIECES):
            send_a, send_b, _ = copies(t, i)
            pl.when(me > 0)(send_a.wait_send)
            pl.when(me < count - 1)(send_b.wait_send)


def forward_chain(current, count):
    shape = current.shape
    return pl.pallas_call(
        functools.partial(forward_chain_kernel, count),
        out_shape=jax.ShapeDtypeStruct((ROUNDS + 1,) + shape, current.dtype),
        in_specs=[pl.BlockSpec(memory_space=pltpu.VMEM)],
        out_specs=pl.BlockSpec(memory_space=pltpu.VMEM),
        scratch_shapes=[
            pltpu.SemaphoreType.DMA((ROUNDS, 2, PIECES)),
            pltpu.SemaphoreType.DMA((ROUNDS, 2, PIECES)),
            pltpu.SemaphoreType.DMA((ROUNDS + 1, PIECES)),
        ],
        compiler_params=pltpu.CompilerParams(
            collective_id=0, has_side_effects=True, vmem_limit_bytes=48 * 1024 * 1024),
    )(current)


def backward_chain(terms, count):
    shape = terms.shape[1:]
    return pl.pallas_call(
        functools.partial(backward_chain_kernel, count),
        out_shape=jax.ShapeDtypeStruct(shape, jnp.bfloat16),
        in_specs=[pl.BlockSpec(memory_space=pltpu.VMEM)],
        out_specs=pl.BlockSpec(memory_space=pltpu.VMEM),
        scratch_shapes=[
            pltpu.VMEM((ROUNDS,) + shape, jnp.bfloat16),
            pltpu.VMEM((ROUNDS,) + shape, jnp.bfloat16),
            pltpu.SemaphoreType.DMA((ROUNDS, 2, PIECES)),
            pltpu.SemaphoreType.DMA((ROUNDS, 2, PIECES)),
            pltpu.SemaphoreType.DMA((ROUNDS, PIECES)),
        ],
        compiler_params=pltpu.CompilerParams(
            collective_id=1, has_side_effects=True, vmem_limit_bytes=60 * 1024 * 1024),
    )(terms)


def attention_kernel(skip_ref, q_ref, do_ref, win_ref, qdoc_ref, kdoc_ref,
                     o_ref, dq_ref, terms_ref, cache):
    stream = pl.program_id(0)
    first = skip_ref[stream]
    group, span_len, head_dim = q_ref.shape[1:]
    rows = group * span_len
    last = win_ref.shape[0] - 1
    scale = head_dim ** (-0.5)
    q = q_ref[0].reshape(rows, head_dim)
    grad_output = do_ref[0].reshape(rows, head_dim)
    query_doc = qdoc_ref[0]
    later = lax.broadcasted_iota(jnp.int32, (span_len, span_len), 0) > lax.broadcasted_iota(
        jnp.int32, (span_len, span_len), 1)
    contract_last = (((1,), (1,)), ((), ()))

    def scores(j, causal):
        sc = lax.dot_general(win_ref[j, 0, 0, 0], q, contract_last,
                             preferred_element_type=jnp.float32) * scale
        allowed = kdoc_ref[0, j] == query_doc
        if causal:
            allowed = jnp.logical_and(allowed, jnp.logical_not(later))
        allowed = jnp.tile(allowed, (1, group))
        sc = jnp.where(allowed, sc, -jnp.inf)
        cache[j] = sc
        return sc

    sc = scores(last, True)
    top = jnp.max(sc, axis=0, keepdims=True)
    total = jnp.sum(jnp.exp(sc - top), axis=0, keepdims=True)

    def stat_step(j, carry):
        top, total = carry
        sc = scores(j, False)
        new_top = jnp.maximum(top, jnp.max(sc, axis=0, keepdims=True))
        total = total * jnp.exp(top - new_top) + jnp.sum(jnp.exp(sc - new_top), axis=0, keepdims=True)
        return new_top, total

    top, total = lax.fori_loop(first, last, stat_step, (top, total))
    inverse = 1.0 / total

    def out_step(j, acc):
        prob = jnp.exp(cache[j] - top) * inverse
        cache[j] = prob
        value_t = win_ref[j, 0, 1, 0].astype(jnp.float32).T.astype(jnp.bfloat16)
        return acc + jnp.dot(value_t, prob.astype(jnp.bfloat16), preferred_element_type=jnp.float32)

    acc = out_step(last, jnp.zeros((head_dim, rows), jnp.float32))
    acc = lax.fori_loop(first, last, out_step, acc)
    attended_t = acc.astype(jnp.bfloat16)
    o_ref[0] = attended_t.astype(jnp.float32).T.astype(jnp.bfloat16).reshape(group, span_len, head_dim)
    grad_t = grad_output.astype(jnp.float32).T
    delta = jnp.sum(grad_t * attended_t.astype(jnp.float32), axis=0, keepdims=True)

    def grad_step(j, dq):
        prob = cache[j]
        low = prob.astype(jnp.bfloat16)
        grad_w = lax.dot_general(win_ref[j, 0, 1, 0], grad_output, contract_last,
                                 preferred_element_type=jnp.float32)
        grad_s = (prob * (grad_w - delta) * scale).astype(jnp.bfloat16)
        terms_ref[j, 0, 0, 0] = jnp.dot(grad_s, q, preferred_element_type=jnp.float32)
        terms_ref[j, 0, 1, 0] = jnp.dot(low, grad_output, preferred_element_type=jnp.float32)
        key_t = win_ref[j, 0, 0, 0].astype(jnp.float32).T.astype(jnp.bfloat16)
        return dq + jnp.dot(key_t, grad_s, preferred_element_type=jnp.float32)

    dq = grad_step(last, jnp.zeros((head_dim, rows), jnp.float32))
    dq = lax.fori_loop(first, last, grad_step, dq)
    dq_ref[0] = dq.T.astype(jnp.bfloat16).reshape(group, span_len, head_dim)

    def clear(j, carry):
        terms_ref[j] = jnp.zeros(terms_ref.shape[1:], terms_ref.dtype)
        return carry

    lax.fori_loop(0, first, clear, 0)


def attention(skip, q, grad_out, window, query_doc, key_doc, group):
    streams, heads, span_len, head_dim = q.shape
    kv_heads = heads // group
    spans = window.shape[0]
    head_block = pl.BlockSpec((1, group, span_len, head_dim), lambda s, h, sk: (s, h, 0, 0))
    return pl.pallas_call(
        attention_kernel,
        out_shape=(
            jax.ShapeDtypeStruct(q.shape, jnp.bfloat16),
            jax.ShapeDtypeStruct(q.shape, jnp.bfloat16),
            jax.ShapeDtypeStruct((spans, streams, 2, kv_heads, span_len, head_dim), jnp.float32),
        ),
        grid_spec=pltpu.PrefetchScalarGridSpec(
            num_scalar_prefetch=1,
            grid=(streams, kv_heads),
            in_specs=[
                head_block,
                head_block,
                pl.BlockSpec((spans, 1, 2, 1, span_len, head_dim), lambda s, h, sk: (0, s, 0, h, 0, 0)),
                pl.BlockSpec((1, 1, span_len), lambda s, h, sk: (s, 0, 0)),
                pl.BlockSpec((1, spans, span_len, 1), lambda s, h, sk: (s, 0, 0, 0)),
            ],
            out_specs=[
                head_block,
                head_block,
                pl.BlockSpec((spans, 1, 2, 1, span_len, head_dim), lambda s, h, sk: (0, s, 0, h, 0, 0)),
            ],
            scratch_shapes=[pltpu.VMEM((spans, span_len, group * span_len), jnp.float32)],
        ),
        compiler_params=pltpu.CompilerParams(vmem_limit_bytes=48 * 1024 * 1024),
    )(skip, q, grad_out, window, query_doc, key_doc)


def window_docs(doc_starts, key_pos):
    width = key_pos.shape[1]
    before = jnp.sum((doc_starts[None, :] < key_pos[:, :1]).astype(jnp.int32), axis=1)
    padded = jnp.concatenate(
        [doc_starts, jnp.full((width // 2,), jnp.iinfo(jnp.int32).max, doc_starts.dtype)])
    local = jnp.stack([lax.dynamic_slice_in_dim(padded, before[i], width // 2) for i in range(2)])
    inside = jnp.sum((local[:, None, :] <= key_pos[:, :, None]).astype(jnp.int32), axis=2)
    return before[:, None] + inside - 1


def body(query, keys, values, grad_out, doc_starts):
    shard_count = lax.axis_size("seq")
    device_index = lax.axis_index("seq")
    window = ROUNDS
    span_len = query.shape[2]
    kv_heads = keys.shape[3]
    head_dim = query.shape[4]
    group = query.shape[3] // kv_heads
    q = jnp.transpose(query[:, 0], (0, 2, 1, 3))
    grad_o = jnp.transpose(grad_out[:, 0], (0, 2, 1, 3))
    current = jnp.stack([jnp.transpose(keys[:, 0], (0, 2, 1, 3)),
                         jnp.transpose(values[:, 0], (0, 2, 1, 3))], axis=1)
    flat = current.reshape(2, 2, kv_heads * span_len, head_dim)
    spans = forward_chain(flat, shard_count).reshape((window + 1,) + current.shape)
    span_firsts = jnp.stack([device_index, 2 * shard_count - 1 - device_index])
    key_pos = (span_firsts[:, None] - window) * span_len + jnp.arange(
        (window + 1) * span_len, dtype=jnp.int32)[None]
    key_doc = window_docs(doc_starts, key_pos)
    key_doc = key_doc.reshape(2, window + 1, span_len)
    query_doc = key_doc[:, window]
    skip = jnp.sum(key_doc[:, :window, span_len - 1] < query_doc[:, :1], axis=1).astype(jnp.int32)
    attended, grad_q, terms = attention(
        skip, q, grad_o, spans, query_doc[:, None, :], key_doc[:, :, :, None], group)
    term_flat = terms.reshape(window + 1, 2, 2, kv_heads * span_len, head_dim)
    totals = backward_chain(term_flat, shard_count).reshape(current.shape)
    grad_kv = jnp.transpose(totals, (1, 0, 3, 2, 4))[:, :, None]
    return (
        jnp.transpose(attended, (0, 2, 1, 3))[:, None],
        jnp.transpose(grad_q, (0, 2, 1, 3))[:, None],
        grad_kv[0],
        grad_kv[1],
    )


def solution(mesh):
    placed = (
        P("batch", "seq", None, "head", None),
        P("batch", "seq", None, "head", None),
        P("batch", "seq", None, "head", None),
        P("batch", "seq", None, "head", None),
        P("batch"),
    )
    return jax.shard_map(
        body,
        mesh=mesh,
        in_specs=placed,
        out_specs=(
            P("batch", "seq", None, "head", None),
            P("batch", "seq", None, "head", None),
            P("batch", "seq", None, "head", None),
            P("batch", "seq", None, "head", None),
        ),
        check_vma=False,
    )
```

```python
import functools

import jax
import jax.numpy as jnp
from jax import lax
from jax.sharding import PartitionSpec as P

from jax.experimental import pallas as pl
from jax.experimental.pallas import tpu as pltpu

ROUNDS = 16


def greet_neighbours(me, count):
    barrier = pltpu.get_barrier_semaphore()

    @pl.when(me > 0)
    def _():
        pl.semaphore_signal(barrier, 1, device_id={"seq": me - 1})

    @pl.when(me < count - 1)
    def _():
        pl.semaphore_signal(barrier, 1, device_id={"seq": me + 1})

    @pl.when(jnp.logical_and(me > 0, me < count - 1))
    def _():
        pl.semaphore_wait(barrier, 2)

    @pl.when(jnp.logical_or(me == 0, me == count - 1))
    def _():
        pl.semaphore_wait(barrier, 1)


PIECES = 8


def piece_rows(i, total):
    size = total // (PIECES // 2)
    return i // (PIECES // 2), pl.ds((i % (PIECES // 2)) * size, size)


def forward_chain_kernel(count, cur, hist, send_sem, recv_sem, local_sem):
    me = lax.axis_index("seq")
    own = pltpu.make_async_copy(cur, hist.at[ROUNDS], local_sem.at[ROUNDS, 0])
    own.start()
    greet_neighbours(me, count)
    total = cur.shape[2]

    def copies(k, i):
        slot = ROUNDS - k
        kv, rows = piece_rows(i, total)
        src_a = cur.at[0, kv, rows] if k == 1 else hist.at[slot + 1, 0, kv, rows]
        src_b = cur.at[1, kv, rows] if k == 1 else hist.at[slot + 1, 1, kv, rows]
        send_a = pltpu.make_async_remote_copy(
            src_a, hist.at[slot, 0, kv, rows], send_sem.at[slot, 0, i], recv_sem.at[slot, 0, i],
            device_id={"seq": me + 1})
        send_b = pltpu.make_async_remote_copy(
            src_b, hist.at[slot, 1, kv, rows], send_sem.at[slot, 1, i], recv_sem.at[slot, 1, i],
            device_id={"seq": me - 1})
        local_b = pltpu.make_async_copy(src_a, hist.at[slot, 1, kv, rows], local_sem.at[slot, i])
        return send_a, send_b, local_b

    def a_sends(k):
        return jnp.logical_and(me < count - 1, me >= k - 1)

    def receive(k, i):
        send_a, send_b, local_b = copies(k, i)
        pl.when(me >= k)(send_a.wait_recv)
        pl.when(me < count - 1)(send_b.wait_recv)
        pl.when(me == count - 1)(local_b.wait)

    for k in range(1, ROUNDS + 1):
        for i in range(PIECES):
            if k > 1:
                receive(k - 1, i)
            send_a, send_b, local_b = copies(k, i)
            pl.when(a_sends(k))(send_a.start)
            pl.when(me > 0)(send_b.start)
            pl.when(me == count - 1)(local_b.start)

        @pl.when(me < k)
        def _():
            hist[ROUNDS - k, 0] = jnp.zeros(hist.shape[2:], hist.dtype)

    for i in range(PIECES):
        receive(ROUNDS, i)
    for k in range(1, ROUNDS + 1):
        for i in range(PIECES):
            send_a, send_b, _ = copies(k, i)
            pl.when(a_sends(k))(send_a.wait_send)
            pl.when(me > 0)(send_b.wait_send)
    own.wait()


def backward_chain_kernel(count, terms, out, send_buf, recv_buf, send_sem, recv_sem, local_sem):
    me = lax.axis_index("seq")
    greet_neighbours(me, count)
    total = terms.shape[3]

    def copies(t, i):
        slot = t - 1
        kv, rows = piece_rows(i, total)
        send_a = pltpu.make_async_remote_copy(
            send_buf.at[slot, 0, kv, rows], recv_buf.at[slot, 0, kv, rows],
            send_sem.at[slot, 0, i], recv_sem.at[slot, 0, i], device_id={"seq": me - 1})
        send_b = pltpu.make_async_remote_copy(
            send_buf.at[slot, 1, kv, rows], recv_buf.at[slot, 1, kv, rows],
            send_sem.at[slot, 1, i], recv_sem.at[slot, 1, i], device_id={"seq": me + 1})
        local_b = pltpu.make_async_copy(
            send_buf.at[slot, 1, kv, rows], recv_buf.at[slot, 0, kv, rows], local_sem.at[slot, i])
        return send_a, send_b, local_b

    def start(t, i):
        send_a, send_b, local_b = copies(t, i)
        pl.when(me > 0)(send_a.start)
        pl.when(me < count - 1)(send_b.start)
        pl.when(me == count - 1)(local_b.start)

    for i in range(PIECES):
        kv, rows = piece_rows(i, total)
        send_buf[0, :, kv, rows] = terms[0, :, kv, rows].astype(send_buf.dtype)
        start(1, i)
    for t in range(1, ROUNDS + 1):
        slot = t - 1
        for i in range(PIECES):
            kv, rows = piece_rows(i, total)
            send_a, send_b, local_b = copies(t, i)
            pl.when(me < count - 1)(send_a.wait_recv)
            pl.when(me == count - 1)(local_b.wait)
            pl.when(me > 0)(send_b.wait_recv)
            total_a = recv_buf[slot, 0, kv, rows].astype(jnp.float32) + terms[t, 0, kv, rows]
            if t < ROUNDS:
                send_buf[t, 0, kv, rows] = total_a.astype(send_buf.dtype)
            else:
                out[0, kv, rows] = total_a.astype(out.dtype)

            @pl.when(me > 0)
            def _():
                total_b = recv_buf[slot, 1, kv, rows].astype(jnp.float32) + terms[t, 1, kv, rows]
                if t < ROUNDS:
                    send_buf[t, 1, kv, rows] = total_b.astype(send_buf.dtype)
                else:
                    out[1, kv, rows] = total_b.astype(out.dtype)

            @pl.when(me == 0)
            def _():
                total_b = terms[t, 1, kv, rows]
                if t < ROUNDS:
                    send_buf[t, 1, kv, rows] = total_b.astype(send_buf.dtype)
                else:
                    out[1, kv, rows] = total_b.astype(out.dtype)

            if t < ROUNDS:
                start(t + 1, i)
    for t in range(1, ROUNDS + 1):
        for i in range(PIECES):
            send_a, send_b, _ = copies(t, i)
            pl.when(me > 0)(send_a.wait_send)
            pl.when(me < count - 1)(send_b.wait_send)


def forward_chain(current, count):
    shape = current.shape
    return pl.pallas_call(
        functools.partial(forward_chain_kernel, count),
        out_shape=jax.ShapeDtypeStruct((ROUNDS + 1,) + shape, current.dtype),
        in_specs=[pl.BlockSpec(memory_space=pltpu.VMEM)],
        out_specs=pl.BlockSpec(memory_space=pltpu.VMEM),
        scratch_shapes=[
            pltpu.SemaphoreType.DMA((ROUNDS, 2, PIECES)),
            pltpu.SemaphoreType.DMA((ROUNDS, 2, PIECES)),
            pltpu.SemaphoreType.DMA((ROUNDS + 1, PIECES)),
        ],
        compiler_params=pltpu.CompilerParams(
            collective_id=0, has_side_effects=True, vmem_limit_bytes=48 * 1024 * 1024),
    )(current)


def backward_chain(terms, count):
    shape = terms.shape[1:]
    return pl.pallas_call(
        functools.partial(backward_chain_kernel, count),
        out_shape=jax.ShapeDtypeStruct(shape, jnp.bfloat16),
        in_specs=[pl.BlockSpec(memory_space=pltpu.VMEM)],
        out_specs=pl.BlockSpec(memory_space=pltpu.VMEM),
        scratch_shapes=[
            pltpu.VMEM((ROUNDS,) + shape, jnp.bfloat16),
            pltpu.VMEM((ROUNDS,) + shape, jnp.bfloat16),
            pltpu.SemaphoreType.DMA((ROUNDS, 2, PIECES)),
            pltpu.SemaphoreType.DMA((ROUNDS, 2, PIECES)),
            pltpu.SemaphoreType.DMA((ROUNDS, PIECES)),
        ],
        compiler_params=pltpu.CompilerParams(
            collective_id=1, has_side_effects=True, vmem_limit_bytes=60 * 1024 * 1024),
    )(terms)


def attention_kernel(skip_ref, q_ref, do_ref, win_ref, qdoc_ref, kdoc_ref,
                     o_ref, dq_ref, terms_ref, cache):
    stream = pl.program_id(0)
    first = skip_ref[stream]
    group, span_len, head_dim = q_ref.shape[1:]
    rows = group * span_len
    last = win_ref.shape[0] - 1
    scale = head_dim ** (-0.5)
    q = q_ref[0].reshape(rows, head_dim)
    grad_output = do_ref[0].reshape(rows, head_dim)
    query_doc = qdoc_ref[0]
    later = lax.broadcasted_iota(jnp.int32, (span_len, span_len), 0) > lax.broadcasted_iota(
        jnp.int32, (span_len, span_len), 1)
    contract_last = (((1,), (1,)), ((), ()))

    def scores(j, causal):
        sc = lax.dot_general(win_ref[j, 0, 0, 0], q, contract_last,
                             preferred_element_type=jnp.float32) * scale
        allowed = kdoc_ref[0, j] == query_doc
        if causal:
            allowed = jnp.logical_and(allowed, jnp.logical_not(later))
        allowed = jnp.tile(allowed, (1, group))
        sc = jnp.where(allowed, sc, -jnp.inf)
        cache[j] = sc
        return sc

    sc = scores(last, True)
    top = jnp.max(sc, axis=0, keepdims=True)
    total = jnp.sum(jnp.exp(sc - top), axis=0, keepdims=True)

    def stat_step(j, carry):
        top, total = carry
        sc = scores(j, False)
        new_top = jnp.maximum(top, jnp.max(sc, axis=0, keepdims=True))
        total = total * jnp.exp(top - new_top) + jnp.sum(jnp.exp(sc - new_top), axis=0, keepdims=True)
        return new_top, total

    top, total = lax.fori_loop(first, last, stat_step, (top, total))
    inverse = 1.0 / total

    def out_step(j, acc):
        prob = jnp.exp(cache[j] - top) * inverse
        cache[j] = prob
        value_t = win_ref[j, 0, 1, 0].astype(jnp.float32).T.astype(jnp.bfloat16)
        return acc + jnp.dot(value_t, prob.astype(jnp.bfloat16), preferred_element_type=jnp.float32)

    acc = out_step(last, jnp.zeros((head_dim, rows), jnp.float32))
    acc = lax.fori_loop(first, last, out_step, acc)
    attended_t = acc.astype(jnp.bfloat16)
    o_ref[0] = attended_t.astype(jnp.float32).T.astype(jnp.bfloat16).reshape(group, span_len, head_dim)
    grad_t = grad_output.astype(jnp.float32).T
    delta = jnp.sum(grad_t * attended_t.astype(jnp.float32), axis=0, keepdims=True)

    def grad_step(j, dq):
        prob = cache[j]
        low = prob.astype(jnp.bfloat16)
        grad_w = lax.dot_general(win_ref[j, 0, 1, 0], grad_output, contract_last,
                                 preferred_element_type=jnp.float32)
        grad_s = (prob * (grad_w - delta) * scale).astype(jnp.bfloat16)
        terms_ref[j, 0, 0, 0] = jnp.dot(grad_s, q, preferred_element_type=jnp.float32)
        terms_ref[j, 0, 1, 0] = jnp.dot(low, grad_output, preferred_element_type=jnp.float32)
        key_t = win_ref[j, 0, 0, 0].astype(jnp.float32).T.astype(jnp.bfloat16)
        return dq + jnp.dot(key_t, grad_s, preferred_element_type=jnp.float32)

    dq = grad_step(last, jnp.zeros((head_dim, rows), jnp.float32))
    dq = lax.fori_loop(first, last, grad_step, dq)
    dq_ref[0] = dq.T.astype(jnp.bfloat16).reshape(group, span_len, head_dim)

    def clear(j, carry):
        terms_ref[j] = jnp.zeros(terms_ref.shape[1:], terms_ref.dtype)
        return carry

    lax.fori_loop(0, first, clear, 0)


def attention(skip, q, grad_out, window, query_doc, key_doc, group):
    streams, heads, span_len, head_dim = q.shape
    kv_heads = heads // group
    spans = window.shape[0]
    head_block = pl.BlockSpec((1, group, span_len, head_dim), lambda s, h, sk: (s, h, 0, 0))
    return pl.pallas_call(
        attention_kernel,
        out_shape=(
            jax.ShapeDtypeStruct(q.shape, jnp.bfloat16),
            jax.ShapeDtypeStruct(q.shape, jnp.bfloat16),
            jax.ShapeDtypeStruct((spans, streams, 2, kv_heads, span_len, head_dim), jnp.float32),
        ),
        grid_spec=pltpu.PrefetchScalarGridSpec(
            num_scalar_prefetch=1,
            grid=(streams, kv_heads),
            in_specs=[
                head_block,
                head_block,
                pl.BlockSpec((spans, 1, 2, 1, span_len, head_dim), lambda s, h, sk: (0, s, 0, h, 0, 0)),
                pl.BlockSpec((1, 1, span_len), lambda s, h, sk: (s, 0, 0)),
                pl.BlockSpec((1, spans, span_len, 1), lambda s, h, sk: (s, 0, 0, 0)),
            ],
            out_specs=[
                head_block,
                head_block,
                pl.BlockSpec((spans, 1, 2, 1, span_len, head_dim), lambda s, h, sk: (0, s, 0, h, 0, 0)),
            ],
            scratch_shapes=[pltpu.VMEM((spans, span_len, group * span_len), jnp.float32)],
        ),
        compiler_params=pltpu.CompilerParams(vmem_limit_bytes=48 * 1024 * 1024),
    )(skip, q, grad_out, window, query_doc, key_doc)


def window_docs(doc_starts, key_pos):
    width = key_pos.shape[1]
    before = jnp.sum((doc_starts[None, :] < key_pos[:, :1]).astype(jnp.int32), axis=1)
    padded = jnp.concatenate(
        [doc_starts, jnp.full((width // 2,), jnp.iinfo(jnp.int32).max, doc_starts.dtype)])
    local = jnp.stack([lax.dynamic_slice_in_dim(padded, before[i], width // 2) for i in range(2)])
    inside = jnp.sum((local[:, None, :] <= key_pos[:, :, None]).astype(jnp.int32), axis=2)
    return before[:, None] + inside - 1


def body(query, keys, values, grad_out, doc_starts):
    shard_count = lax.axis_size("seq")
    device_index = lax.axis_index("seq")
    window = ROUNDS
    span_len = query.shape[2]
    kv_heads = keys.shape[3]
    head_dim = query.shape[4]
    group = query.shape[3] // kv_heads
    q = jnp.transpose(query[:, 0], (0, 2, 1, 3))
    grad_o = jnp.transpose(grad_out[:, 0], (0, 2, 1, 3))
    current = jnp.stack([jnp.transpose(keys[:, 0], (0, 2, 1, 3)),
                         jnp.transpose(values[:, 0], (0, 2, 1, 3))], axis=1)
    flat = current.reshape(2, 2, kv_heads * span_len, head_dim)
    spans = forward_chain(flat, shard_count).reshape((window + 1,) + current.shape)
    span_firsts = jnp.stack([device_index, 2 * shard_count - 1 - device_index])
    key_pos = (span_firsts[:, None] - window) * span_len + jnp.arange(
        (window + 1) * span_len, dtype=jnp.int32)[None]
    key_doc = window_docs(doc_starts, key_pos)
    key_doc = key_doc.reshape(2, window + 1, span_len)
    query_doc = key_doc[:, window]
    skip = jnp.sum(key_doc[:, :window, span_len - 1] < query_doc[:, :1], axis=1).astype(jnp.int32)
    attended, grad_q, terms = attention(
        skip, q, grad_o, spans, query_doc[:, None, :], key_doc[:, :, :, None], group)
    term_flat = terms.reshape(window + 1, 2, 2, kv_heads * span_len, head_dim)
    totals = backward_chain(term_flat, shard_count).reshape(current.shape)
    grad_kv = jnp.transpose(totals, (1, 0, 3, 2, 4))[:, :, None]
    return (
        jnp.transpose(attended, (0, 2, 1, 3))[:, None],
        jnp.transpose(grad_q, (0, 2, 1, 3))[:, None],
        grad_kv[0],
        grad_kv[1],
    )


def solution(mesh):
    placed = (
        P("batch", "seq", None, "head", None),
        P("batch", "seq", None, "head", None),
        P("batch", "seq", None, "head", None),
        P("batch", "seq", None, "head", None),
        P("batch"),
    )
    return jax.shard_map(
        body,
        mesh=mesh,
        in_specs=placed,
        out_specs=(
            P("batch", "seq", None, "head", None),
            P("batch", "seq", None, "head", None),
            P("batch", "seq", None, "head", None),
            P("batch", "seq", None, "head", None),
        ),
        check_vma=False,
    )
```

```python
import functools

import jax
import jax.numpy as jnp
from jax import lax
from jax.sharding import PartitionSpec as P

from jax.experimental import pallas as pl
from jax.experimental.pallas import tpu as pltpu

ROUNDS = 16


def greet_neighbours(me, count):
    barrier = pltpu.get_barrier_semaphore()

    @pl.when(me > 0)
    def _():
        pl.semaphore_signal(barrier, 1, device_id={"seq": me - 1})

    @pl.when(me < count - 1)
    def _():
        pl.semaphore_signal(barrier, 1, device_id={"seq": me + 1})

    @pl.when(jnp.logical_and(me > 0, me < count - 1))
    def _():
        pl.semaphore_wait(barrier, 2)

    @pl.when(jnp.logical_or(me == 0, me == count - 1))
    def _():
        pl.semaphore_wait(barrier, 1)


PIECES = 8


def piece_rows(i, total):
    size = total // (PIECES // 2)
    return i // (PIECES // 2), pl.ds((i % (PIECES // 2)) * size, size)


def forward_chain_kernel(count, cur, hist, send_sem, recv_sem, local_sem):
    me = lax.axis_index("seq")
    own = pltpu.make_async_copy(cur, hist.at[ROUNDS], local_sem.at[ROUNDS, 0])
    own.start()
    greet_neighbours(me, count)
    total = cur.shape[2]

    def copies(k, i):
        slot = ROUNDS - k
        kv, rows = piece_rows(i, total)
        src_a = cur.at[0, kv, rows] if k == 1 else hist.at[slot + 1, 0, kv, rows]
        src_b = cur.at[1, kv, rows] if k == 1 else hist.at[slot + 1, 1, kv, rows]
        send_a = pltpu.make_async_remote_copy(
            src_a, hist.at[slot, 0, kv, rows], send_sem.at[slot, 0, i], recv_sem.at[slot, 0, i],
            device_id={"seq": me + 1})
        send_b = pltpu.make_async_remote_copy(
            src_b, hist.at[slot, 1, kv, rows], send_sem.at[slot, 1, i], recv_sem.at[slot, 1, i],
            device_id={"seq": me - 1})
        local_b = pltpu.make_async_copy(src_a, hist.at[slot, 1, kv, rows], local_sem.at[slot, i])
        return send_a, send_b, local_b

    def a_sends(k):
        return jnp.logical_and(me < count - 1, me >= k - 1)

    def receive(k, i):
        send_a, send_b, local_b = copies(k, i)
        pl.when(me >= k)(send_a.wait_recv)
        pl.when(me < count - 1)(send_b.wait_recv)
        pl.when(me == count - 1)(local_b.wait)

    for k in range(1, ROUNDS + 1):
        for i in range(PIECES):
            if k > 1:
                receive(k - 1, i)
            send_a, send_b, local_b = copies(k, i)
            pl.when(a_sends(k))(send_a.start)
            pl.when(me > 0)(send_b.start)
            pl.when(me == count - 1)(local_b.start)

        @pl.when(me < k)
        def _():
            hist[ROUNDS - k, 0] = jnp.zeros(hist.shape[2:], hist.dtype)

    for i in range(PIECES):
        receive(ROUNDS, i)
    for k in range(1, ROUNDS + 1):
        for i in range(PIECES):
            send_a, send_b, _ = copies(k, i)
            pl.when(a_sends(k))(send_a.wait_send)
            pl.when(me > 0)(send_b.wait_send)
    own.wait()


def backward_chain_kernel(count, terms, out, send_buf, recv_buf, send_sem, recv_sem, local_sem):
    me = lax.axis_index("seq")
    greet_neighbours(me, count)
    total = terms.shape[3]

    def copies(t, i):
        slot = t - 1
        kv, rows = piece_rows(i, total)
        send_a = pltpu.make_async_remote_copy(
            send_buf.at[slot, 0, kv, rows], recv_buf.at[slot, 0, kv, rows],
            send_sem.at[slot, 0, i], recv_sem.at[slot, 0, i], device_id={"seq": me - 1})
        send_b = pltpu.make_async_remote_copy(
            send_buf.at[slot, 1, kv, rows], recv_buf.at[slot, 1, kv, rows],
            send_sem.at[slot, 1, i], recv_sem.at[slot, 1, i], device_id={"seq": me + 1})
        local_b = pltpu.make_async_copy(
            send_buf.at[slot, 1, kv, rows], recv_buf.at[slot, 0, kv, rows], local_sem.at[slot, i])
        return send_a, send_b, local_b

    def start(t, i):
        send_a, send_b, local_b = copies(t, i)
        pl.when(me > 0)(send_a.start)
        pl.when(me < count - 1)(send_b.start)
        pl.when(me == count - 1)(local_b.start)

    for i in range(PIECES):
        kv, rows = piece_rows(i, total)
        send_buf[0, :, kv, rows] = terms[0, :, kv, rows].astype(send_buf.dtype)
        start(1, i)
    for t in range(1, ROUNDS + 1):
        slot = t - 1
        for i in range(PIECES):
            kv, rows = piece_rows(i, total)
            send_a, send_b, local_b = copies(t, i)
            pl.when(me < count - 1)(send_a.wait_recv)
            pl.when(me == count - 1)(local_b.wait)
            pl.when(me > 0)(send_b.wait_recv)
            total_a = recv_buf[slot, 0, kv, rows].astype(jnp.float32) + terms[t, 0, kv, rows]
            if t < ROUNDS:
                send_buf[t, 0, kv, rows] = total_a.astype(send_buf.dtype)
            else:
                out[0, kv, rows] = total_a.astype(out.dtype)

            @pl.when(me > 0)
            def _():
                total_b = recv_buf[slot, 1, kv, rows].astype(jnp.float32) + terms[t, 1, kv, rows]
                if t < ROUNDS:
                    send_buf[t, 1, kv, rows] = total_b.astype(send_buf.dtype)
                else:
                    out[1, kv, rows] = total_b.astype(out.dtype)

            @pl.when(me == 0)
            def _():
                total_b = terms[t, 1, kv, rows]
                if t < ROUNDS:
                    send_buf[t, 1, kv, rows] = total_b.astype(send_buf.dtype)
                else:
                    out[1, kv, rows] = total_b.astype(out.dtype)

            if t < ROUNDS:
                start(t + 1, i)
    for t in range(1, ROUNDS + 1):
        for i in range(PIECES):
            send_a, send_b, _ = copies(t, i)
            pl.when(me > 0)(send_a.wait_send)
            pl.when(me < count - 1)(send_b.wait_send)


def forward_chain(current, count):
    shape = current.shape
    return pl.pallas_call(
        functools.partial(forward_chain_kernel, count),
        out_shape=jax.ShapeDtypeStruct((ROUNDS + 1,) + shape, current.dtype),
        in_specs=[pl.BlockSpec(memory_space=pltpu.VMEM)],
        out_specs=pl.BlockSpec(memory_space=pltpu.VMEM),
        scratch_shapes=[
            pltpu.SemaphoreType.DMA((ROUNDS, 2, PIECES)),
            pltpu.SemaphoreType.DMA((ROUNDS, 2, PIECES)),
            pltpu.SemaphoreType.DMA((ROUNDS + 1, PIECES)),
        ],
        compiler_params=pltpu.CompilerParams(
            collective_id=0, has_side_effects=True, vmem_limit_bytes=48 * 1024 * 1024),
    )(current)


def backward_chain(terms, count):
    shape = terms.shape[1:]
    return pl.pallas_call(
        functools.partial(backward_chain_kernel, count),
        out_shape=jax.ShapeDtypeStruct(shape, jnp.bfloat16),
        in_specs=[pl.BlockSpec(memory_space=pltpu.VMEM)],
        out_specs=pl.BlockSpec(memory_space=pltpu.VMEM),
        scratch_shapes=[
            pltpu.VMEM((ROUNDS,) + shape, jnp.bfloat16),
            pltpu.VMEM((ROUNDS,) + shape, jnp.bfloat16),
            pltpu.SemaphoreType.DMA((ROUNDS, 2, PIECES)),
            pltpu.SemaphoreType.DMA((ROUNDS, 2, PIECES)),
            pltpu.SemaphoreType.DMA((ROUNDS, PIECES)),
        ],
        compiler_params=pltpu.CompilerParams(
            collective_id=1, has_side_effects=True, vmem_limit_bytes=60 * 1024 * 1024),
    )(terms)


def attention_kernel(skip_ref, q_ref, do_ref, win_ref, qdoc_ref, kdoc_ref,
                     o_ref, dq_ref, terms_ref, cache):
    stream = pl.program_id(0)
    first = skip_ref[stream]
    group, span_len, head_dim = q_ref.shape[1:]
    rows = group * span_len
    last = win_ref.shape[0] - 1
    scale = head_dim ** (-0.5)
    q = q_ref[0].reshape(rows, head_dim)
    grad_output = do_ref[0].reshape(rows, head_dim)
    q_t = q.astype(jnp.float32).T.astype(jnp.bfloat16)
    grad_t = grad_output.astype(jnp.float32).T
    grad_t_low = grad_t.astype(jnp.bfloat16)
    query_doc = qdoc_ref[0]
    later = lax.broadcasted_iota(jnp.int32, (span_len, span_len), 0) > lax.broadcasted_iota(
        jnp.int32, (span_len, span_len), 1)

    def scores(j, causal):
        sc = jnp.dot(win_ref[j, 0, 0, 0], q_t, preferred_element_type=jnp.float32) * scale
        allowed = kdoc_ref[0, j] == query_doc
        if causal:
            allowed = jnp.logical_and(allowed, jnp.logical_not(later))
        allowed = jnp.tile(allowed, (1, group))
        sc = jnp.where(allowed, sc, -jnp.inf)
        cache[j] = sc
        return sc

    sc = scores(last, True)
    top = jnp.max(sc, axis=0, keepdims=True)
    total = jnp.sum(jnp.exp(sc - top), axis=0, keepdims=True)

    def stat_step(j, carry):
        top, total = carry
        sc = scores(j, False)
        new_top = jnp.maximum(top, jnp.max(sc, axis=0, keepdims=True))
        total = total * jnp.exp(top - new_top) + jnp.sum(jnp.exp(sc - new_top), axis=0, keepdims=True)
        return new_top, total

    top, total = lax.fori_loop(first, last, stat_step, (top, total))
    inverse = 1.0 / total

    def out_step(j, acc):
        prob = jnp.exp(cache[j] - top) * inverse
        cache[j] = prob
        value_t = win_ref[j, 0, 1, 0].astype(jnp.float32).T.astype(jnp.bfloat16)
        return acc + jnp.dot(value_t, prob.astype(jnp.bfloat16), preferred_element_type=jnp.float32)

    acc = out_step(last, jnp.zeros((head_dim, rows), jnp.float32))
    acc = lax.fori_loop(first, last, out_step, acc)
    attended_t = acc.astype(jnp.bfloat16)
    o_ref[0] = attended_t.astype(jnp.float32).T.astype(jnp.bfloat16).reshape(group, span_len, head_dim)
    delta = jnp.sum(grad_t * attended_t.astype(jnp.float32), axis=0, keepdims=True)

    def grad_step(j, dq):
        prob = cache[j]
        low = prob.astype(jnp.bfloat16)
        grad_w = jnp.dot(win_ref[j, 0, 1, 0], grad_t_low, preferred_element_type=jnp.float32)
        grad_s = (prob * (grad_w - delta) * scale).astype(jnp.bfloat16)
        terms_ref[j, 0, 0, 0] = jnp.dot(grad_s, q, preferred_element_type=jnp.float32)
        terms_ref[j, 0, 1, 0] = jnp.dot(low, grad_output, preferred_element_type=jnp.float32)
        key_t = win_ref[j, 0, 0, 0].astype(jnp.float32).T.astype(jnp.bfloat16)
        return dq + jnp.dot(key_t, grad_s, preferred_element_type=jnp.float32)

    dq = grad_step(last, jnp.zeros((head_dim, rows), jnp.float32))
    dq = lax.fori_loop(first, last, grad_step, dq)
    dq_ref[0] = dq.T.astype(jnp.bfloat16).reshape(group, span_len, head_dim)

    def clear(j, carry):
        terms_ref[j] = jnp.zeros(terms_ref.shape[1:], terms_ref.dtype)
        return carry

    lax.fori_loop(0, first, clear, 0)


def attention(skip, q, grad_out, window, query_doc, key_doc, group):
    streams, heads, span_len, head_dim = q.shape
    kv_heads = heads // group
    spans = window.shape[0]
    head_block = pl.BlockSpec((1, group, span_len, head_dim), lambda s, h, sk: (s, h, 0, 0))
    return pl.pallas_call(
        attention_kernel,
        out_shape=(
            jax.ShapeDtypeStruct(q.shape, jnp.bfloat16),
            jax.ShapeDtypeStruct(q.shape, jnp.bfloat16),
            jax.ShapeDtypeStruct((spans, streams, 2, kv_heads, span_len, head_dim), jnp.float32),
        ),
        grid_spec=pltpu.PrefetchScalarGridSpec(
            num_scalar_prefetch=1,
            grid=(streams, kv_heads),
            in_specs=[
                head_block,
                head_block,
                pl.BlockSpec((spans, 1, 2, 1, span_len, head_dim), lambda s, h, sk: (0, s, 0, h, 0, 0)),
                pl.BlockSpec((1, 1, span_len), lambda s, h, sk: (s, 0, 0)),
                pl.BlockSpec((1, spans, span_len, 1), lambda s, h, sk: (s, 0, 0, 0)),
            ],
            out_specs=[
                head_block,
                head_block,
                pl.BlockSpec((spans, 1, 2, 1, span_len, head_dim), lambda s, h, sk: (0, s, 0, h, 0, 0)),
            ],
            scratch_shapes=[pltpu.VMEM((spans, span_len, group * span_len), jnp.float32)],
        ),
        compiler_params=pltpu.CompilerParams(vmem_limit_bytes=48 * 1024 * 1024),
    )(skip, q, grad_out, window, query_doc, key_doc)


def window_docs(doc_starts, key_pos):
    width = key_pos.shape[1]
    before = jnp.sum((doc_starts[None, :] < key_pos[:, :1]).astype(jnp.int32), axis=1)
    padded = jnp.concatenate(
        [doc_starts, jnp.full((width // 2,), jnp.iinfo(jnp.int32).max, doc_starts.dtype)])
    local = jnp.stack([lax.dynamic_slice_in_dim(padded, before[i], width // 2) for i in range(2)])
    inside = jnp.sum((local[:, None, :] <= key_pos[:, :, None]).astype(jnp.int32), axis=2)
    return before[:, None] + inside - 1


def body(query, keys, values, grad_out, doc_starts):
    shard_count = lax.axis_size("seq")
    device_index = lax.axis_index("seq")
    window = ROUNDS
    span_len = query.shape[2]
    kv_heads = keys.shape[3]
    head_dim = query.shape[4]
    group = query.shape[3] // kv_heads
    q = jnp.transpose(query[:, 0], (0, 2, 1, 3))
    grad_o = jnp.transpose(grad_out[:, 0], (0, 2, 1, 3))
    current = jnp.stack([jnp.transpose(keys[:, 0], (0, 2, 1, 3)),
                         jnp.transpose(values[:, 0], (0, 2, 1, 3))], axis=1)
    flat = current.reshape(2, 2, kv_heads * span_len, head_dim)
    spans = forward_chain(flat, shard_count).reshape((window + 1,) + current.shape)
    span_firsts = jnp.stack([device_index, 2 * shard_count - 1 - device_index])
    key_pos = (span_firsts[:, None] - window) * span_len + jnp.arange(
        (window + 1) * span_len, dtype=jnp.int32)[None]
    key_doc = window_docs(doc_starts, key_pos)
    key_doc = key_doc.reshape(2, window + 1, span_len)
    query_doc = key_doc[:, window]
    skip = jnp.sum(key_doc[:, :window, span_len - 1] < query_doc[:, :1], axis=1).astype(jnp.int32)
    attended, grad_q, terms = attention(
        skip, q, grad_o, spans, query_doc[:, None, :], key_doc[:, :, :, None], group)
    term_flat = terms.reshape(window + 1, 2, 2, kv_heads * span_len, head_dim)
    totals = backward_chain(term_flat, shard_count).reshape(current.shape)
    grad_kv = jnp.transpose(totals, (1, 0, 3, 2, 4))[:, :, None]
    return (
        jnp.transpose(attended, (0, 2, 1, 3))[:, None],
        jnp.transpose(grad_q, (0, 2, 1, 3))[:, None],
        grad_kv[0],
        grad_kv[1],
    )


def solution(mesh):
    placed = (
        P("batch", "seq", None, "head", None),
        P("batch", "seq", None, "head", None),
        P("batch", "seq", None, "head", None),
        P("batch", "seq", None, "head", None),
        P("batch"),
    )
    return jax.shard_map(
        body,
        mesh=mesh,
        in_specs=placed,
        out_specs=(
            P("batch", "seq", None, "head", None),
            P("batch", "seq", None, "head", None),
            P("batch", "seq", None, "head", None),
            P("batch", "seq", None, "head", None),
        ),
        check_vma=False,
    )
```

```python
import functools

import jax
import jax.numpy as jnp
from jax import lax
from jax.sharding import PartitionSpec as P

from jax.experimental import pallas as pl
from jax.experimental.pallas import tpu as pltpu

ROUNDS = 16


def greet_neighbours(me, count):
    barrier = pltpu.get_barrier_semaphore()

    @pl.when(me > 0)
    def _():
        pl.semaphore_signal(barrier, 1, device_id={"seq": me - 1})

    @pl.when(me < count - 1)
    def _():
        pl.semaphore_signal(barrier, 1, device_id={"seq": me + 1})

    @pl.when(jnp.logical_and(me > 0, me < count - 1))
    def _():
        pl.semaphore_wait(barrier, 2)

    @pl.when(jnp.logical_or(me == 0, me == count - 1))
    def _():
        pl.semaphore_wait(barrier, 1)


PIECES = 8


def piece_rows(i, total):
    size = total // (PIECES // 2)
    return i // (PIECES // 2), pl.ds((i % (PIECES // 2)) * size, size)


def forward_chain_kernel(count, cur, hist, send_sem, recv_sem, local_sem):
    me = lax.axis_index("seq")
    own = pltpu.make_async_copy(cur, hist.at[ROUNDS], local_sem.at[ROUNDS, 0])
    own.start()
    greet_neighbours(me, count)
    total = cur.shape[2]

    def copies(k, i):
        slot = ROUNDS - k
        kv, rows = piece_rows(i, total)
        src_a = cur.at[0, kv, rows] if k == 1 else hist.at[slot + 1, 0, kv, rows]
        src_b = cur.at[1, kv, rows] if k == 1 else hist.at[slot + 1, 1, kv, rows]
        send_a = pltpu.make_async_remote_copy(
            src_a, hist.at[slot, 0, kv, rows], send_sem.at[slot, 0, i], recv_sem.at[slot, 0, i],
            device_id={"seq": me + 1})
        send_b = pltpu.make_async_remote_copy(
            src_b, hist.at[slot, 1, kv, rows], send_sem.at[slot, 1, i], recv_sem.at[slot, 1, i],
            device_id={"seq": me - 1})
        local_b = pltpu.make_async_copy(src_a, hist.at[slot, 1, kv, rows], local_sem.at[slot, i])
        return send_a, send_b, local_b

    def a_sends(k):
        return jnp.logical_and(me < count - 1, me >= k - 1)

    def receive(k, i):
        send_a, send_b, local_b = copies(k, i)
        pl.when(me >= k)(send_a.wait_recv)
        pl.when(me < count - 1)(send_b.wait_recv)
        pl.when(me == count - 1)(local_b.wait)

    for k in range(1, ROUNDS + 1):
        for i in range(PIECES):
            if k > 1:
                receive(k - 1, i)
            send_a, send_b, local_b = copies(k, i)
            pl.when(a_sends(k))(send_a.start)
            pl.when(me > 0)(send_b.start)
            pl.when(me == count - 1)(local_b.start)

        @pl.when(me < k)
        def _():
            hist[ROUNDS - k, 0] = jnp.zeros(hist.shape[2:], hist.dtype)

    for i in range(PIECES):
        receive(ROUNDS, i)
    for k in range(1, ROUNDS + 1):
        for i in range(PIECES):
            send_a, send_b, _ = copies(k, i)
            pl.when(a_sends(k))(send_a.wait_send)
            pl.when(me > 0)(send_b.wait_send)
    own.wait()


def backward_chain_kernel(count, terms, out, send_buf, recv_buf, send_sem, recv_sem, local_sem):
    me = lax.axis_index("seq")
    greet_neighbours(me, count)
    total = terms.shape[3]

    def copies(t, i):
        slot = t - 1
        kv, rows = piece_rows(i, total)
        send_a = pltpu.make_async_remote_copy(
            send_buf.at[slot, 0, kv, rows], recv_buf.at[slot, 0, kv, rows],
            send_sem.at[slot, 0, i], recv_sem.at[slot, 0, i], device_id={"seq": me - 1})
        send_b = pltpu.make_async_remote_copy(
            send_buf.at[slot, 1, kv, rows], recv_buf.at[slot, 1, kv, rows],
            send_sem.at[slot, 1, i], recv_sem.at[slot, 1, i], device_id={"seq": me + 1})
        local_b = pltpu.make_async_copy(
            send_buf.at[slot, 1, kv, rows], recv_buf.at[slot, 0, kv, rows], local_sem.at[slot, i])
        return send_a, send_b, local_b

    def start(t, i):
        send_a, send_b, local_b = copies(t, i)
        pl.when(me > 0)(send_a.start)
        pl.when(me < count - 1)(send_b.start)
        pl.when(me == count - 1)(local_b.start)

    for i in range(PIECES):
        kv, rows = piece_rows(i, total)
        send_buf[0, :, kv, rows] = terms[0, :, kv, rows].astype(send_buf.dtype)
        start(1, i)
    for t in range(1, ROUNDS + 1):
        slot = t - 1
        for i in range(PIECES):
            kv, rows = piece_rows(i, total)
            send_a, send_b, local_b = copies(t, i)
            pl.when(me < count - 1)(send_a.wait_recv)
            pl.when(me == count - 1)(local_b.wait)
            pl.when(me > 0)(send_b.wait_recv)
            total_a = recv_buf[slot, 0, kv, rows].astype(jnp.float32) + terms[t, 0, kv, rows]
            if t < ROUNDS:
                send_buf[t, 0, kv, rows] = total_a.astype(send_buf.dtype)
            else:
                out[0, kv, rows] = total_a.astype(out.dtype)

            @pl.when(me > 0)
            def _():
                total_b = recv_buf[slot, 1, kv, rows].astype(jnp.float32) + terms[t, 1, kv, rows]
                if t < ROUNDS:
                    send_buf[t, 1, kv, rows] = total_b.astype(send_buf.dtype)
                else:
                    out[1, kv, rows] = total_b.astype(out.dtype)

            @pl.when(me == 0)
            def _():
                total_b = terms[t, 1, kv, rows]
                if t < ROUNDS:
                    send_buf[t, 1, kv, rows] = total_b.astype(send_buf.dtype)
                else:
                    out[1, kv, rows] = total_b.astype(out.dtype)

            if t < ROUNDS:
                start(t + 1, i)
    for t in range(1, ROUNDS + 1):
        for i in range(PIECES):
            send_a, send_b, _ = copies(t, i)
            pl.when(me > 0)(send_a.wait_send)
            pl.when(me < count - 1)(send_b.wait_send)


def forward_chain(current, count):
    shape = current.shape
    return pl.pallas_call(
        functools.partial(forward_chain_kernel, count),
        out_shape=jax.ShapeDtypeStruct((ROUNDS + 1,) + shape, current.dtype),
        in_specs=[pl.BlockSpec(memory_space=pltpu.VMEM)],
        out_specs=pl.BlockSpec(memory_space=pltpu.VMEM),
        scratch_shapes=[
            pltpu.SemaphoreType.DMA((ROUNDS, 2, PIECES)),
            pltpu.SemaphoreType.DMA((ROUNDS, 2, PIECES)),
            pltpu.SemaphoreType.DMA((ROUNDS + 1, PIECES)),
        ],
        compiler_params=pltpu.CompilerParams(
            collective_id=0, has_side_effects=True, vmem_limit_bytes=48 * 1024 * 1024),
    )(current)


def backward_chain(terms, count):
    shape = terms.shape[1:]
    return pl.pallas_call(
        functools.partial(backward_chain_kernel, count),
        out_shape=jax.ShapeDtypeStruct(shape, jnp.bfloat16),
        in_specs=[pl.BlockSpec(memory_space=pltpu.VMEM)],
        out_specs=pl.BlockSpec(memory_space=pltpu.VMEM),
        scratch_shapes=[
            pltpu.VMEM((ROUNDS,) + shape, jnp.bfloat16),
            pltpu.VMEM((ROUNDS,) + shape, jnp.bfloat16),
            pltpu.SemaphoreType.DMA((ROUNDS, 2, PIECES)),
            pltpu.SemaphoreType.DMA((ROUNDS, 2, PIECES)),
            pltpu.SemaphoreType.DMA((ROUNDS, PIECES)),
        ],
        compiler_params=pltpu.CompilerParams(
            collective_id=1, has_side_effects=True, vmem_limit_bytes=60 * 1024 * 1024),
    )(terms)


def attention_kernel(skip_ref, first_ref, q_ref, do_ref, win_ref, qstart_ref,
                     o_ref, dq_ref, terms_ref, cache):
    stream = pl.program_id(0)
    first = skip_ref[stream]
    group, span_len, head_dim = q_ref.shape[1:]
    rows = group * span_len
    last = win_ref.shape[0] - 1
    scale = head_dim ** (-0.5)
    q = q_ref[0].reshape(rows, head_dim)
    grad_output = do_ref[0].reshape(rows, head_dim)
    q_t = q.astype(jnp.float32).T.astype(jnp.bfloat16)
    grad_t = grad_output.astype(jnp.float32).T
    grad_t_low = grad_t.astype(jnp.bfloat16)
    query_start = qstart_ref[0]
    span = first_ref[stream]
    query_pos = lax.broadcasted_iota(jnp.int32, (1, span_len), 1) + span * span_len
    key_offset = lax.broadcasted_iota(jnp.int32, (span_len, span_len), 0)

    def scores(j, causal):
        sc = jnp.dot(win_ref[j, 0, 0, 0], q_t, preferred_element_type=jnp.float32) * scale
        key_pos = key_offset + (span - last + j) * span_len
        allowed = jnp.logical_and(key_pos >= query_start, key_pos <= query_pos)
        allowed = jnp.tile(allowed, (1, group))
        sc = jnp.where(allowed, sc, -jnp.inf)
        cache[j] = sc
        return sc

    sc = scores(last, True)
    top = jnp.max(sc, axis=0, keepdims=True)
    total = jnp.sum(jnp.exp(sc - top), axis=0, keepdims=True)

    def stat_step(j, carry):
        top, total = carry
        sc = scores(j, False)
        new_top = jnp.maximum(top, jnp.max(sc, axis=0, keepdims=True))
        total = total * jnp.exp(top - new_top) + jnp.sum(jnp.exp(sc - new_top), axis=0, keepdims=True)
        return new_top, total

    top, total = lax.fori_loop(first, last, stat_step, (top, total))
    inverse = 1.0 / total

    def out_step(j, acc):
        prob = jnp.exp(cache[j] - top) * inverse
        cache[j] = prob
        value_t = win_ref[j, 0, 1, 0].astype(jnp.float32).T.astype(jnp.bfloat16)
        return acc + jnp.dot(value_t, prob.astype(jnp.bfloat16), preferred_element_type=jnp.float32)

    acc = out_step(last, jnp.zeros((head_dim, rows), jnp.float32))
    acc = lax.fori_loop(first, last, out_step, acc)
    attended_t = acc.astype(jnp.bfloat16)
    o_ref[0] = attended_t.astype(jnp.float32).T.astype(jnp.bfloat16).reshape(group, span_len, head_dim)
    delta = jnp.sum(grad_t * attended_t.astype(jnp.float32), axis=0, keepdims=True)

    def grad_step(j, dq):
        prob = cache[j]
        low = prob.astype(jnp.bfloat16)
        grad_w = jnp.dot(win_ref[j, 0, 1, 0], grad_t_low, preferred_element_type=jnp.float32)
        grad_s = (prob * (grad_w - delta) * scale).astype(jnp.bfloat16)
        terms_ref[j, 0, 0, 0] = jnp.dot(grad_s, q, preferred_element_type=jnp.float32)
        terms_ref[j, 0, 1, 0] = jnp.dot(low, grad_output, preferred_element_type=jnp.float32)
        key_t = win_ref[j, 0, 0, 0].astype(jnp.float32).T.astype(jnp.bfloat16)
        return dq + jnp.dot(key_t, grad_s, preferred_element_type=jnp.float32)

    dq = grad_step(last, jnp.zeros((head_dim, rows), jnp.float32))
    dq = lax.fori_loop(first, last, grad_step, dq)
    dq_ref[0] = dq.T.astype(jnp.bfloat16).reshape(group, span_len, head_dim)

    def clear(j, carry):
        terms_ref[j] = jnp.zeros(terms_ref.shape[1:], terms_ref.dtype)
        return carry

    lax.fori_loop(0, first, clear, 0)


def attention(skip, span_firsts, q, grad_out, window, query_start, group):
    streams, heads, span_len, head_dim = q.shape
    kv_heads = heads // group
    spans = window.shape[0]
    head_block = pl.BlockSpec((1, group, span_len, head_dim), lambda s, h, sk, sf: (s, h, 0, 0))
    return pl.pallas_call(
        attention_kernel,
        out_shape=(
            jax.ShapeDtypeStruct(q.shape, jnp.bfloat16),
            jax.ShapeDtypeStruct(q.shape, jnp.bfloat16),
            jax.ShapeDtypeStruct((spans, streams, 2, kv_heads, span_len, head_dim), jnp.float32),
        ),
        grid_spec=pltpu.PrefetchScalarGridSpec(
            num_scalar_prefetch=2,
            grid=(streams, kv_heads),
            in_specs=[
                head_block,
                head_block,
                pl.BlockSpec((spans, 1, 2, 1, span_len, head_dim), lambda s, h, sk, sf: (0, s, 0, h, 0, 0)),
                pl.BlockSpec((1, 1, span_len), lambda s, h, sk, sf: (s, 0, 0)),
            ],
            out_specs=[
                head_block,
                head_block,
                pl.BlockSpec((spans, 1, 2, 1, span_len, head_dim), lambda s, h, sk, sf: (0, s, 0, h, 0, 0)),
            ],
            scratch_shapes=[pltpu.VMEM((spans, span_len, group * span_len), jnp.float32)],
        ),
        compiler_params=pltpu.CompilerParams(vmem_limit_bytes=48 * 1024 * 1024),
    )(skip, span_firsts, q, grad_out, window, query_start)


def body(query, keys, values, grad_out, doc_starts):
    shard_count = lax.axis_size("seq")
    device_index = lax.axis_index("seq")
    window = ROUNDS
    span_len = query.shape[2]
    kv_heads = keys.shape[3]
    head_dim = query.shape[4]
    group = query.shape[3] // kv_heads
    q = jnp.transpose(query[:, 0], (0, 2, 1, 3))
    grad_o = jnp.transpose(grad_out[:, 0], (0, 2, 1, 3))
    current = jnp.stack([jnp.transpose(keys[:, 0], (0, 2, 1, 3)),
                         jnp.transpose(values[:, 0], (0, 2, 1, 3))], axis=1)
    flat = current.reshape(2, 2, kv_heads * span_len, head_dim)
    spans = forward_chain(flat, shard_count).reshape((window + 1,) + current.shape)
    span_firsts = jnp.stack([device_index, 2 * shard_count - 1 - device_index]).astype(jnp.int32)
    query_pos = span_firsts[:, None] * span_len + jnp.arange(span_len, dtype=jnp.int32)[None]
    query_start = jnp.max(
        jnp.where(doc_starts[None, None, :] <= query_pos[:, :, None], doc_starts[None, None, :], -1), axis=2)
    span_last = (span_firsts[:, None] - window + jnp.arange(window, dtype=jnp.int32)[None]) * span_len + span_len - 1
    skip = jnp.sum(span_last < query_start[:, :1], axis=1).astype(jnp.int32)
    attended, grad_q, terms = attention(
        skip, span_firsts, q, grad_o, spans, query_start[:, None, :], group)
    term_flat = terms.reshape(window + 1, 2, 2, kv_heads * span_len, head_dim)
    totals = backward_chain(term_flat, shard_count).reshape(current.shape)
    grad_kv = jnp.transpose(totals, (1, 0, 3, 2, 4))[:, :, None]
    return (
        jnp.transpose(attended, (0, 2, 1, 3))[:, None],
        jnp.transpose(grad_q, (0, 2, 1, 3))[:, None],
        grad_kv[0],
        grad_kv[1],
    )


def solution(mesh):
    placed = (
        P("batch", "seq", None, "head", None),
        P("batch", "seq", None, "head", None),
        P("batch", "seq", None, "head", None),
        P("batch", "seq", None, "head", None),
        P("batch"),
    )
    return jax.shard_map(
        body,
        mesh=mesh,
        in_specs=placed,
        out_specs=(
            P("batch", "seq", None, "head", None),
            P("batch", "seq", None, "head", None),
            P("batch", "seq", None, "head", None),
            P("batch", "seq", None, "head", None),
        ),
        check_vma=False,
    )
```

```python
import functools

import jax
import jax.numpy as jnp
from jax import lax
from jax.sharding import PartitionSpec as P

from jax.experimental import pallas as pl
from jax.experimental.pallas import tpu as pltpu

ROUNDS = 16


def greet_neighbours(me, count):
    barrier = pltpu.get_barrier_semaphore()

    @pl.when(me > 0)
    def _():
        pl.semaphore_signal(barrier, 1, device_id={"seq": me - 1})

    @pl.when(me < count - 1)
    def _():
        pl.semaphore_signal(barrier, 1, device_id={"seq": me + 1})

    @pl.when(jnp.logical_and(me > 0, me < count - 1))
    def _():
        pl.semaphore_wait(barrier, 2)

    @pl.when(jnp.logical_or(me == 0, me == count - 1))
    def _():
        pl.semaphore_wait(barrier, 1)


PIECES = 8


def piece_rows(i, total):
    size = total // (PIECES // 2)
    return i // (PIECES // 2), pl.ds((i % (PIECES // 2)) * size, size)


def forward_chain_kernel(count, cur, hist, send_sem, recv_sem, local_sem):
    me = lax.axis_index("seq")
    own = pltpu.make_async_copy(cur, hist.at[ROUNDS], local_sem.at[ROUNDS, 0])
    own.start()
    greet_neighbours(me, count)
    total = cur.shape[2]

    def copies(k, i):
        slot = ROUNDS - k
        kv, rows = piece_rows(i, total)
        src_a = cur.at[0, kv, rows] if k == 1 else hist.at[slot + 1, 0, kv, rows]
        src_b = cur.at[1, kv, rows] if k == 1 else hist.at[slot + 1, 1, kv, rows]
        send_a = pltpu.make_async_remote_copy(
            src_a, hist.at[slot, 0, kv, rows], send_sem.at[slot, 0, i], recv_sem.at[slot, 0, i],
            device_id={"seq": me + 1})
        send_b = pltpu.make_async_remote_copy(
            src_b, hist.at[slot, 1, kv, rows], send_sem.at[slot, 1, i], recv_sem.at[slot, 1, i],
            device_id={"seq": me - 1})
        local_b = pltpu.make_async_copy(src_a, hist.at[slot, 1, kv, rows], local_sem.at[slot, i])
        return send_a, send_b, local_b

    def a_sends(k):
        return jnp.logical_and(me < count - 1, me >= k - 1)

    def receive(k, i):
        send_a, send_b, local_b = copies(k, i)
        pl.when(me >= k)(send_a.wait_recv)
        pl.when(me < count - 1)(send_b.wait_recv)
        pl.when(me == count - 1)(local_b.wait)

    for k in range(1, ROUNDS + 1):
        for i in range(PIECES):
            if k > 1:
                receive(k - 1, i)
            send_a, send_b, local_b = copies(k, i)
            pl.when(a_sends(k))(send_a.start)
            pl.when(me > 0)(send_b.start)
            pl.when(me == count - 1)(local_b.start)

        @pl.when(me < k)
        def _():
            hist[ROUNDS - k, 0] = jnp.zeros(hist.shape[2:], hist.dtype)

    for i in range(PIECES):
        receive(ROUNDS, i)
    for k in range(1, ROUNDS + 1):
        for i in range(PIECES):
            send_a, send_b, _ = copies(k, i)
            pl.when(a_sends(k))(send_a.wait_send)
            pl.when(me > 0)(send_b.wait_send)
    own.wait()


def backward_chain_kernel(count, terms, out, send_buf, recv_buf, send_sem, recv_sem, local_sem):
    me = lax.axis_index("seq")
    greet_neighbours(me, count)
    total = terms.shape[3]

    def copies(t, i):
        slot = t - 1
        kv, rows = piece_rows(i, total)
        send_a = pltpu.make_async_remote_copy(
            send_buf.at[slot, 0, kv, rows], recv_buf.at[slot, 0, kv, rows],
            send_sem.at[slot, 0, i], recv_sem.at[slot, 0, i], device_id={"seq": me - 1})
        send_b = pltpu.make_async_remote_copy(
            send_buf.at[slot, 1, kv, rows], recv_buf.at[slot, 1, kv, rows],
            send_sem.at[slot, 1, i], recv_sem.at[slot, 1, i], device_id={"seq": me + 1})
        local_b = pltpu.make_async_copy(
            send_buf.at[slot, 1, kv, rows], recv_buf.at[slot, 0, kv, rows], local_sem.at[slot, i])
        return send_a, send_b, local_b

    def start(t, i):
        send_a, send_b, local_b = copies(t, i)
        pl.when(me > 0)(send_a.start)
        pl.when(me < count - 1)(send_b.start)
        pl.when(me == count - 1)(local_b.start)

    for i in range(PIECES):
        kv, rows = piece_rows(i, total)
        send_buf[0, :, kv, rows] = terms[0, :, kv, rows].astype(send_buf.dtype)
        start(1, i)
    for t in range(1, ROUNDS + 1):
        slot = t - 1
        for i in range(PIECES):
            kv, rows = piece_rows(i, total)
            send_a, send_b, local_b = copies(t, i)
            pl.when(me < count - 1)(send_a.wait_recv)
            pl.when(me == count - 1)(local_b.wait)
            pl.when(me > 0)(send_b.wait_recv)
            total_a = recv_buf[slot, 0, kv, rows].astype(jnp.float32) + terms[t, 0, kv, rows]
            if t < ROUNDS:
                send_buf[t, 0, kv, rows] = total_a.astype(send_buf.dtype)
            else:
                out[0, kv, rows] = total_a.astype(out.dtype)

            @pl.when(me > 0)
            def _():
                total_b = recv_buf[slot, 1, kv, rows].astype(jnp.float32) + terms[t, 1, kv, rows]
                if t < ROUNDS:
                    send_buf[t, 1, kv, rows] = total_b.astype(send_buf.dtype)
                else:
                    out[1, kv, rows] = total_b.astype(out.dtype)

            @pl.when(me == 0)
            def _():
                total_b = terms[t, 1, kv, rows]
                if t < ROUNDS:
                    send_buf[t, 1, kv, rows] = total_b.astype(send_buf.dtype)
                else:
                    out[1, kv, rows] = total_b.astype(out.dtype)

            if t < ROUNDS:
                start(t + 1, i)
    for t in range(1, ROUNDS + 1):
        for i in range(PIECES):
            send_a, send_b, _ = copies(t, i)
            pl.when(me > 0)(send_a.wait_send)
            pl.when(me < count - 1)(send_b.wait_send)


def forward_chain(current, count):
    shape = current.shape
    return pl.pallas_call(
        functools.partial(forward_chain_kernel, count),
        out_shape=jax.ShapeDtypeStruct((ROUNDS + 1,) + shape, current.dtype),
        in_specs=[pl.BlockSpec(memory_space=pltpu.VMEM)],
        out_specs=pl.BlockSpec(memory_space=pltpu.VMEM),
        scratch_shapes=[
            pltpu.SemaphoreType.DMA((ROUNDS, 2, PIECES)),
            pltpu.SemaphoreType.DMA((ROUNDS, 2, PIECES)),
            pltpu.SemaphoreType.DMA((ROUNDS + 1, PIECES)),
        ],
        compiler_params=pltpu.CompilerParams(
            collective_id=0, has_side_effects=True, vmem_limit_bytes=48 * 1024 * 1024),
    )(current)


def backward_chain(terms, count):
    shape = terms.shape[1:]
    return pl.pallas_call(
        functools.partial(backward_chain_kernel, count),
        out_shape=jax.ShapeDtypeStruct(shape, jnp.bfloat16),
        in_specs=[pl.BlockSpec(memory_space=pltpu.VMEM)],
        out_specs=pl.BlockSpec(memory_space=pltpu.VMEM),
        scratch_shapes=[
            pltpu.VMEM((ROUNDS,) + shape, jnp.bfloat16),
            pltpu.VMEM((ROUNDS,) + shape, jnp.bfloat16),
            pltpu.SemaphoreType.DMA((ROUNDS, 2, PIECES)),
            pltpu.SemaphoreType.DMA((ROUNDS, 2, PIECES)),
            pltpu.SemaphoreType.DMA((ROUNDS, PIECES)),
        ],
        compiler_params=pltpu.CompilerParams(
            collective_id=1, has_side_effects=True, vmem_limit_bytes=60 * 1024 * 1024),
    )(terms)


def attention_kernel(skip_ref, first_ref, q_ref, do_ref, win_ref, qstart_ref,
                     o_ref, dq_ref, terms_ref, cache, tops):
    stream = pl.program_id(0)
    first = skip_ref[stream]
    group, span_len, head_dim = q_ref.shape[1:]
    rows = group * span_len
    last = win_ref.shape[0] - 1
    scale = head_dim ** (-0.5)
    q = q_ref[0].reshape(rows, head_dim)
    grad_output = do_ref[0].reshape(rows, head_dim)
    q_t = q.astype(jnp.float32).T.astype(jnp.bfloat16)
    grad_t = grad_output.astype(jnp.float32).T
    grad_t_low = grad_t.astype(jnp.bfloat16)
    query_start = qstart_ref[0]
    span = first_ref[stream]
    query_pos = lax.broadcasted_iota(jnp.int32, (1, span_len), 1) + span * span_len
    key_offset = lax.broadcasted_iota(jnp.int32, (span_len, span_len), 0)

    def scores(j, causal):
        sc = jnp.dot(win_ref[j, 0, 0, 0], q_t, preferred_element_type=jnp.float32) * scale
        key_pos = key_offset + (span - last + j) * span_len
        allowed = jnp.logical_and(key_pos >= query_start, key_pos <= query_pos)
        allowed = jnp.tile(allowed, (1, group))
        return jnp.where(allowed, sc, -jnp.inf)

    sc = scores(last, True)
    top = jnp.max(sc, axis=0, keepdims=True)
    expon = jnp.exp(sc - top)
    cache[last] = expon
    tops[last] = top
    total = jnp.sum(expon, axis=0, keepdims=True)

    def stat_step(j, carry):
        top, total = carry
        sc = scores(j, False)
        new_top = jnp.maximum(top, jnp.max(sc, axis=0, keepdims=True))
        expon = jnp.exp(sc - new_top)
        cache[j] = expon
        tops[j] = new_top
        total = total * jnp.exp(top - new_top) + jnp.sum(expon, axis=0, keepdims=True)
        return new_top, total

    top, total = lax.fori_loop(first, last, stat_step, (top, total))
    inverse = 1.0 / total

    def out_step(j, acc):
        prob = cache[j] * (jnp.exp(tops[j] - top) * inverse)
        cache[j] = prob
        value_t = win_ref[j, 0, 1, 0].astype(jnp.float32).T.astype(jnp.bfloat16)
        return acc + jnp.dot(value_t, prob.astype(jnp.bfloat16), preferred_element_type=jnp.float32)

    acc = out_step(last, jnp.zeros((head_dim, rows), jnp.float32))
    acc = lax.fori_loop(first, last, out_step, acc)
    attended_t = acc.astype(jnp.bfloat16)
    o_ref[0] = attended_t.astype(jnp.float32).T.astype(jnp.bfloat16).reshape(group, span_len, head_dim)
    delta = jnp.sum(grad_t * attended_t.astype(jnp.float32), axis=0, keepdims=True)

    def grad_step(j, dq):
        prob = cache[j]
        low = prob.astype(jnp.bfloat16)
        grad_w = jnp.dot(win_ref[j, 0, 1, 0], grad_t_low, preferred_element_type=jnp.float32)
        grad_s = (prob * (grad_w - delta) * scale).astype(jnp.bfloat16)
        terms_ref[j, 0, 0, 0] = jnp.dot(grad_s, q, preferred_element_type=jnp.float32)
        terms_ref[j, 0, 1, 0] = jnp.dot(low, grad_output, preferred_element_type=jnp.float32)
        key_t = win_ref[j, 0, 0, 0].astype(jnp.float32).T.astype(jnp.bfloat16)
        return dq + jnp.dot(key_t, grad_s, preferred_element_type=jnp.float32)

    dq = grad_step(last, jnp.zeros((head_dim, rows), jnp.float32))
    dq = lax.fori_loop(first, last, grad_step, dq)
    dq_ref[0] = dq.T.astype(jnp.bfloat16).reshape(group, span_len, head_dim)

    def clear(j, carry):
        terms_ref[j] = jnp.zeros(terms_ref.shape[1:], terms_ref.dtype)
        return carry

    lax.fori_loop(0, first, clear, 0)


def attention(skip, span_firsts, q, grad_out, window, query_start, group):
    streams, heads, span_len, head_dim = q.shape
    kv_heads = heads // group
    spans = window.shape[0]
    head_block = pl.BlockSpec((1, group, span_len, head_dim), lambda s, h, sk, sf: (s, h, 0, 0))
    return pl.pallas_call(
        attention_kernel,
        out_shape=(
            jax.ShapeDtypeStruct(q.shape, jnp.bfloat16),
            jax.ShapeDtypeStruct(q.shape, jnp.bfloat16),
            jax.ShapeDtypeStruct((spans, streams, 2, kv_heads, span_len, head_dim), jnp.float32),
        ),
        grid_spec=pltpu.PrefetchScalarGridSpec(
            num_scalar_prefetch=2,
            grid=(streams, kv_heads),
            in_specs=[
                head_block,
                head_block,
                pl.BlockSpec((spans, 1, 2, 1, span_len, head_dim), lambda s, h, sk, sf: (0, s, 0, h, 0, 0)),
                pl.BlockSpec((1, 1, span_len), lambda s, h, sk, sf: (s, 0, 0)),
            ],
            out_specs=[
                head_block,
                head_block,
                pl.BlockSpec((spans, 1, 2, 1, span_len, head_dim), lambda s, h, sk, sf: (0, s, 0, h, 0, 0)),
            ],
            scratch_shapes=[pltpu.VMEM((spans, span_len, group * span_len), jnp.float32),
                            pltpu.VMEM((spans, 1, group * span_len), jnp.float32)],
        ),
        compiler_params=pltpu.CompilerParams(vmem_limit_bytes=48 * 1024 * 1024),
    )(skip, span_firsts, q, grad_out, window, query_start)


def body(query, keys, values, grad_out, doc_starts):
    shard_count = lax.axis_size("seq")
    device_index = lax.axis_index("seq")
    window = ROUNDS
    span_len = query.shape[2]
    kv_heads = keys.shape[3]
    head_dim = query.shape[4]
    group = query.shape[3] // kv_heads
    q = jnp.transpose(query[:, 0], (0, 2, 1, 3))
    grad_o = jnp.transpose(grad_out[:, 0], (0, 2, 1, 3))
    current = jnp.stack([jnp.transpose(keys[:, 0], (0, 2, 1, 3)),
                         jnp.transpose(values[:, 0], (0, 2, 1, 3))], axis=1)
    flat = current.reshape(2, 2, kv_heads * span_len, head_dim)
    spans = forward_chain(flat, shard_count).reshape((window + 1,) + current.shape)
    span_firsts = jnp.stack([device_index, 2 * shard_count - 1 - device_index]).astype(jnp.int32)
    query_pos = span_firsts[:, None] * span_len + jnp.arange(span_len, dtype=jnp.int32)[None]
    query_start = jnp.max(
        jnp.where(doc_starts[None, None, :] <= query_pos[:, :, None], doc_starts[None, None, :], -1), axis=2)
    span_last = (span_firsts[:, None] - window + jnp.arange(window, dtype=jnp.int32)[None]) * span_len + span_len - 1
    skip = jnp.sum(span_last < query_start[:, :1], axis=1).astype(jnp.int32)
    attended, grad_q, terms = attention(
        skip, span_firsts, q, grad_o, spans, query_start[:, None, :], group)
    term_flat = terms.reshape(window + 1, 2, 2, kv_heads * span_len, head_dim)
    totals = backward_chain(term_flat, shard_count).reshape(current.shape)
    grad_kv = jnp.transpose(totals, (1, 0, 3, 2, 4))[:, :, None]
    return (
        jnp.transpose(attended, (0, 2, 1, 3))[:, None],
        jnp.transpose(grad_q, (0, 2, 1, 3))[:, None],
        grad_kv[0],
        grad_kv[1],
    )


def solution(mesh):
    placed = (
        P("batch", "seq", None, "head", None),
        P("batch", "seq", None, "head", None),
        P("batch", "seq", None, "head", None),
        P("batch", "seq", None, "head", None),
        P("batch"),
    )
    return jax.shard_map(
        body,
        mesh=mesh,
        in_specs=placed,
        out_specs=(
            P("batch", "seq", None, "head", None),
            P("batch", "seq", None, "head", None),
            P("batch", "seq", None, "head", None),
            P("batch", "seq", None, "head", None),
        ),
        check_vma=False,
    )
```

```python
import functools

import jax
import jax.numpy as jnp
from jax import lax
from jax.sharding import PartitionSpec as P

from jax.experimental import pallas as pl
from jax.experimental.pallas import tpu as pltpu

ROUNDS = 16


def greet_neighbours(me, count):
    barrier = pltpu.get_barrier_semaphore()

    @pl.when(me > 0)
    def _():
        pl.semaphore_signal(barrier, 1, device_id={"seq": me - 1})

    @pl.when(me < count - 1)
    def _():
        pl.semaphore_signal(barrier, 1, device_id={"seq": me + 1})

    @pl.when(jnp.logical_and(me > 0, me < count - 1))
    def _():
        pl.semaphore_wait(barrier, 2)

    @pl.when(jnp.logical_or(me == 0, me == count - 1))
    def _():
        pl.semaphore_wait(barrier, 1)


PIECES = 8


def piece_rows(i, total):
    size = total // (PIECES // 2)
    return i // (PIECES // 2), pl.ds((i % (PIECES // 2)) * size, size)


def forward_chain_kernel(count, cur, hist, send_sem, recv_sem, local_sem):
    me = lax.axis_index("seq")
    own = pltpu.make_async_copy(cur, hist.at[ROUNDS], local_sem.at[ROUNDS, 0])
    own.start()
    greet_neighbours(me, count)
    total = cur.shape[2]

    def copies(k, i):
        slot = ROUNDS - k
        kv, rows = piece_rows(i, total)
        src_a = cur.at[0, kv, rows] if k == 1 else hist.at[slot + 1, 0, kv, rows]
        src_b = cur.at[1, kv, rows] if k == 1 else hist.at[slot + 1, 1, kv, rows]
        send_a = pltpu.make_async_remote_copy(
            src_a, hist.at[slot, 0, kv, rows], send_sem.at[slot, 0, i], recv_sem.at[slot, 0, i],
            device_id={"seq": me + 1})
        send_b = pltpu.make_async_remote_copy(
            src_b, hist.at[slot, 1, kv, rows], send_sem.at[slot, 1, i], recv_sem.at[slot, 1, i],
            device_id={"seq": me - 1})
        local_b = pltpu.make_async_copy(src_a, hist.at[slot, 1, kv, rows], local_sem.at[slot, i])
        return send_a, send_b, local_b

    def a_sends(k):
        return jnp.logical_and(me < count - 1, me >= k - 1)

    def receive(k, i):
        send_a, send_b, local_b = copies(k, i)
        pl.when(me >= k)(send_a.wait_recv)
        pl.when(me < count - 1)(send_b.wait_recv)
        pl.when(me == count - 1)(local_b.wait)

    for k in range(1, ROUNDS + 1):
        for i in range(PIECES):
            if k > 1:
                receive(k - 1, i)
            send_a, send_b, local_b = copies(k, i)
            pl.when(a_sends(k))(send_a.start)
            pl.when(me > 0)(send_b.start)
            pl.when(me == count - 1)(local_b.start)

        @pl.when(me < k)
        def _():
            hist[ROUNDS - k, 0] = jnp.zeros(hist.shape[2:], hist.dtype)

    for i in range(PIECES):
        receive(ROUNDS, i)
    for k in range(1, ROUNDS + 1):
        for i in range(PIECES):
            send_a, send_b, _ = copies(k, i)
            pl.when(a_sends(k))(send_a.wait_send)
            pl.when(me > 0)(send_b.wait_send)
    own.wait()


def backward_chain_kernel(count, terms, out, send_buf, recv_buf, send_sem, recv_sem, local_sem):
    me = lax.axis_index("seq")
    greet_neighbours(me, count)
    total = terms.shape[3]

    def copies(t, i):
        slot = t - 1
        kv, rows = piece_rows(i, total)
        send_a = pltpu.make_async_remote_copy(
            send_buf.at[slot, 0, kv, rows], recv_buf.at[slot, 0, kv, rows],
            send_sem.at[slot, 0, i], recv_sem.at[slot, 0, i], device_id={"seq": me - 1})
        send_b = pltpu.make_async_remote_copy(
            send_buf.at[slot, 1, kv, rows], recv_buf.at[slot, 1, kv, rows],
            send_sem.at[slot, 1, i], recv_sem.at[slot, 1, i], device_id={"seq": me + 1})
        local_b = pltpu.make_async_copy(
            send_buf.at[slot, 1, kv, rows], recv_buf.at[slot, 0, kv, rows], local_sem.at[slot, i])
        return send_a, send_b, local_b

    def start(t, i):
        send_a, send_b, local_b = copies(t, i)
        pl.when(me > 0)(send_a.start)
        pl.when(me < count - 1)(send_b.start)
        pl.when(me == count - 1)(local_b.start)

    for i in range(PIECES):
        kv, rows = piece_rows(i, total)
        send_buf[0, :, kv, rows] = terms[0, :, kv, rows].astype(send_buf.dtype)
        start(1, i)
    for t in range(1, ROUNDS + 1):
        slot = t - 1
        for i in range(PIECES):
            kv, rows = piece_rows(i, total)
            send_a, send_b, local_b = copies(t, i)
            pl.when(me < count - 1)(send_a.wait_recv)
            pl.when(me == count - 1)(local_b.wait)
            pl.when(me > 0)(send_b.wait_recv)
            total_a = recv_buf[slot, 0, kv, rows].astype(jnp.float32) + terms[t, 0, kv, rows]
            if t < ROUNDS:
                send_buf[t, 0, kv, rows] = total_a.astype(send_buf.dtype)
            else:
                out[0, kv, rows] = total_a.astype(out.dtype)

            @pl.when(me > 0)
            def _():
                total_b = recv_buf[slot, 1, kv, rows].astype(jnp.float32) + terms[t, 1, kv, rows]
                if t < ROUNDS:
                    send_buf[t, 1, kv, rows] = total_b.astype(send_buf.dtype)
                else:
                    out[1, kv, rows] = total_b.astype(out.dtype)

            @pl.when(me == 0)
            def _():
                total_b = terms[t, 1, kv, rows]
                if t < ROUNDS:
                    send_buf[t, 1, kv, rows] = total_b.astype(send_buf.dtype)
                else:
                    out[1, kv, rows] = total_b.astype(out.dtype)

            if t < ROUNDS:
                start(t + 1, i)
    for t in range(1, ROUNDS + 1):
        for i in range(PIECES):
            send_a, send_b, _ = copies(t, i)
            pl.when(me > 0)(send_a.wait_send)
            pl.when(me < count - 1)(send_b.wait_send)


def forward_chain(current, count):
    shape = current.shape
    return pl.pallas_call(
        functools.partial(forward_chain_kernel, count),
        out_shape=jax.ShapeDtypeStruct((ROUNDS + 1,) + shape, current.dtype),
        in_specs=[pl.BlockSpec(memory_space=pltpu.VMEM)],
        out_specs=pl.BlockSpec(memory_space=pltpu.VMEM),
        scratch_shapes=[
            pltpu.SemaphoreType.DMA((ROUNDS, 2, PIECES)),
            pltpu.SemaphoreType.DMA((ROUNDS, 2, PIECES)),
            pltpu.SemaphoreType.DMA((ROUNDS + 1, PIECES)),
        ],
        compiler_params=pltpu.CompilerParams(
            collective_id=0, has_side_effects=True, vmem_limit_bytes=48 * 1024 * 1024),
    )(current)


def backward_chain(terms, count):
    shape = terms.shape[1:]
    return pl.pallas_call(
        functools.partial(backward_chain_kernel, count),
        out_shape=jax.ShapeDtypeStruct(shape, jnp.bfloat16),
        in_specs=[pl.BlockSpec(memory_space=pltpu.VMEM)],
        out_specs=pl.BlockSpec(memory_space=pltpu.VMEM),
        scratch_shapes=[
            pltpu.VMEM((ROUNDS,) + shape, jnp.bfloat16),
            pltpu.VMEM((ROUNDS,) + shape, jnp.bfloat16),
            pltpu.SemaphoreType.DMA((ROUNDS, 2, PIECES)),
            pltpu.SemaphoreType.DMA((ROUNDS, 2, PIECES)),
            pltpu.SemaphoreType.DMA((ROUNDS, PIECES)),
        ],
        compiler_params=pltpu.CompilerParams(
            collective_id=1, has_side_effects=True, vmem_limit_bytes=60 * 1024 * 1024),
    )(terms)


def attention_kernel(skip_ref, first_ref, q_ref, do_ref, win_ref, qstart_ref,
                     o_ref, dq_ref, terms_ref, cache, tops):
    stream = pl.program_id(0)
    first = skip_ref[stream]
    pair = win_ref.shape[3]
    group = q_ref.shape[1] // pair
    span_len, head_dim = q_ref.shape[2:]
    rows = group * span_len
    last = win_ref.shape[0] - 1
    scale = head_dim ** (-0.5)
    heads = range(pair)
    qs = [q_ref[0, h * group:(h + 1) * group].reshape(rows, head_dim) for h in heads]
    grads = [do_ref[0, h * group:(h + 1) * group].reshape(rows, head_dim) for h in heads]
    q_ts = [q.astype(jnp.float32).T.astype(jnp.bfloat16) for q in qs]
    grad_ts = [g.astype(jnp.float32).T for g in grads]
    grad_t_lows = [g.astype(jnp.bfloat16) for g in grad_ts]
    query_start = qstart_ref[0]
    span = first_ref[stream]
    query_pos = lax.broadcasted_iota(jnp.int32, (1, span_len), 1) + span * span_len
    key_offset = lax.broadcasted_iota(jnp.int32, (span_len, span_len), 0)

    def mask(j):
        key_pos = key_offset + (span - last + j) * span_len
        allowed = jnp.logical_and(key_pos >= query_start, key_pos <= query_pos)
        return jnp.tile(allowed, (1, group))

    def scores(j, h, allowed):
        sc = jnp.dot(win_ref[j, 0, 0, h], q_ts[h], preferred_element_type=jnp.float32) * scale
        return jnp.where(allowed, sc, -jnp.inf)

    allowed = mask(last)
    top_list, total_list = [], []
    for h in heads:
        sc = scores(last, h, allowed)
        top = jnp.max(sc, axis=0, keepdims=True)
        expon = jnp.exp(sc - top)
        cache[last, h] = expon
        tops[last, h] = top
        top_list.append(top)
        total_list.append(jnp.sum(expon, axis=0, keepdims=True))

    def stat_step(j, carry):
        top_c, total_c = carry
        allowed = mask(j)
        new_tops, new_totals = [], []
        for h in heads:
            sc = scores(j, h, allowed)
            new_top = jnp.maximum(top_c[h], jnp.max(sc, axis=0, keepdims=True))
            expon = jnp.exp(sc - new_top)
            cache[j, h] = expon
            tops[j, h] = new_top
            new_tops.append(new_top)
            new_totals.append(total_c[h] * jnp.exp(top_c[h] - new_top)
                              + jnp.sum(expon, axis=0, keepdims=True))
        return tuple(new_tops), tuple(new_totals)

    top_list, total_list = lax.fori_loop(first, last, stat_step, (tuple(top_list), tuple(total_list)))
    inverses = [1.0 / t for t in total_list]

    def out_step(j, accs):
        new = []
        for h in heads:
            prob = cache[j, h] * (jnp.exp(tops[j, h] - top_list[h]) * inverses[h])
            cache[j, h] = prob
            value_t = win_ref[j, 0, 1, h].astype(jnp.float32).T.astype(jnp.bfloat16)
            new.append(accs[h] + jnp.dot(value_t, prob.astype(jnp.bfloat16),
                                         preferred_element_type=jnp.float32))
        return tuple(new)

    zero = jnp.zeros((head_dim, rows), jnp.float32)
    accs = out_step(last, tuple(zero for _ in heads))
    accs = lax.fori_loop(first, last, out_step, accs)
    deltas = []
    for h in heads:
        attended_t = accs[h].astype(jnp.bfloat16)
        o_ref[0, h * group:(h + 1) * group] = attended_t.astype(jnp.float32).T.astype(
            jnp.bfloat16).reshape(group, span_len, head_dim)
        deltas.append(jnp.sum(grad_ts[h] * attended_t.astype(jnp.float32), axis=0, keepdims=True))

    def grad_step(j, dqs):
        new = []
        for h in heads:
            prob = cache[j, h]
            low = prob.astype(jnp.bfloat16)
            grad_w = jnp.dot(win_ref[j, 0, 1, h], grad_t_lows[h], preferred_element_type=jnp.float32)
            grad_s = (prob * (grad_w - deltas[h]) * scale).astype(jnp.bfloat16)
            terms_ref[j, 0, 0, h] = jnp.dot(grad_s, qs[h], preferred_element_type=jnp.float32)
            terms_ref[j, 0, 1, h] = jnp.dot(low, grads[h], preferred_element_type=jnp.float32)
            key_t = win_ref[j, 0, 0, h].astype(jnp.float32).T.astype(jnp.bfloat16)
            new.append(dqs[h] + jnp.dot(key_t, grad_s, preferred_element_type=jnp.float32))
        return tuple(new)

    dqs = grad_step(last, tuple(zero for _ in heads))
    dqs = lax.fori_loop(first, last, grad_step, dqs)
    for h in heads:
        dq_ref[0, h * group:(h + 1) * group] = dqs[h].T.astype(jnp.bfloat16).reshape(
            group, span_len, head_dim)

    def clear(j, carry):
        terms_ref[j] = jnp.zeros(terms_ref.shape[1:], terms_ref.dtype)
        return carry

    lax.fori_loop(0, first, clear, 0)


HEAD_PAIR = 2


def attention(skip, span_firsts, q, grad_out, window, query_start, group):
    streams, heads, span_len, head_dim = q.shape
    kv_heads = heads // group
    spans = window.shape[0]
    head_block = pl.BlockSpec((1, group * HEAD_PAIR, span_len, head_dim), lambda s, h, sk, sf: (s, h, 0, 0))
    window_block = pl.BlockSpec((spans, 1, 2, HEAD_PAIR, span_len, head_dim),
                                lambda s, h, sk, sf: (0, s, 0, h, 0, 0))
    return pl.pallas_call(
        attention_kernel,
        out_shape=(
            jax.ShapeDtypeStruct(q.shape, jnp.bfloat16),
            jax.ShapeDtypeStruct(q.shape, jnp.bfloat16),
            jax.ShapeDtypeStruct((spans, streams, 2, kv_heads, span_len, head_dim), jnp.float32),
        ),
        grid_spec=pltpu.PrefetchScalarGridSpec(
            num_scalar_prefetch=2,
            grid=(streams, kv_heads // HEAD_PAIR),
            in_specs=[
                head_block,
                head_block,
                window_block,
                pl.BlockSpec((1, 1, span_len), lambda s, h, sk, sf: (s, 0, 0)),
            ],
            out_specs=[head_block, head_block, window_block],
            scratch_shapes=[pltpu.VMEM((spans, HEAD_PAIR, span_len, group * span_len), jnp.float32),
                            pltpu.VMEM((spans, HEAD_PAIR, 1, group * span_len), jnp.float32)],
        ),
        compiler_params=pltpu.CompilerParams(vmem_limit_bytes=56 * 1024 * 1024),
    )(skip, span_firsts, q, grad_out, window, query_start)


def body(query, keys, values, grad_out, doc_starts):
    shard_count = lax.axis_size("seq")
    device_index = lax.axis_index("seq")
    window = ROUNDS
    span_len = query.shape[2]
    kv_heads = keys.shape[3]
    head_dim = query.shape[4]
    group = query.shape[3] // kv_heads
    q = jnp.transpose(query[:, 0], (0, 2, 1, 3))
    grad_o = jnp.transpose(grad_out[:, 0], (0, 2, 1, 3))
    current = jnp.stack([jnp.transpose(keys[:, 0], (0, 2, 1, 3)),
                         jnp.transpose(values[:, 0], (0, 2, 1, 3))], axis=1)
    flat = current.reshape(2, 2, kv_heads * span_len, head_dim)
    spans = forward_chain(flat, shard_count).reshape((window + 1,) + current.shape)
    span_firsts = jnp.stack([device_index, 2 * shard_count - 1 - device_index]).astype(jnp.int32)
    query_pos = span_firsts[:, None] * span_len + jnp.arange(span_len, dtype=jnp.int32)[None]
    query_start = jnp.max(
        jnp.where(doc_starts[None, None, :] <= query_pos[:, :, None], doc_starts[None, None, :], -1), axis=2)
    span_last = (span_firsts[:, None] - window + jnp.arange(window, dtype=jnp.int32)[None]) * span_len + span_len - 1
    skip = jnp.sum(span_last < query_start[:, :1], axis=1).astype(jnp.int32)
    attended, grad_q, terms = attention(
        skip, span_firsts, q, grad_o, spans, query_start[:, None, :], group)
    term_flat = terms.reshape(window + 1, 2, 2, kv_heads * span_len, head_dim)
    totals = backward_chain(term_flat, shard_count).reshape(current.shape)
    grad_kv = jnp.transpose(totals, (1, 0, 3, 2, 4))[:, :, None]
    return (
        jnp.transpose(attended, (0, 2, 1, 3))[:, None],
        jnp.transpose(grad_q, (0, 2, 1, 3))[:, None],
        grad_kv[0],
        grad_kv[1],
    )


def solution(mesh):
    placed = (
        P("batch", "seq", None, "head", None),
        P("batch", "seq", None, "head", None),
        P("batch", "seq", None, "head", None),
        P("batch", "seq", None, "head", None),
        P("batch"),
    )
    return jax.shard_map(
        body,
        mesh=mesh,
        in_specs=placed,
        out_specs=(
            P("batch", "seq", None, "head", None),
            P("batch", "seq", None, "head", None),
            P("batch", "seq", None, "head", None),
            P("batch", "seq", None, "head", None),
        ),
        check_vma=False,
    )
```

```python
import functools

import jax
import jax.numpy as jnp
from jax import lax
from jax.sharding import PartitionSpec as P

from jax.experimental import pallas as pl
from jax.experimental.pallas import tpu as pltpu

ROUNDS = 16


def greet_neighbours(me, count):
    barrier = pltpu.get_barrier_semaphore()

    @pl.when(me > 0)
    def _():
        pl.semaphore_signal(barrier, 1, device_id={"seq": me - 1})

    @pl.when(me < count - 1)
    def _():
        pl.semaphore_signal(barrier, 1, device_id={"seq": me + 1})

    @pl.when(jnp.logical_and(me > 0, me < count - 1))
    def _():
        pl.semaphore_wait(barrier, 2)

    @pl.when(jnp.logical_or(me == 0, me == count - 1))
    def _():
        pl.semaphore_wait(barrier, 1)


PIECES = 8


def piece_rows(i, total):
    size = total // (PIECES // 2)
    return i // (PIECES // 2), pl.ds((i % (PIECES // 2)) * size, size)


def forward_chain_kernel(count, cur, hist, send_sem, recv_sem, local_sem):
    me = lax.axis_index("seq")
    own = pltpu.make_async_copy(cur, hist.at[ROUNDS], local_sem.at[ROUNDS, 0])
    own.start()
    greet_neighbours(me, count)
    total = cur.shape[2]

    def copies(k, i):
        slot = ROUNDS - k
        kv, rows = piece_rows(i, total)
        src_a = cur.at[0, kv, rows] if k == 1 else hist.at[slot + 1, 0, kv, rows]
        src_b = cur.at[1, kv, rows] if k == 1 else hist.at[slot + 1, 1, kv, rows]
        send_a = pltpu.make_async_remote_copy(
            src_a, hist.at[slot, 0, kv, rows], send_sem.at[slot, 0, i], recv_sem.at[slot, 0, i],
            device_id={"seq": me + 1})
        send_b = pltpu.make_async_remote_copy(
            src_b, hist.at[slot, 1, kv, rows], send_sem.at[slot, 1, i], recv_sem.at[slot, 1, i],
            device_id={"seq": me - 1})
        local_b = pltpu.make_async_copy(src_a, hist.at[slot, 1, kv, rows], local_sem.at[slot, i])
        return send_a, send_b, local_b

    def a_sends(k):
        return jnp.logical_and(me < count - 1, me >= k - 1)

    def receive(k, i):
        send_a, send_b, local_b = copies(k, i)
        pl.when(me >= k)(send_a.wait_recv)
        pl.when(me < count - 1)(send_b.wait_recv)
        pl.when(me == count - 1)(local_b.wait)

    for k in range(1, ROUNDS + 1):
        for i in range(PIECES):
            if k > 1:
                receive(k - 1, i)
            send_a, send_b, local_b = copies(k, i)
            pl.when(a_sends(k))(send_a.start)
            pl.when(me > 0)(send_b.start)
            pl.when(me == count - 1)(local_b.start)

        @pl.when(me < k)
        def _():
            hist[ROUNDS - k, 0] = jnp.zeros(hist.shape[2:], hist.dtype)

    for i in range(PIECES):
        receive(ROUNDS, i)
    for k in range(1, ROUNDS + 1):
        for i in range(PIECES):
            send_a, send_b, _ = copies(k, i)
            pl.when(a_sends(k))(send_a.wait_send)
            pl.when(me > 0)(send_b.wait_send)
    own.wait()


def backward_chain_kernel(count, terms, out, send_buf, recv_buf, send_sem, recv_sem, local_sem):
    me = lax.axis_index("seq")
    greet_neighbours(me, count)
    total = terms.shape[3]

    def copies(t, i):
        slot = t - 1
        kv, rows = piece_rows(i, total)
        send_a = pltpu.make_async_remote_copy(
            send_buf.at[slot, 0, kv, rows], recv_buf.at[slot, 0, kv, rows],
            send_sem.at[slot, 0, i], recv_sem.at[slot, 0, i], device_id={"seq": me - 1})
        send_b = pltpu.make_async_remote_copy(
            send_buf.at[slot, 1, kv, rows], recv_buf.at[slot, 1, kv, rows],
            send_sem.at[slot, 1, i], recv_sem.at[slot, 1, i], device_id={"seq": me + 1})
        local_b = pltpu.make_async_copy(
            send_buf.at[slot, 1, kv, rows], recv_buf.at[slot, 0, kv, rows], local_sem.at[slot, i])
        return send_a, send_b, local_b

    def start(t, i):
        send_a, send_b, local_b = copies(t, i)
        pl.when(me > 0)(send_a.start)
        pl.when(me < count - 1)(send_b.start)
        pl.when(me == count - 1)(local_b.start)

    for i in range(PIECES):
        kv, rows = piece_rows(i, total)
        send_buf[0, :, kv, rows] = terms[0, :, kv, rows].astype(send_buf.dtype)
        start(1, i)
    for t in range(1, ROUNDS + 1):
        slot = t - 1
        for i in range(PIECES):
            kv, rows = piece_rows(i, total)
            send_a, send_b, local_b = copies(t, i)
            pl.when(me < count - 1)(send_a.wait_recv)
            pl.when(me == count - 1)(local_b.wait)
            pl.when(me > 0)(send_b.wait_recv)
            total_a = recv_buf[slot, 0, kv, rows].astype(jnp.float32) + terms[t, 0, kv, rows]
            if t < ROUNDS:
                send_buf[t, 0, kv, rows] = total_a.astype(send_buf.dtype)
            else:
                out[0, kv, rows] = total_a.astype(out.dtype)

            @pl.when(me > 0)
            def _():
                total_b = recv_buf[slot, 1, kv, rows].astype(jnp.float32) + terms[t, 1, kv, rows]
                if t < ROUNDS:
                    send_buf[t, 1, kv, rows] = total_b.astype(send_buf.dtype)
                else:
                    out[1, kv, rows] = total_b.astype(out.dtype)

            @pl.when(me == 0)
            def _():
                total_b = terms[t, 1, kv, rows]
                if t < ROUNDS:
                    send_buf[t, 1, kv, rows] = total_b.astype(send_buf.dtype)
                else:
                    out[1, kv, rows] = total_b.astype(out.dtype)

            if t < ROUNDS:
                start(t + 1, i)
    for t in range(1, ROUNDS + 1):
        for i in range(PIECES):
            send_a, send_b, _ = copies(t, i)
            pl.when(me > 0)(send_a.wait_send)
            pl.when(me < count - 1)(send_b.wait_send)


def forward_chain(current, count):
    shape = current.shape
    return pl.pallas_call(
        functools.partial(forward_chain_kernel, count),
        out_shape=jax.ShapeDtypeStruct((ROUNDS + 1,) + shape, current.dtype),
        in_specs=[pl.BlockSpec(memory_space=pltpu.VMEM)],
        out_specs=pl.BlockSpec(memory_space=pltpu.VMEM),
        scratch_shapes=[
            pltpu.SemaphoreType.DMA((ROUNDS, 2, PIECES)),
            pltpu.SemaphoreType.DMA((ROUNDS, 2, PIECES)),
            pltpu.SemaphoreType.DMA((ROUNDS + 1, PIECES)),
        ],
        compiler_params=pltpu.CompilerParams(
            collective_id=0, has_side_effects=True, vmem_limit_bytes=48 * 1024 * 1024),
    )(current)


def backward_chain(terms, count):
    shape = terms.shape[1:]
    return pl.pallas_call(
        functools.partial(backward_chain_kernel, count),
        out_shape=jax.ShapeDtypeStruct(shape, jnp.bfloat16),
        in_specs=[pl.BlockSpec(memory_space=pltpu.VMEM)],
        out_specs=pl.BlockSpec(memory_space=pltpu.VMEM),
        scratch_shapes=[
            pltpu.VMEM((ROUNDS,) + shape, jnp.bfloat16),
            pltpu.VMEM((ROUNDS,) + shape, jnp.bfloat16),
            pltpu.SemaphoreType.DMA((ROUNDS, 2, PIECES)),
            pltpu.SemaphoreType.DMA((ROUNDS, 2, PIECES)),
            pltpu.SemaphoreType.DMA((ROUNDS, PIECES)),
        ],
        compiler_params=pltpu.CompilerParams(
            collective_id=1, has_side_effects=True, vmem_limit_bytes=60 * 1024 * 1024),
    )(terms)


def attention_kernel(skip_ref, first_ref, q_ref, do_ref, win_ref, qstart_ref,
                     o_ref, dq_ref, terms_ref, cache, tops):
    stream = pl.program_id(0)
    first = skip_ref[stream]
    pair = win_ref.shape[3]
    group = q_ref.shape[1] // pair
    span_len, head_dim = q_ref.shape[2:]
    rows = group * span_len
    last = win_ref.shape[0] - 1
    scale = head_dim ** (-0.5)
    heads = range(pair)
    qs = [q_ref[0, h * group:(h + 1) * group].reshape(rows, head_dim) for h in heads]
    grads = [do_ref[0, h * group:(h + 1) * group].reshape(rows, head_dim) for h in heads]
    q_ts = [q.astype(jnp.float32).T.astype(jnp.bfloat16) for q in qs]
    grad_ts = [g.astype(jnp.float32).T for g in grads]
    grad_t_lows = [g.astype(jnp.bfloat16) for g in grad_ts]
    query_start = qstart_ref[0]
    span = first_ref[stream]
    query_pos = lax.broadcasted_iota(jnp.int32, (1, span_len), 1) + span * span_len
    key_offset = lax.broadcasted_iota(jnp.int32, (span_len, span_len), 0)

    def mask(j):
        key_pos = key_offset + (span - last + j) * span_len
        allowed = jnp.logical_and(key_pos >= query_start, key_pos <= query_pos)
        return jnp.tile(allowed, (1, group))

    def scores(j, h, allowed):
        sc = jnp.dot(win_ref[j, 0, 0, h], q_ts[h], preferred_element_type=jnp.float32) * scale
        return jnp.where(allowed, sc, -jnp.inf)

    allowed = mask(last)
    top_list, total_list = [], []
    for h in heads:
        sc = scores(last, h, allowed)
        top = jnp.max(sc, axis=0, keepdims=True)
        expon = jnp.exp(sc - top)
        cache[last, h] = expon
        tops[last, h] = top
        top_list.append(top)
        total_list.append(jnp.sum(expon, axis=0, keepdims=True))

    def stat_step(j, carry):
        top_c, total_c = carry
        allowed = mask(j)
        new_tops, new_totals = [], []
        for h in heads:
            sc = scores(j, h, allowed)
            new_top = jnp.maximum(top_c[h], jnp.max(sc, axis=0, keepdims=True))
            expon = jnp.exp(sc - new_top)
            cache[j, h] = expon
            tops[j, h] = new_top
            new_tops.append(new_top)
            new_totals.append(total_c[h] * jnp.exp(top_c[h] - new_top)
                              + jnp.sum(expon, axis=0, keepdims=True))
        return tuple(new_tops), tuple(new_totals)

    top_list, total_list = lax.fori_loop(first, last, stat_step, (tuple(top_list), tuple(total_list)))
    inverses = [1.0 / t for t in total_list]

    def out_step(j, accs):
        new = []
        for h in heads:
            prob = cache[j, h] * (jnp.exp(tops[j, h] - top_list[h]) * inverses[h])
            cache[j, h] = prob
            value_t = win_ref[j, 0, 1, h].astype(jnp.float32).T.astype(jnp.bfloat16)
            new.append(accs[h] + jnp.dot(value_t, prob.astype(jnp.bfloat16),
                                         preferred_element_type=jnp.float32))
        return tuple(new)

    zero = jnp.zeros((head_dim, rows), jnp.float32)
    accs = out_step(last, tuple(zero for _ in heads))
    accs = lax.fori_loop(first, last, out_step, accs)
    deltas = []
    for h in heads:
        attended_t = accs[h].astype(jnp.bfloat16)
        o_ref[0, h * group:(h + 1) * group] = attended_t.astype(jnp.float32).T.astype(
            jnp.bfloat16).reshape(group, span_len, head_dim)
        deltas.append(jnp.sum(grad_ts[h] * attended_t.astype(jnp.float32), axis=0, keepdims=True))

    def grad_step(j, dqs):
        new = []
        for h in heads:
            prob = cache[j, h]
            low = prob.astype(jnp.bfloat16)
            grad_w = jnp.dot(win_ref[j, 0, 1, h], grad_t_lows[h], preferred_element_type=jnp.float32)
            grad_s = (prob * (grad_w - deltas[h]) * scale).astype(jnp.bfloat16)
            terms_ref[j, 0, 0, h] = jnp.dot(grad_s, qs[h], preferred_element_type=jnp.float32)
            terms_ref[j, 0, 1, h] = jnp.dot(low, grads[h], preferred_element_type=jnp.float32)
            key_t = win_ref[j, 0, 0, h].astype(jnp.float32).T.astype(jnp.bfloat16)
            new.append(dqs[h] + jnp.dot(key_t, grad_s, preferred_element_type=jnp.float32))
        return tuple(new)

    dqs = grad_step(last, tuple(zero for _ in heads))
    dqs = lax.fori_loop(first, last, grad_step, dqs)
    for h in heads:
        dq_ref[0, h * group:(h + 1) * group] = dqs[h].T.astype(jnp.bfloat16).reshape(
            group, span_len, head_dim)

    def clear(j, carry):
        terms_ref[j] = jnp.zeros(terms_ref.shape[1:], terms_ref.dtype)
        return carry

    lax.fori_loop(0, first, clear, 0)


HEAD_PAIR = 4


def attention(skip, span_firsts, q, grad_out, window, query_start, group):
    streams, heads, span_len, head_dim = q.shape
    kv_heads = heads // group
    spans = window.shape[0]
    head_block = pl.BlockSpec((1, group * HEAD_PAIR, span_len, head_dim), lambda s, h, sk, sf: (s, h, 0, 0))
    window_block = pl.BlockSpec((spans, 1, 2, HEAD_PAIR, span_len, head_dim),
                                lambda s, h, sk, sf: (0, s, 0, h, 0, 0))
    return pl.pallas_call(
        attention_kernel,
        out_shape=(
            jax.ShapeDtypeStruct(q.shape, jnp.bfloat16),
            jax.ShapeDtypeStruct(q.shape, jnp.bfloat16),
            jax.ShapeDtypeStruct((spans, streams, 2, kv_heads, span_len, head_dim), jnp.float32),
        ),
        grid_spec=pltpu.PrefetchScalarGridSpec(
            num_scalar_prefetch=2,
            grid=(streams, kv_heads // HEAD_PAIR),
            in_specs=[
                head_block,
                head_block,
                window_block,
                pl.BlockSpec((1, 1, span_len), lambda s, h, sk, sf: (s, 0, 0)),
            ],
            out_specs=[head_block, head_block, window_block],
            scratch_shapes=[pltpu.VMEM((spans, HEAD_PAIR, span_len, group * span_len), jnp.float32),
                            pltpu.VMEM((spans, HEAD_PAIR, 1, group * span_len), jnp.float32)],
        ),
        compiler_params=pltpu.CompilerParams(vmem_limit_bytes=63 * 1024 * 1024),
    )(skip, span_firsts, q, grad_out, window, query_start)


def body(query, keys, values, grad_out, doc_starts):
    shard_count = lax.axis_size("seq")
    device_index = lax.axis_index("seq")
    window = ROUNDS
    span_len = query.shape[2]
    kv_heads = keys.shape[3]
    head_dim = query.shape[4]
    group = query.shape[3] // kv_heads
    q = jnp.transpose(query[:, 0], (0, 2, 1, 3))
    grad_o = jnp.transpose(grad_out[:, 0], (0, 2, 1, 3))
    current = jnp.stack([jnp.transpose(keys[:, 0], (0, 2, 1, 3)),
                         jnp.transpose(values[:, 0], (0, 2, 1, 3))], axis=1)
    flat = current.reshape(2, 2, kv_heads * span_len, head_dim)
    spans = forward_chain(flat, shard_count).reshape((window + 1,) + current.shape)
    span_firsts = jnp.stack([device_index, 2 * shard_count - 1 - device_index]).astype(jnp.int32)
    query_pos = span_firsts[:, None] * span_len + jnp.arange(span_len, dtype=jnp.int32)[None]
    query_start = jnp.max(
        jnp.where(doc_starts[None, None, :] <= query_pos[:, :, None], doc_starts[None, None, :], -1), axis=2)
    span_last = (span_firsts[:, None] - window + jnp.arange(window, dtype=jnp.int32)[None]) * span_len + span_len - 1
    skip = jnp.sum(span_last < query_start[:, :1], axis=1).astype(jnp.int32)
    attended, grad_q, terms = attention(
        skip, span_firsts, q, grad_o, spans, query_start[:, None, :], group)
    term_flat = terms.reshape(window + 1, 2, 2, kv_heads * span_len, head_dim)
    totals = backward_chain(term_flat, shard_count).reshape(current.shape)
    grad_kv = jnp.transpose(totals, (1, 0, 3, 2, 4))[:, :, None]
    return (
        jnp.transpose(attended, (0, 2, 1, 3))[:, None],
        jnp.transpose(grad_q, (0, 2, 1, 3))[:, None],
        grad_kv[0],
        grad_kv[1],
    )


def solution(mesh):
    placed = (
        P("batch", "seq", None, "head", None),
        P("batch", "seq", None, "head", None),
        P("batch", "seq", None, "head", None),
        P("batch", "seq", None, "head", None),
        P("batch"),
    )
    return jax.shard_map(
        body,
        mesh=mesh,
        in_specs=placed,
        out_specs=(
            P("batch", "seq", None, "head", None),
            P("batch", "seq", None, "head", None),
            P("batch", "seq", None, "head", None),
            P("batch", "seq", None, "head", None),
        ),
        check_vma=False,
    )
```

```python
import functools

import jax
import jax.numpy as jnp
from jax import lax
from jax.sharding import PartitionSpec as P

from jax.experimental import pallas as pl
from jax.experimental.pallas import tpu as pltpu

ROUNDS = 16


def greet_neighbours(me, count):
    barrier = pltpu.get_barrier_semaphore()

    @pl.when(me > 0)
    def _():
        pl.semaphore_signal(barrier, 1, device_id={"seq": me - 1})

    @pl.when(me < count - 1)
    def _():
        pl.semaphore_signal(barrier, 1, device_id={"seq": me + 1})

    @pl.when(jnp.logical_and(me > 0, me < count - 1))
    def _():
        pl.semaphore_wait(barrier, 2)

    @pl.when(jnp.logical_or(me == 0, me == count - 1))
    def _():
        pl.semaphore_wait(barrier, 1)


PIECES = 8


def piece_rows(i, total):
    size = total // (PIECES // 2)
    return i // (PIECES // 2), pl.ds((i % (PIECES // 2)) * size, size)


def forward_chain_kernel(count, cur, hist, send_sem, recv_sem, local_sem):
    me = lax.axis_index("seq")
    own = pltpu.make_async_copy(cur, hist.at[ROUNDS], local_sem.at[ROUNDS, 0])
    own.start()
    greet_neighbours(me, count)
    total = cur.shape[2]

    def copies(k, i):
        slot = ROUNDS - k
        kv, rows = piece_rows(i, total)
        src_a = cur.at[0, kv, rows] if k == 1 else hist.at[slot + 1, 0, kv, rows]
        src_b = cur.at[1, kv, rows] if k == 1 else hist.at[slot + 1, 1, kv, rows]
        send_a = pltpu.make_async_remote_copy(
            src_a, hist.at[slot, 0, kv, rows], send_sem.at[slot, 0, i], recv_sem.at[slot, 0, i],
            device_id={"seq": me + 1})
        send_b = pltpu.make_async_remote_copy(
            src_b, hist.at[slot, 1, kv, rows], send_sem.at[slot, 1, i], recv_sem.at[slot, 1, i],
            device_id={"seq": me - 1})
        local_b = pltpu.make_async_copy(src_a, hist.at[slot, 1, kv, rows], local_sem.at[slot, i])
        return send_a, send_b, local_b

    def a_sends(k):
        return jnp.logical_and(me < count - 1, me >= k - 1)

    def receive(k, i):
        send_a, send_b, local_b = copies(k, i)
        pl.when(me >= k)(send_a.wait_recv)
        pl.when(me < count - 1)(send_b.wait_recv)
        pl.when(me == count - 1)(local_b.wait)

    for k in range(1, ROUNDS + 1):
        for i in range(PIECES):
            if k > 1:
                receive(k - 1, i)
            send_a, send_b, local_b = copies(k, i)
            pl.when(a_sends(k))(send_a.start)
            pl.when(me > 0)(send_b.start)
            pl.when(me == count - 1)(local_b.start)

        @pl.when(me < k)
        def _():
            hist[ROUNDS - k, 0] = jnp.zeros(hist.shape[2:], hist.dtype)

    for i in range(PIECES):
        receive(ROUNDS, i)
    for k in range(1, ROUNDS + 1):
        for i in range(PIECES):
            send_a, send_b, _ = copies(k, i)
            pl.when(a_sends(k))(send_a.wait_send)
            pl.when(me > 0)(send_b.wait_send)
    own.wait()


def backward_chain_kernel(count, terms, out, send_buf, recv_buf, staged, send_sem, recv_sem, local_sem,
                          fetch_sem):
    me = lax.axis_index("seq")

    def fetch(t):
        return pltpu.make_async_copy(terms.at[t], staged.at[t % 2], fetch_sem.at[t % 2])

    fetch(0).start()
    greet_neighbours(me, count)
    total = terms.shape[3]

    def copies(t, i):
        slot = t - 1
        kv, rows = piece_rows(i, total)
        send_a = pltpu.make_async_remote_copy(
            send_buf.at[slot, 0, kv, rows], recv_buf.at[slot, 0, kv, rows],
            send_sem.at[slot, 0, i], recv_sem.at[slot, 0, i], device_id={"seq": me - 1})
        send_b = pltpu.make_async_remote_copy(
            send_buf.at[slot, 1, kv, rows], recv_buf.at[slot, 1, kv, rows],
            send_sem.at[slot, 1, i], recv_sem.at[slot, 1, i], device_id={"seq": me + 1})
        local_b = pltpu.make_async_copy(
            send_buf.at[slot, 1, kv, rows], recv_buf.at[slot, 0, kv, rows], local_sem.at[slot, i])
        return send_a, send_b, local_b

    def start(t, i):
        send_a, send_b, local_b = copies(t, i)
        pl.when(me > 0)(send_a.start)
        pl.when(me < count - 1)(send_b.start)
        pl.when(me == count - 1)(local_b.start)

    fetch(0).wait()
    fetch(1).start()
    for i in range(PIECES):
        kv, rows = piece_rows(i, total)
        send_buf[0, :, kv, rows] = staged[0, :, kv, rows].astype(send_buf.dtype)
        start(1, i)
    for t in range(1, ROUNDS + 1):
        slot = t - 1
        fetch(t).wait()
        if t < ROUNDS:
            fetch(t + 1).start()
        for i in range(PIECES):
            kv, rows = piece_rows(i, total)
            send_a, send_b, local_b = copies(t, i)
            pl.when(me < count - 1)(send_a.wait_recv)
            pl.when(me == count - 1)(local_b.wait)
            pl.when(me > 0)(send_b.wait_recv)
            total_a = recv_buf[slot, 0, kv, rows].astype(jnp.float32) + staged[t % 2, 0, kv, rows]
            if t < ROUNDS:
                send_buf[t, 0, kv, rows] = total_a.astype(send_buf.dtype)
            else:
                out[0, kv, rows] = total_a.astype(out.dtype)

            @pl.when(me > 0)
            def _():
                total_b = recv_buf[slot, 1, kv, rows].astype(jnp.float32) + staged[t % 2, 1, kv, rows]
                if t < ROUNDS:
                    send_buf[t, 1, kv, rows] = total_b.astype(send_buf.dtype)
                else:
                    out[1, kv, rows] = total_b.astype(out.dtype)

            @pl.when(me == 0)
            def _():
                total_b = staged[t % 2, 1, kv, rows]
                if t < ROUNDS:
                    send_buf[t, 1, kv, rows] = total_b.astype(send_buf.dtype)
                else:
                    out[1, kv, rows] = total_b.astype(out.dtype)

            if t < ROUNDS:
                start(t + 1, i)
    for t in range(1, ROUNDS + 1):
        for i in range(PIECES):
            send_a, send_b, _ = copies(t, i)
            pl.when(me > 0)(send_a.wait_send)
            pl.when(me < count - 1)(send_b.wait_send)


def forward_chain(current, count):
    shape = current.shape
    return pl.pallas_call(
        functools.partial(forward_chain_kernel, count),
        out_shape=jax.ShapeDtypeStruct((ROUNDS + 1,) + shape, current.dtype),
        in_specs=[pl.BlockSpec(memory_space=pltpu.VMEM)],
        out_specs=pl.BlockSpec(memory_space=pltpu.VMEM),
        scratch_shapes=[
            pltpu.SemaphoreType.DMA((ROUNDS, 2, PIECES)),
            pltpu.SemaphoreType.DMA((ROUNDS, 2, PIECES)),
            pltpu.SemaphoreType.DMA((ROUNDS + 1, PIECES)),
        ],
        compiler_params=pltpu.CompilerParams(
            collective_id=0, has_side_effects=True, vmem_limit_bytes=48 * 1024 * 1024),
    )(current)


def backward_chain(terms, count):
    shape = terms.shape[1:]
    return pl.pallas_call(
        functools.partial(backward_chain_kernel, count),
        out_shape=jax.ShapeDtypeStruct(shape, jnp.bfloat16),
        in_specs=[pl.BlockSpec(memory_space=pl.ANY)],
        out_specs=pl.BlockSpec(memory_space=pltpu.VMEM),
        scratch_shapes=[
            pltpu.VMEM((ROUNDS,) + shape, jnp.bfloat16),
            pltpu.VMEM((ROUNDS,) + shape, jnp.bfloat16),
            pltpu.VMEM((2,) + shape, jnp.float32),
            pltpu.SemaphoreType.DMA((ROUNDS, 2, PIECES)),
            pltpu.SemaphoreType.DMA((ROUNDS, 2, PIECES)),
            pltpu.SemaphoreType.DMA((ROUNDS, PIECES)),
            pltpu.SemaphoreType.DMA((2,)),
        ],
        compiler_params=pltpu.CompilerParams(
            collective_id=1, has_side_effects=True, vmem_limit_bytes=60 * 1024 * 1024),
    )(terms)


def attention_kernel(skip_ref, first_ref, q_ref, do_ref, win_ref, qstart_ref,
                     o_ref, dq_ref, terms_ref, cache, tops):
    stream = pl.program_id(0)
    first = skip_ref[stream]
    pair = win_ref.shape[3]
    group = q_ref.shape[1] // pair
    span_len, head_dim = q_ref.shape[2:]
    rows = group * span_len
    last = win_ref.shape[0] - 1
    scale = head_dim ** (-0.5)
    heads = range(pair)
    qs = [q_ref[0, h * group:(h + 1) * group].reshape(rows, head_dim) for h in heads]
    grads = [do_ref[0, h * group:(h + 1) * group].reshape(rows, head_dim) for h in heads]
    q_ts = [q.astype(jnp.float32).T.astype(jnp.bfloat16) for q in qs]
    grad_ts = [g.astype(jnp.float32).T for g in grads]
    grad_t_lows = [g.astype(jnp.bfloat16) for g in grad_ts]
    query_start = qstart_ref[0]
    span = first_ref[stream]
    query_pos = lax.broadcasted_iota(jnp.int32, (1, span_len), 1) + span * span_len
    key_offset = lax.broadcasted_iota(jnp.int32, (span_len, span_len), 0)

    def mask(j):
        key_pos = key_offset + (span - last + j) * span_len
        allowed = jnp.logical_and(key_pos >= query_start, key_pos <= query_pos)
        return jnp.tile(allowed, (1, group))

    def scores(j, h, allowed):
        sc = jnp.dot(win_ref[j, 0, 0, h], q_ts[h], preferred_element_type=jnp.float32) * scale
        return jnp.where(allowed, sc, -jnp.inf)

    allowed = mask(last)
    top_list, total_list = [], []
    for h in heads:
        sc = scores(last, h, allowed)
        top = jnp.max(sc, axis=0, keepdims=True)
        expon = jnp.exp(sc - top)
        cache[last, h] = expon
        tops[last, h] = top
        top_list.append(top)
        total_list.append(jnp.sum(expon, axis=0, keepdims=True))

    def stat_step(j, carry):
        top_c, total_c = carry
        allowed = mask(j)
        new_tops, new_totals = [], []
        for h in heads:
            sc = scores(j, h, allowed)
            new_top = jnp.maximum(top_c[h], jnp.max(sc, axis=0, keepdims=True))
            expon = jnp.exp(sc - new_top)
            cache[j, h] = expon
            tops[j, h] = new_top
            new_tops.append(new_top)
            new_totals.append(total_c[h] * jnp.exp(top_c[h] - new_top)
                              + jnp.sum(expon, axis=0, keepdims=True))
        return tuple(new_tops), tuple(new_totals)

    top_list, total_list = lax.fori_loop(first, last, stat_step, (tuple(top_list), tuple(total_list)))
    inverses = [1.0 / t for t in total_list]

    def out_step(j, accs):
        new = []
        for h in heads:
            prob = cache[j, h] * (jnp.exp(tops[j, h] - top_list[h]) * inverses[h])
            cache[j, h] = prob
            value_t = win_ref[j, 0, 1, h].astype(jnp.float32).T.astype(jnp.bfloat16)
            new.append(accs[h] + jnp.dot(value_t, prob.astype(jnp.bfloat16),
                                         preferred_element_type=jnp.float32))
        return tuple(new)

    zero = jnp.zeros((head_dim, rows), jnp.float32)
    accs = out_step(last, tuple(zero for _ in heads))
    accs = lax.fori_loop(first, last, out_step, accs)
    deltas = []
    for h in heads:
        attended_t = accs[h].astype(jnp.bfloat16)
        o_ref[0, h * group:(h + 1) * group] = attended_t.astype(jnp.float32).T.astype(
            jnp.bfloat16).reshape(group, span_len, head_dim)
        deltas.append(jnp.sum(grad_ts[h] * attended_t.astype(jnp.float32), axis=0, keepdims=True))

    def grad_step(j, dqs):
        new = []
        for h in heads:
            prob = cache[j, h]
            low = prob.astype(jnp.bfloat16)
            grad_w = jnp.dot(win_ref[j, 0, 1, h], grad_t_lows[h], preferred_element_type=jnp.float32)
            grad_s = (prob * (grad_w - deltas[h]) * scale).astype(jnp.bfloat16)
            terms_ref[j, 0, 0, h] = jnp.dot(grad_s, qs[h], preferred_element_type=jnp.float32)
            terms_ref[j, 0, 1, h] = jnp.dot(low, grads[h], preferred_element_type=jnp.float32)
            key_t = win_ref[j, 0, 0, h].astype(jnp.float32).T.astype(jnp.bfloat16)
            new.append(dqs[h] + jnp.dot(key_t, grad_s, preferred_element_type=jnp.float32))
        return tuple(new)

    dqs = grad_step(last, tuple(zero for _ in heads))
    dqs = lax.fori_loop(first, last, grad_step, dqs)
    for h in heads:
        dq_ref[0, h * group:(h + 1) * group] = dqs[h].T.astype(jnp.bfloat16).reshape(
            group, span_len, head_dim)

    def clear(j, carry):
        terms_ref[j] = jnp.zeros(terms_ref.shape[1:], terms_ref.dtype)
        return carry

    lax.fori_loop(0, first, clear, 0)


HEAD_PAIR = 4


def attention(skip, span_firsts, q, grad_out, window, query_start, group):
    streams, heads, span_len, head_dim = q.shape
    kv_heads = heads // group
    spans = window.shape[0]
    head_block = pl.BlockSpec((1, group * HEAD_PAIR, span_len, head_dim), lambda s, h, sk, sf: (s, h, 0, 0))
    window_block = pl.BlockSpec((spans, 1, 2, HEAD_PAIR, span_len, head_dim),
                                lambda s, h, sk, sf: (0, s, 0, h, 0, 0))
    return pl.pallas_call(
        attention_kernel,
        out_shape=(
            jax.ShapeDtypeStruct(q.shape, jnp.bfloat16),
            jax.ShapeDtypeStruct(q.shape, jnp.bfloat16),
            jax.ShapeDtypeStruct((spans, streams, 2, kv_heads, span_len, head_dim), jnp.float32),
        ),
        grid_spec=pltpu.PrefetchScalarGridSpec(
            num_scalar_prefetch=2,
            grid=(streams, kv_heads // HEAD_PAIR),
            in_specs=[
                head_block,
                head_block,
                window_block,
                pl.BlockSpec((1, 1, span_len), lambda s, h, sk, sf: (s, 0, 0)),
            ],
            out_specs=[head_block, head_block, window_block],
            scratch_shapes=[pltpu.VMEM((spans, HEAD_PAIR, span_len, group * span_len), jnp.float32),
                            pltpu.VMEM((spans, HEAD_PAIR, 1, group * span_len), jnp.float32)],
        ),
        compiler_params=pltpu.CompilerParams(vmem_limit_bytes=63 * 1024 * 1024),
    )(skip, span_firsts, q, grad_out, window, query_start)


def body(query, keys, values, grad_out, doc_starts):
    shard_count = lax.axis_size("seq")
    device_index = lax.axis_index("seq")
    window = ROUNDS
    span_len = query.shape[2]
    kv_heads = keys.shape[3]
    head_dim = query.shape[4]
    group = query.shape[3] // kv_heads
    q = jnp.transpose(query[:, 0], (0, 2, 1, 3))
    grad_o = jnp.transpose(grad_out[:, 0], (0, 2, 1, 3))
    current = jnp.stack([jnp.transpose(keys[:, 0], (0, 2, 1, 3)),
                         jnp.transpose(values[:, 0], (0, 2, 1, 3))], axis=1)
    flat = current.reshape(2, 2, kv_heads * span_len, head_dim)
    spans = forward_chain(flat, shard_count).reshape((window + 1,) + current.shape)
    span_firsts = jnp.stack([device_index, 2 * shard_count - 1 - device_index]).astype(jnp.int32)
    query_pos = span_firsts[:, None] * span_len + jnp.arange(span_len, dtype=jnp.int32)[None]
    query_start = jnp.max(
        jnp.where(doc_starts[None, None, :] <= query_pos[:, :, None], doc_starts[None, None, :], -1), axis=2)
    span_last = (span_firsts[:, None] - window + jnp.arange(window, dtype=jnp.int32)[None]) * span_len + span_len - 1
    skip = jnp.sum(span_last < query_start[:, :1], axis=1).astype(jnp.int32)
    attended, grad_q, terms = attention(
        skip, span_firsts, q, grad_o, spans, query_start[:, None, :], group)
    term_flat = terms.reshape(window + 1, 2, 2, kv_heads * span_len, head_dim)
    totals = backward_chain(term_flat, shard_count).reshape(current.shape)
    grad_kv = jnp.transpose(totals, (1, 0, 3, 2, 4))[:, :, None]
    return (
        jnp.transpose(attended, (0, 2, 1, 3))[:, None],
        jnp.transpose(grad_q, (0, 2, 1, 3))[:, None],
        grad_kv[0],
        grad_kv[1],
    )


def solution(mesh):
    placed = (
        P("batch", "seq", None, "head", None),
        P("batch", "seq", None, "head", None),
        P("batch", "seq", None, "head", None),
        P("batch", "seq", None, "head", None),
        P("batch"),
    )
    return jax.shard_map(
        body,
        mesh=mesh,
        in_specs=placed,
        out_specs=(
            P("batch", "seq", None, "head", None),
            P("batch", "seq", None, "head", None),
            P("batch", "seq", None, "head", None),
            P("batch", "seq", None, "head", None),
        ),
        check_vma=False,
    )
```

```python
import functools

import jax
import jax.numpy as jnp
from jax import lax
from jax.sharding import PartitionSpec as P

from jax.experimental import pallas as pl
from jax.experimental.pallas import tpu as pltpu

ROUNDS = 16


def greet_neighbours(me, count):
    barrier = pltpu.get_barrier_semaphore()

    @pl.when(me > 0)
    def _():
        pl.semaphore_signal(barrier, 1, device_id={"seq": me - 1})

    @pl.when(me < count - 1)
    def _():
        pl.semaphore_signal(barrier, 1, device_id={"seq": me + 1})

    @pl.when(jnp.logical_and(me > 0, me < count - 1))
    def _():
        pl.semaphore_wait(barrier, 2)

    @pl.when(jnp.logical_or(me == 0, me == count - 1))
    def _():
        pl.semaphore_wait(barrier, 1)


PIECES = 8


def piece_rows(i, total):
    size = total // (PIECES // 2)
    return i // (PIECES // 2), pl.ds((i % (PIECES // 2)) * size, size)


def forward_chain_kernel(count, cur, hist, send_sem, recv_sem, local_sem):
    me = lax.axis_index("seq")
    own = pltpu.make_async_copy(cur, hist.at[ROUNDS], local_sem.at[ROUNDS, 0])
    own.start()
    greet_neighbours(me, count)
    total = cur.shape[2]

    def copies(k, i):
        slot = ROUNDS - k
        kv, rows = piece_rows(i, total)
        src_a = cur.at[0, kv, rows] if k == 1 else hist.at[slot + 1, 0, kv, rows]
        src_b = cur.at[1, kv, rows] if k == 1 else hist.at[slot + 1, 1, kv, rows]
        send_a = pltpu.make_async_remote_copy(
            src_a, hist.at[slot, 0, kv, rows], send_sem.at[slot, 0, i], recv_sem.at[slot, 0, i],
            device_id={"seq": me + 1})
        send_b = pltpu.make_async_remote_copy(
            src_b, hist.at[slot, 1, kv, rows], send_sem.at[slot, 1, i], recv_sem.at[slot, 1, i],
            device_id={"seq": me - 1})
        local_b = pltpu.make_async_copy(src_a, hist.at[slot, 1, kv, rows], local_sem.at[slot, i])
        return send_a, send_b, local_b

    def a_sends(k):
        return jnp.logical_and(me < count - 1, me >= k - 1)

    def receive(k, i):
        send_a, send_b, local_b = copies(k, i)
        pl.when(me >= k)(send_a.wait_recv)
        pl.when(me < count - 1)(send_b.wait_recv)
        pl.when(me == count - 1)(local_b.wait)

    for k in range(1, ROUNDS + 1):
        for i in range(PIECES):
            if k > 1:
                receive(k - 1, i)
            send_a, send_b, local_b = copies(k, i)
            pl.when(a_sends(k))(send_a.start)
            pl.when(me > 0)(send_b.start)
            pl.when(me == count - 1)(local_b.start)

        @pl.when(me < k)
        def _():
            hist[ROUNDS - k, 0] = jnp.zeros(hist.shape[2:], hist.dtype)

    for i in range(PIECES):
        receive(ROUNDS, i)
    for k in range(1, ROUNDS + 1):
        for i in range(PIECES):
            send_a, send_b, _ = copies(k, i)
            pl.when(a_sends(k))(send_a.wait_send)
            pl.when(me > 0)(send_b.wait_send)
    own.wait()


def backward_chain_kernel(count, terms, out, send_buf, recv_buf, staged, send_sem, recv_sem, local_sem,
                          fetch_sem):
    me = lax.axis_index("seq")

    def fetch(t):
        return pltpu.make_async_copy(terms.at[t], staged.at[t % 2], fetch_sem.at[t % 2])

    fetch(0).start()
    greet_neighbours(me, count)
    total = terms.shape[3]

    def copies(t, i):
        slot = t - 1
        kv, rows = piece_rows(i, total)
        send_a = pltpu.make_async_remote_copy(
            send_buf.at[slot, 0, kv, rows], recv_buf.at[slot, 0, kv, rows],
            send_sem.at[slot, 0, i], recv_sem.at[slot, 0, i], device_id={"seq": me - 1})
        send_b = pltpu.make_async_remote_copy(
            send_buf.at[slot, 1, kv, rows], recv_buf.at[slot, 1, kv, rows],
            send_sem.at[slot, 1, i], recv_sem.at[slot, 1, i], device_id={"seq": me + 1})
        local_b = pltpu.make_async_copy(
            send_buf.at[slot, 1, kv, rows], recv_buf.at[slot, 0, kv, rows], local_sem.at[slot, i])
        return send_a, send_b, local_b

    def start(t, i):
        send_a, send_b, local_b = copies(t, i)
        pl.when(me > 0)(send_a.start)
        pl.when(me < count - 1)(send_b.start)
        pl.when(me == count - 1)(local_b.start)

    fetch(0).wait()
    fetch(1).start()
    for i in range(PIECES):
        kv, rows = piece_rows(i, total)
        send_buf[0, :, kv, rows] = staged[0, :, kv, rows].astype(send_buf.dtype)
        start(1, i)
    for t in range(1, ROUNDS + 1):
        slot = t - 1
        fetch(t).wait()
        if t < ROUNDS:
            fetch(t + 1).start()
        for i in range(PIECES):
            kv, rows = piece_rows(i, total)
            send_a, send_b, local_b = copies(t, i)
            pl.when(me < count - 1)(send_a.wait_recv)
            pl.when(me == count - 1)(local_b.wait)
            pl.when(me > 0)(send_b.wait_recv)
            total_a = recv_buf[slot, 0, kv, rows].astype(jnp.float32) + staged[t % 2, 0, kv, rows]
            if t < ROUNDS:
                send_buf[t, 0, kv, rows] = total_a.astype(send_buf.dtype)
            else:
                out[0, kv, rows] = total_a.astype(out.dtype)

            @pl.when(me > 0)
            def _():
                total_b = recv_buf[slot, 1, kv, rows].astype(jnp.float32) + staged[t % 2, 1, kv, rows]
                if t < ROUNDS:
                    send_buf[t, 1, kv, rows] = total_b.astype(send_buf.dtype)
                else:
                    out[1, kv, rows] = total_b.astype(out.dtype)

            @pl.when(me == 0)
            def _():
                total_b = staged[t % 2, 1, kv, rows]
                if t < ROUNDS:
                    send_buf[t, 1, kv, rows] = total_b.astype(send_buf.dtype)
                else:
                    out[1, kv, rows] = total_b.astype(out.dtype)

            if t < ROUNDS:
                start(t + 1, i)
    for t in range(1, ROUNDS + 1):
        for i in range(PIECES):
            send_a, send_b, _ = copies(t, i)
            pl.when(me > 0)(send_a.wait_send)
            pl.when(me < count - 1)(send_b.wait_send)


def forward_chain(current, count):
    shape = current.shape
    return pl.pallas_call(
        functools.partial(forward_chain_kernel, count),
        out_shape=jax.ShapeDtypeStruct((ROUNDS + 1,) + shape, current.dtype),
        in_specs=[pl.BlockSpec(memory_space=pltpu.VMEM)],
        out_specs=pl.BlockSpec(memory_space=pltpu.VMEM),
        scratch_shapes=[
            pltpu.SemaphoreType.DMA((ROUNDS, 2, PIECES)),
            pltpu.SemaphoreType.DMA((ROUNDS, 2, PIECES)),
            pltpu.SemaphoreType.DMA((ROUNDS + 1, PIECES)),
        ],
        compiler_params=pltpu.CompilerParams(
            collective_id=0, has_side_effects=True, vmem_limit_bytes=48 * 1024 * 1024),
    )(current)


def backward_chain(terms, count):
    shape = terms.shape[1:]
    return pl.pallas_call(
        functools.partial(backward_chain_kernel, count),
        out_shape=jax.ShapeDtypeStruct(shape, jnp.bfloat16),
        in_specs=[pl.BlockSpec(memory_space=pl.ANY)],
        out_specs=pl.BlockSpec(memory_space=pltpu.VMEM),
        scratch_shapes=[
            pltpu.VMEM((ROUNDS,) + shape, jnp.bfloat16),
            pltpu.VMEM((ROUNDS,) + shape, jnp.bfloat16),
            pltpu.VMEM((2,) + shape, jnp.float32),
            pltpu.SemaphoreType.DMA((ROUNDS, 2, PIECES)),
            pltpu.SemaphoreType.DMA((ROUNDS, 2, PIECES)),
            pltpu.SemaphoreType.DMA((ROUNDS, PIECES)),
            pltpu.SemaphoreType.DMA((2,)),
        ],
        compiler_params=pltpu.CompilerParams(
            collective_id=1, has_side_effects=True, vmem_limit_bytes=60 * 1024 * 1024),
    )(terms)


def attention_kernel(skip_ref, first_ref, q_ref, do_ref, win_ref, qstart_ref,
                     o_ref, dq_ref, terms_ref, cache, tops):
    stream = pl.program_id(0)
    first = skip_ref[stream]
    pair = win_ref.shape[3]
    group = q_ref.shape[1] // pair
    span_len, head_dim = q_ref.shape[2:]
    rows = group * span_len
    last = win_ref.shape[0] - 1
    scale = head_dim ** (-0.5)
    heads = range(pair)
    def lanes(ref, h):
        block = ref[0, h * group:(h + 1) * group]
        return jnp.concatenate([block[g] for g in range(group)], axis=1)

    q_ts = [lanes(q_ref, h) for h in heads]
    grad_t_lows = [lanes(do_ref, h) for h in heads]
    grad_ts = [g.astype(jnp.float32) for g in grad_t_lows]
    contract_last = (((1,), (1,)), ((), ()))
    query_start = qstart_ref[0]
    span = first_ref[stream]
    query_pos = lax.broadcasted_iota(jnp.int32, (1, span_len), 1) + span * span_len
    key_offset = lax.broadcasted_iota(jnp.int32, (span_len, span_len), 0)

    def mask(j):
        key_pos = key_offset + (span - last + j) * span_len
        allowed = jnp.logical_and(key_pos >= query_start, key_pos <= query_pos)
        return jnp.tile(allowed, (1, group))

    def scores(j, h, allowed):
        sc = jnp.dot(win_ref[j, 0, 0, h], q_ts[h], preferred_element_type=jnp.float32) * scale
        return jnp.where(allowed, sc, -jnp.inf)

    allowed = mask(last)
    top_list, total_list = [], []
    for h in heads:
        sc = scores(last, h, allowed)
        top = jnp.max(sc, axis=0, keepdims=True)
        expon = jnp.exp(sc - top)
        cache[last, h] = expon
        tops[last, h] = top
        top_list.append(top)
        total_list.append(jnp.sum(expon, axis=0, keepdims=True))

    def stat_step(j, carry):
        top_c, total_c = carry
        allowed = mask(j)
        new_tops, new_totals = [], []
        for h in heads:
            sc = scores(j, h, allowed)
            new_top = jnp.maximum(top_c[h], jnp.max(sc, axis=0, keepdims=True))
            expon = jnp.exp(sc - new_top)
            cache[j, h] = expon
            tops[j, h] = new_top
            new_tops.append(new_top)
            new_totals.append(total_c[h] * jnp.exp(top_c[h] - new_top)
                              + jnp.sum(expon, axis=0, keepdims=True))
        return tuple(new_tops), tuple(new_totals)

    top_list, total_list = lax.fori_loop(first, last, stat_step, (tuple(top_list), tuple(total_list)))
    inverses = [1.0 / t for t in total_list]

    def out_step(j, accs):
        new = []
        for h in heads:
            prob = cache[j, h] * (jnp.exp(tops[j, h] - top_list[h]) * inverses[h])
            cache[j, h] = prob
            value_t = win_ref[j, 0, 1, h].astype(jnp.float32).T.astype(jnp.bfloat16)
            new.append(accs[h] + jnp.dot(value_t, prob.astype(jnp.bfloat16),
                                         preferred_element_type=jnp.float32))
        return tuple(new)

    zero = jnp.zeros((head_dim, rows), jnp.float32)
    accs = out_step(last, tuple(zero for _ in heads))
    accs = lax.fori_loop(first, last, out_step, accs)
    deltas = []
    for h in heads:
        attended_t = accs[h].astype(jnp.bfloat16)
        for g in range(group):
            o_ref[0, h * group + g] = attended_t[:, g * span_len:(g + 1) * span_len]
        deltas.append(jnp.sum(grad_ts[h] * attended_t.astype(jnp.float32), axis=0, keepdims=True))

    def grad_step(j, dqs):
        new = []
        for h in heads:
            prob = cache[j, h]
            low = prob.astype(jnp.bfloat16)
            grad_w = jnp.dot(win_ref[j, 0, 1, h], grad_t_lows[h], preferred_element_type=jnp.float32)
            grad_s = (prob * (grad_w - deltas[h]) * scale).astype(jnp.bfloat16)
            terms_ref[j, 0, 0, h] = lax.dot_general(q_ts[h], grad_s, contract_last,
                                                    preferred_element_type=jnp.float32)
            terms_ref[j, 0, 1, h] = lax.dot_general(grad_t_lows[h], low, contract_last,
                                                    preferred_element_type=jnp.float32)
            key_t = win_ref[j, 0, 0, h].astype(jnp.float32).T.astype(jnp.bfloat16)
            new.append(dqs[h] + jnp.dot(key_t, grad_s, preferred_element_type=jnp.float32))
        return tuple(new)

    dqs = grad_step(last, tuple(zero for _ in heads))
    dqs = lax.fori_loop(first, last, grad_step, dqs)
    for h in heads:
        dq_low = dqs[h].astype(jnp.bfloat16)
        for g in range(group):
            dq_ref[0, h * group + g] = dq_low[:, g * span_len:(g + 1) * span_len]

    def clear(j, carry):
        terms_ref[j] = jnp.zeros(terms_ref.shape[1:], terms_ref.dtype)
        return carry

    lax.fori_loop(0, first, clear, 0)


HEAD_PAIR = 4


def attention(skip, span_firsts, q, grad_out, window, query_start, group):
    streams, heads, span_len, head_dim = q.shape
    kv_heads = heads // group
    spans = window.shape[0]
    head_block = pl.BlockSpec((1, group * HEAD_PAIR, span_len, head_dim), lambda s, h, sk, sf: (s, h, 0, 0))
    window_block = pl.BlockSpec((spans, 1, 2, HEAD_PAIR, span_len, head_dim),
                                lambda s, h, sk, sf: (0, s, 0, h, 0, 0))
    return pl.pallas_call(
        attention_kernel,
        out_shape=(
            jax.ShapeDtypeStruct(q.shape, jnp.bfloat16),
            jax.ShapeDtypeStruct(q.shape, jnp.bfloat16),
            jax.ShapeDtypeStruct((spans, streams, 2, kv_heads, span_len, head_dim), jnp.float32),
        ),
        grid_spec=pltpu.PrefetchScalarGridSpec(
            num_scalar_prefetch=2,
            grid=(streams, kv_heads // HEAD_PAIR),
            in_specs=[
                head_block,
                head_block,
                window_block,
                pl.BlockSpec((1, 1, span_len), lambda s, h, sk, sf: (s, 0, 0)),
            ],
            out_specs=[head_block, head_block, window_block],
            scratch_shapes=[pltpu.VMEM((spans, HEAD_PAIR, span_len, group * span_len), jnp.float32),
                            pltpu.VMEM((spans, HEAD_PAIR, 1, group * span_len), jnp.float32)],
        ),
        compiler_params=pltpu.CompilerParams(vmem_limit_bytes=63 * 1024 * 1024),
    )(skip, span_firsts, q, grad_out, window, query_start)


def body(query, keys, values, grad_out, doc_starts):
    shard_count = lax.axis_size("seq")
    device_index = lax.axis_index("seq")
    window = ROUNDS
    span_len = query.shape[2]
    kv_heads = keys.shape[3]
    head_dim = query.shape[4]
    group = query.shape[3] // kv_heads
    q = jnp.transpose(query[:, 0], (0, 2, 3, 1))
    grad_o = jnp.transpose(grad_out[:, 0], (0, 2, 3, 1))
    current = jnp.stack([jnp.transpose(keys[:, 0], (0, 2, 1, 3)),
                         jnp.transpose(values[:, 0], (0, 2, 1, 3))], axis=1)
    flat = current.reshape(2, 2, kv_heads * span_len, head_dim)
    spans = forward_chain(flat, shard_count).reshape((window + 1,) + current.shape)
    span_firsts = jnp.stack([device_index, 2 * shard_count - 1 - device_index]).astype(jnp.int32)
    query_pos = span_firsts[:, None] * span_len + jnp.arange(span_len, dtype=jnp.int32)[None]
    query_start = jnp.max(
        jnp.where(doc_starts[None, None, :] <= query_pos[:, :, None], doc_starts[None, None, :], -1), axis=2)
    span_last = (span_firsts[:, None] - window + jnp.arange(window, dtype=jnp.int32)[None]) * span_len + span_len - 1
    skip = jnp.sum(span_last < query_start[:, :1], axis=1).astype(jnp.int32)
    attended, grad_q, terms = attention(
        skip, span_firsts, q, grad_o, spans, query_start[:, None, :], group)
    term_flat = terms.reshape(window + 1, 2, 2, kv_heads * span_len, head_dim)
    totals = backward_chain(term_flat, shard_count).reshape(current.shape)
    grad_kv = jnp.transpose(totals, (1, 0, 4, 2, 3))[:, :, None]
    return (
        jnp.transpose(attended, (0, 3, 1, 2))[:, None],
        jnp.transpose(grad_q, (0, 3, 1, 2))[:, None],
        grad_kv[0],
        grad_kv[1],
    )


def solution(mesh):
    placed = (
        P("batch", "seq", None, "head", None),
        P("batch", "seq", None, "head", None),
        P("batch", "seq", None, "head", None),
        P("batch", "seq", None, "head", None),
        P("batch"),
    )
    return jax.shard_map(
        body,
        mesh=mesh,
        in_specs=placed,
        out_specs=(
            P("batch", "seq", None, "head", None),
            P("batch", "seq", None, "head", None),
            P("batch", "seq", None, "head", None),
            P("batch", "seq", None, "head", None),
        ),
        check_vma=False,
    )
```

```python
import functools

import jax
import jax.numpy as jnp
from jax import lax
from jax.sharding import PartitionSpec as P

from jax.experimental import pallas as pl
from jax.experimental.pallas import tpu as pltpu

ROUNDS = 16


def greet_neighbours(me, count):
    barrier = pltpu.get_barrier_semaphore()

    @pl.when(me > 0)
    def _():
        pl.semaphore_signal(barrier, 1, device_id={"seq": me - 1})

    @pl.when(me < count - 1)
    def _():
        pl.semaphore_signal(barrier, 1, device_id={"seq": me + 1})

    @pl.when(jnp.logical_and(me > 0, me < count - 1))
    def _():
        pl.semaphore_wait(barrier, 2)

    @pl.when(jnp.logical_or(me == 0, me == count - 1))
    def _():
        pl.semaphore_wait(barrier, 1)


PIECES = 8


def piece_rows(i, total):
    size = total // (PIECES // 2)
    return i // (PIECES // 2), pl.ds((i % (PIECES // 2)) * size, size)


def forward_chain_kernel(count, cur, hist, send_sem, recv_sem, local_sem):
    me = lax.axis_index("seq")
    own = pltpu.make_async_copy(cur, hist.at[ROUNDS], local_sem.at[ROUNDS, 0])
    own.start()
    greet_neighbours(me, count)
    total = cur.shape[2]

    def copies(k, i):
        slot = ROUNDS - k
        kv, rows = piece_rows(i, total)
        src_a = cur.at[0, kv, rows] if k == 1 else hist.at[slot + 1, 0, kv, rows]
        src_b = cur.at[1, kv, rows] if k == 1 else hist.at[slot + 1, 1, kv, rows]
        send_a = pltpu.make_async_remote_copy(
            src_a, hist.at[slot, 0, kv, rows], send_sem.at[slot, 0, i], recv_sem.at[slot, 0, i],
            device_id={"seq": me + 1})
        send_b = pltpu.make_async_remote_copy(
            src_b, hist.at[slot, 1, kv, rows], send_sem.at[slot, 1, i], recv_sem.at[slot, 1, i],
            device_id={"seq": me - 1})
        local_b = pltpu.make_async_copy(src_a, hist.at[slot, 1, kv, rows], local_sem.at[slot, i])
        return send_a, send_b, local_b

    def a_sends(k):
        return jnp.logical_and(me < count - 1, me >= k - 1)

    def receive(k, i):
        send_a, send_b, local_b = copies(k, i)
        pl.when(me >= k)(send_a.wait_recv)
        pl.when(me < count - 1)(send_b.wait_recv)
        pl.when(me == count - 1)(local_b.wait)

    for k in range(1, ROUNDS + 1):
        for i in range(PIECES):
            if k > 1:
                receive(k - 1, i)
            send_a, send_b, local_b = copies(k, i)
            pl.when(a_sends(k))(send_a.start)
            pl.when(me > 0)(send_b.start)
            pl.when(me == count - 1)(local_b.start)

        @pl.when(me < k)
        def _():
            hist[ROUNDS - k, 0] = jnp.zeros(hist.shape[2:], hist.dtype)

    for i in range(PIECES):
        receive(ROUNDS, i)
    for k in range(1, ROUNDS + 1):
        for i in range(PIECES):
            send_a, send_b, _ = copies(k, i)
            pl.when(a_sends(k))(send_a.wait_send)
            pl.when(me > 0)(send_b.wait_send)
    own.wait()


def backward_chain_kernel(count, terms, out, send_buf, recv_buf, staged, send_sem, recv_sem, local_sem,
                          fetch_sem):
    me = lax.axis_index("seq")

    def fetch(t):
        return pltpu.make_async_copy(terms.at[t], staged.at[t % 2], fetch_sem.at[t % 2])

    fetch(0).start()
    greet_neighbours(me, count)
    total = terms.shape[3]

    def copies(t, i):
        slot = t - 1
        kv, rows = piece_rows(i, total)
        send_a = pltpu.make_async_remote_copy(
            send_buf.at[slot, 0, kv, rows], recv_buf.at[slot, 0, kv, rows],
            send_sem.at[slot, 0, i], recv_sem.at[slot, 0, i], device_id={"seq": me - 1})
        send_b = pltpu.make_async_remote_copy(
            send_buf.at[slot, 1, kv, rows], recv_buf.at[slot, 1, kv, rows],
            send_sem.at[slot, 1, i], recv_sem.at[slot, 1, i], device_id={"seq": me + 1})
        local_b = pltpu.make_async_copy(
            send_buf.at[slot, 1, kv, rows], recv_buf.at[slot, 0, kv, rows], local_sem.at[slot, i])
        return send_a, send_b, local_b

    def start(t, i):
        send_a, send_b, local_b = copies(t, i)
        pl.when(me > 0)(send_a.start)
        pl.when(me < count - 1)(send_b.start)
        pl.when(me == count - 1)(local_b.start)

    fetch(0).wait()
    fetch(1).start()
    for i in range(PIECES):
        kv, rows = piece_rows(i, total)
        send_buf[0, :, kv, rows] = staged[0, :, kv, rows].astype(send_buf.dtype)
        start(1, i)
    for t in range(1, ROUNDS + 1):
        slot = t - 1
        fetch(t).wait()
        if t < ROUNDS:
            fetch(t + 1).start()
        for i in range(PIECES):
            kv, rows = piece_rows(i, total)
            send_a, send_b, local_b = copies(t, i)
            pl.when(me < count - 1)(send_a.wait_recv)
            pl.when(me == count - 1)(local_b.wait)
            pl.when(me > 0)(send_b.wait_recv)
            total_a = recv_buf[slot, 0, kv, rows].astype(jnp.float32) + staged[t % 2, 0, kv, rows]
            if t < ROUNDS:
                send_buf[t, 0, kv, rows] = total_a.astype(send_buf.dtype)
            else:
                out[0, kv, rows] = total_a.astype(out.dtype)

            @pl.when(me > 0)
            def _():
                total_b = recv_buf[slot, 1, kv, rows].astype(jnp.float32) + staged[t % 2, 1, kv, rows]
                if t < ROUNDS:
                    send_buf[t, 1, kv, rows] = total_b.astype(send_buf.dtype)
                else:
                    out[1, kv, rows] = total_b.astype(out.dtype)

            @pl.when(me == 0)
            def _():
                total_b = staged[t % 2, 1, kv, rows]
                if t < ROUNDS:
                    send_buf[t, 1, kv, rows] = total_b.astype(send_buf.dtype)
                else:
                    out[1, kv, rows] = total_b.astype(out.dtype)

            if t < ROUNDS:
                start(t + 1, i)
    for t in range(1, ROUNDS + 1):
        for i in range(PIECES):
            send_a, send_b, _ = copies(t, i)
            pl.when(me > 0)(send_a.wait_send)
            pl.when(me < count - 1)(send_b.wait_send)


def forward_chain(current, count):
    shape = current.shape
    return pl.pallas_call(
        functools.partial(forward_chain_kernel, count),
        out_shape=jax.ShapeDtypeStruct((ROUNDS + 1,) + shape, current.dtype),
        in_specs=[pl.BlockSpec(memory_space=pltpu.VMEM)],
        out_specs=pl.BlockSpec(memory_space=pltpu.VMEM),
        scratch_shapes=[
            pltpu.SemaphoreType.DMA((ROUNDS, 2, PIECES)),
            pltpu.SemaphoreType.DMA((ROUNDS, 2, PIECES)),
            pltpu.SemaphoreType.DMA((ROUNDS + 1, PIECES)),
        ],
        compiler_params=pltpu.CompilerParams(
            collective_id=0, has_side_effects=True, vmem_limit_bytes=48 * 1024 * 1024),
    )(current)


def backward_chain(terms, count):
    shape = terms.shape[1:]
    return pl.pallas_call(
        functools.partial(backward_chain_kernel, count),
        out_shape=jax.ShapeDtypeStruct(shape, jnp.bfloat16),
        in_specs=[pl.BlockSpec(memory_space=pl.ANY)],
        out_specs=pl.BlockSpec(memory_space=pltpu.VMEM),
        scratch_shapes=[
            pltpu.VMEM((ROUNDS,) + shape, jnp.bfloat16),
            pltpu.VMEM((ROUNDS,) + shape, jnp.bfloat16),
            pltpu.VMEM((2,) + shape, jnp.float32),
            pltpu.SemaphoreType.DMA((ROUNDS, 2, PIECES)),
            pltpu.SemaphoreType.DMA((ROUNDS, 2, PIECES)),
            pltpu.SemaphoreType.DMA((ROUNDS, PIECES)),
            pltpu.SemaphoreType.DMA((2,)),
        ],
        compiler_params=pltpu.CompilerParams(
            collective_id=1, has_side_effects=True, vmem_limit_bytes=60 * 1024 * 1024),
    )(terms)


def attention_kernel(skip_ref, first_ref, q_ref, do_ref, win_ref, qstart_ref,
                     o_ref, dq_ref, terms_ref, cache, tops):
    stream = pl.program_id(0)
    first = skip_ref[stream]
    pair = win_ref.shape[3]
    group = q_ref.shape[1] // pair
    span_len, head_dim = q_ref.shape[2:]
    rows = group * span_len
    last = win_ref.shape[0] - 1
    scale = head_dim ** (-0.5)
    heads = range(pair)
    def lanes(ref, h):
        block = ref[0, h * group:(h + 1) * group]
        return jnp.concatenate([block[g] for g in range(group)], axis=1)

    q_ts = [lanes(q_ref, h) for h in heads]
    grad_t_lows = [lanes(do_ref, h) for h in heads]
    grad_ts = [g.astype(jnp.float32) for g in grad_t_lows]
    qs = [q.astype(jnp.float32).T.astype(jnp.bfloat16) for q in q_ts]
    grads = [g.T.astype(jnp.bfloat16) for g in grad_ts]
    query_start = qstart_ref[0]
    span = first_ref[stream]
    query_pos = lax.broadcasted_iota(jnp.int32, (1, span_len), 1) + span * span_len
    key_offset = lax.broadcasted_iota(jnp.int32, (span_len, span_len), 0)

    def mask(j):
        key_pos = key_offset + (span - last + j) * span_len
        allowed = jnp.logical_and(key_pos >= query_start, key_pos <= query_pos)
        return jnp.tile(allowed, (1, group))

    def scores(j, h, allowed):
        sc = jnp.dot(win_ref[j, 0, 0, h], q_ts[h], preferred_element_type=jnp.float32) * scale
        return jnp.where(allowed, sc, -jnp.inf)

    allowed = mask(last)
    top_list, total_list = [], []
    for h in heads:
        sc = scores(last, h, allowed)
        top = jnp.max(sc, axis=0, keepdims=True)
        expon = jnp.exp(sc - top)
        cache[last, h] = expon
        tops[last, h] = top
        top_list.append(top)
        total_list.append(jnp.sum(expon, axis=0, keepdims=True))

    def stat_step(j, carry):
        top_c, total_c = carry
        allowed = mask(j)
        new_tops, new_totals = [], []
        for h in heads:
            sc = scores(j, h, allowed)
            new_top = jnp.maximum(top_c[h], jnp.max(sc, axis=0, keepdims=True))
            expon = jnp.exp(sc - new_top)
            cache[j, h] = expon
            tops[j, h] = new_top
            new_tops.append(new_top)
            new_totals.append(total_c[h] * jnp.exp(top_c[h] - new_top)
                              + jnp.sum(expon, axis=0, keepdims=True))
        return tuple(new_tops), tuple(new_totals)

    top_list, total_list = lax.fori_loop(first, last, stat_step, (tuple(top_list), tuple(total_list)))
    inverses = [1.0 / t for t in total_list]

    def out_step(j, accs):
        new = []
        for h in heads:
            prob = cache[j, h] * (jnp.exp(tops[j, h] - top_list[h]) * inverses[h])
            cache[j, h] = prob
            value_t = win_ref[j, 0, 1, h].astype(jnp.float32).T.astype(jnp.bfloat16)
            new.append(accs[h] + jnp.dot(value_t, prob.astype(jnp.bfloat16),
                                         preferred_element_type=jnp.float32))
        return tuple(new)

    zero = jnp.zeros((head_dim, rows), jnp.float32)
    accs = out_step(last, tuple(zero for _ in heads))
    accs = lax.fori_loop(first, last, out_step, accs)
    deltas = []
    for h in heads:
        attended_t = accs[h].astype(jnp.bfloat16)
        o_ref[0, h * group:(h + 1) * group] = attended_t.astype(jnp.float32).T.astype(
            jnp.bfloat16).reshape(group, span_len, head_dim)
        deltas.append(jnp.sum(grad_ts[h] * attended_t.astype(jnp.float32), axis=0, keepdims=True))

    def grad_step(j, dqs):
        new = []
        for h in heads:
            prob = cache[j, h]
            low = prob.astype(jnp.bfloat16)
            grad_w = jnp.dot(win_ref[j, 0, 1, h], grad_t_lows[h], preferred_element_type=jnp.float32)
            grad_s = (prob * (grad_w - deltas[h]) * scale).astype(jnp.bfloat16)
            terms_ref[j, 0, 0, h] = jnp.dot(grad_s, qs[h], preferred_element_type=jnp.float32)
            terms_ref[j, 0, 1, h] = jnp.dot(low, grads[h], preferred_element_type=jnp.float32)
            key_t = win_ref[j, 0, 0, h].astype(jnp.float32).T.astype(jnp.bfloat16)
            new.append(dqs[h] + jnp.dot(key_t, grad_s, preferred_element_type=jnp.float32))
        return tuple(new)

    dqs = grad_step(last, tuple(zero for _ in heads))
    dqs = lax.fori_loop(first, last, grad_step, dqs)
    for h in heads:
        dq_ref[0, h * group:(h + 1) * group] = dqs[h].T.astype(jnp.bfloat16).reshape(
            group, span_len, head_dim)

    def clear(j, carry):
        terms_ref[j] = jnp.zeros(terms_ref.shape[1:], terms_ref.dtype)
        return carry

    lax.fori_loop(0, first, clear, 0)


HEAD_PAIR = 4


def attention(skip, span_firsts, q, grad_out, window, query_start, group):
    streams, heads, span_len, head_dim = q.shape
    kv_heads = heads // group
    spans = window.shape[0]
    head_block = pl.BlockSpec((1, group * HEAD_PAIR, span_len, head_dim), lambda s, h, sk, sf: (s, h, 0, 0))
    window_block = pl.BlockSpec((spans, 1, 2, HEAD_PAIR, span_len, head_dim),
                                lambda s, h, sk, sf: (0, s, 0, h, 0, 0))
    return pl.pallas_call(
        attention_kernel,
        out_shape=(
            jax.ShapeDtypeStruct(q.shape, jnp.bfloat16),
            jax.ShapeDtypeStruct(q.shape, jnp.bfloat16),
            jax.ShapeDtypeStruct((spans, streams, 2, kv_heads, span_len, head_dim), jnp.float32),
        ),
        grid_spec=pltpu.PrefetchScalarGridSpec(
            num_scalar_prefetch=2,
            grid=(streams, kv_heads // HEAD_PAIR),
            in_specs=[
                head_block,
                head_block,
                window_block,
                pl.BlockSpec((1, 1, span_len), lambda s, h, sk, sf: (s, 0, 0)),
            ],
            out_specs=[head_block, head_block, window_block],
            scratch_shapes=[pltpu.VMEM((spans, HEAD_PAIR, span_len, group * span_len), jnp.float32),
                            pltpu.VMEM((spans, HEAD_PAIR, 1, group * span_len), jnp.float32)],
        ),
        compiler_params=pltpu.CompilerParams(vmem_limit_bytes=63 * 1024 * 1024),
    )(skip, span_firsts, q, grad_out, window, query_start)


def body(query, keys, values, grad_out, doc_starts):
    shard_count = lax.axis_size("seq")
    device_index = lax.axis_index("seq")
    window = ROUNDS
    span_len = query.shape[2]
    kv_heads = keys.shape[3]
    head_dim = query.shape[4]
    group = query.shape[3] // kv_heads
    q = jnp.transpose(query[:, 0], (0, 2, 3, 1))
    grad_o = jnp.transpose(grad_out[:, 0], (0, 2, 3, 1))
    current = jnp.stack([jnp.transpose(keys[:, 0], (0, 2, 1, 3)),
                         jnp.transpose(values[:, 0], (0, 2, 1, 3))], axis=1)
    flat = current.reshape(2, 2, kv_heads * span_len, head_dim)
    spans = forward_chain(flat, shard_count).reshape((window + 1,) + current.shape)
    span_firsts = jnp.stack([device_index, 2 * shard_count - 1 - device_index]).astype(jnp.int32)
    query_pos = span_firsts[:, None] * span_len + jnp.arange(span_len, dtype=jnp.int32)[None]
    query_start = jnp.max(
        jnp.where(doc_starts[None, None, :] <= query_pos[:, :, None], doc_starts[None, None, :], -1), axis=2)
    span_last = (span_firsts[:, None] - window + jnp.arange(window, dtype=jnp.int32)[None]) * span_len + span_len - 1
    skip = jnp.sum(span_last < query_start[:, :1], axis=1).astype(jnp.int32)
    attended, grad_q, terms = attention(
        skip, span_firsts, q, grad_o, spans, query_start[:, None, :], group)
    term_flat = terms.reshape(window + 1, 2, 2, kv_heads * span_len, head_dim)
    totals = backward_chain(term_flat, shard_count).reshape(current.shape)
    grad_kv = jnp.transpose(totals, (1, 0, 3, 2, 4))[:, :, None]
    return (
        jnp.transpose(attended, (0, 2, 1, 3))[:, None],
        jnp.transpose(grad_q, (0, 2, 1, 3))[:, None],
        grad_kv[0],
        grad_kv[1],
    )


def solution(mesh):
    placed = (
        P("batch", "seq", None, "head", None),
        P("batch", "seq", None, "head", None),
        P("batch", "seq", None, "head", None),
        P("batch", "seq", None, "head", None),
        P("batch"),
    )
    return jax.shard_map(
        body,
        mesh=mesh,
        in_specs=placed,
        out_specs=(
            P("batch", "seq", None, "head", None),
            P("batch", "seq", None, "head", None),
            P("batch", "seq", None, "head", None),
            P("batch", "seq", None, "head", None),
        ),
        check_vma=False,
    )
```

```python
import functools

import jax
import jax.numpy as jnp
from jax import lax
from jax.sharding import PartitionSpec as P

from jax.experimental import pallas as pl
from jax.experimental.pallas import tpu as pltpu

ROUNDS = 16


def greet_neighbours(me, count):
    barrier = pltpu.get_barrier_semaphore()

    @pl.when(me > 0)
    def _():
        pl.semaphore_signal(barrier, 1, device_id={"seq": me - 1})

    @pl.when(me < count - 1)
    def _():
        pl.semaphore_signal(barrier, 1, device_id={"seq": me + 1})

    @pl.when(jnp.logical_and(me > 0, me < count - 1))
    def _():
        pl.semaphore_wait(barrier, 2)

    @pl.when(jnp.logical_or(me == 0, me == count - 1))
    def _():
        pl.semaphore_wait(barrier, 1)


PIECES = 8


def piece_rows(i, total):
    size = total // (PIECES // 2)
    return i // (PIECES // 2), pl.ds((i % (PIECES // 2)) * size, size)


def forward_chain_kernel(count, cur, hist, send_sem, recv_sem, local_sem):
    me = lax.axis_index("seq")
    own = pltpu.make_async_copy(cur, hist.at[ROUNDS], local_sem.at[ROUNDS, 0])
    own.start()
    greet_neighbours(me, count)
    total = cur.shape[2]

    def copies(k, i):
        slot = ROUNDS - k
        kv, rows = piece_rows(i, total)
        src_a = cur.at[0, kv, rows] if k == 1 else hist.at[slot + 1, 0, kv, rows]
        src_b = cur.at[1, kv, rows] if k == 1 else hist.at[slot + 1, 1, kv, rows]
        send_a = pltpu.make_async_remote_copy(
            src_a, hist.at[slot, 0, kv, rows], send_sem.at[slot, 0, i], recv_sem.at[slot, 0, i],
            device_id={"seq": me + 1})
        send_b = pltpu.make_async_remote_copy(
            src_b, hist.at[slot, 1, kv, rows], send_sem.at[slot, 1, i], recv_sem.at[slot, 1, i],
            device_id={"seq": me - 1})
        local_b = pltpu.make_async_copy(src_a, hist.at[slot, 1, kv, rows], local_sem.at[slot, i])
        return send_a, send_b, local_b

    def a_sends(k):
        return jnp.logical_and(me < count - 1, me >= k - 1)

    def receive(k, i):
        send_a, send_b, local_b = copies(k, i)
        pl.when(me >= k)(send_a.wait_recv)
        pl.when(me < count - 1)(send_b.wait_recv)
        pl.when(me == count - 1)(local_b.wait)

    for k in range(1, ROUNDS + 1):
        for i in range(PIECES):
            if k > 1:
                receive(k - 1, i)
            send_a, send_b, local_b = copies(k, i)
            pl.when(a_sends(k))(send_a.start)
            pl.when(me > 0)(send_b.start)
            pl.when(me == count - 1)(local_b.start)

        @pl.when(me < k)
        def _():
            hist[ROUNDS - k, 0] = jnp.zeros(hist.shape[2:], hist.dtype)

    for i in range(PIECES):
        receive(ROUNDS, i)
    for k in range(1, ROUNDS + 1):
        for i in range(PIECES):
            send_a, send_b, _ = copies(k, i)
            pl.when(a_sends(k))(send_a.wait_send)
            pl.when(me > 0)(send_b.wait_send)
    own.wait()


def backward_chain_kernel(count, terms, out, send_buf, recv_buf, staged, send_sem, recv_sem, local_sem,
                          fetch_sem):
    me = lax.axis_index("seq")

    def fetch(t):
        return pltpu.make_async_copy(terms.at[t], staged.at[t % 2], fetch_sem.at[t % 2])

    fetch(0).start()
    greet_neighbours(me, count)
    total = terms.shape[3]

    def copies(t, i):
        slot = t - 1
        kv, rows = piece_rows(i, total)
        send_a = pltpu.make_async_remote_copy(
            send_buf.at[slot, 0, kv, rows], recv_buf.at[slot, 0, kv, rows],
            send_sem.at[slot, 0, i], recv_sem.at[slot, 0, i], device_id={"seq": me - 1})
        send_b = pltpu.make_async_remote_copy(
            send_buf.at[slot, 1, kv, rows], recv_buf.at[slot, 1, kv, rows],
            send_sem.at[slot, 1, i], recv_sem.at[slot, 1, i], device_id={"seq": me + 1})
        local_b = pltpu.make_async_copy(
            send_buf.at[slot, 1, kv, rows], recv_buf.at[slot, 0, kv, rows], local_sem.at[slot, i])
        return send_a, send_b, local_b

    def start(t, i):
        send_a, send_b, local_b = copies(t, i)
        pl.when(me > 0)(send_a.start)
        pl.when(me < count - 1)(send_b.start)
        pl.when(me == count - 1)(local_b.start)

    fetch(0).wait()
    fetch(1).start()
    for i in range(PIECES):
        kv, rows = piece_rows(i, total)
        send_buf[0, :, kv, rows] = staged[0, :, kv, rows].astype(send_buf.dtype)
        start(1, i)
    for t in range(1, ROUNDS + 1):
        slot = t - 1
        fetch(t).wait()
        if t < ROUNDS:
            fetch(t + 1).start()
        for i in range(PIECES):
            kv, rows = piece_rows(i, total)
            send_a, send_b, local_b = copies(t, i)
            pl.when(me < count - 1)(send_a.wait_recv)
            pl.when(me == count - 1)(local_b.wait)
            pl.when(me > 0)(send_b.wait_recv)
            total_a = recv_buf[slot, 0, kv, rows].astype(jnp.float32) + staged[t % 2, 0, kv, rows].astype(jnp.float32)
            if t < ROUNDS:
                send_buf[t, 0, kv, rows] = total_a.astype(send_buf.dtype)
            else:
                out[0, kv, rows] = total_a.astype(out.dtype)

            @pl.when(me > 0)
            def _():
                total_b = recv_buf[slot, 1, kv, rows].astype(jnp.float32) + staged[t % 2, 1, kv, rows].astype(jnp.float32)
                if t < ROUNDS:
                    send_buf[t, 1, kv, rows] = total_b.astype(send_buf.dtype)
                else:
                    out[1, kv, rows] = total_b.astype(out.dtype)

            @pl.when(me == 0)
            def _():
                total_b = staged[t % 2, 1, kv, rows].astype(jnp.float32)
                if t < ROUNDS:
                    send_buf[t, 1, kv, rows] = total_b.astype(send_buf.dtype)
                else:
                    out[1, kv, rows] = total_b.astype(out.dtype)

            if t < ROUNDS:
                start(t + 1, i)
    for t in range(1, ROUNDS + 1):
        for i in range(PIECES):
            send_a, send_b, _ = copies(t, i)
            pl.when(me > 0)(send_a.wait_send)
            pl.when(me < count - 1)(send_b.wait_send)


def forward_chain(current, count):
    shape = current.shape
    return pl.pallas_call(
        functools.partial(forward_chain_kernel, count),
        out_shape=jax.ShapeDtypeStruct((ROUNDS + 1,) + shape, current.dtype),
        in_specs=[pl.BlockSpec(memory_space=pltpu.VMEM)],
        out_specs=pl.BlockSpec(memory_space=pltpu.VMEM),
        scratch_shapes=[
            pltpu.SemaphoreType.DMA((ROUNDS, 2, PIECES)),
            pltpu.SemaphoreType.DMA((ROUNDS, 2, PIECES)),
            pltpu.SemaphoreType.DMA((ROUNDS + 1, PIECES)),
        ],
        compiler_params=pltpu.CompilerParams(
            collective_id=0, has_side_effects=True, vmem_limit_bytes=48 * 1024 * 1024),
    )(current)


def backward_chain(terms, count):
    shape = terms.shape[1:]
    return pl.pallas_call(
        functools.partial(backward_chain_kernel, count),
        out_shape=jax.ShapeDtypeStruct(shape, jnp.bfloat16),
        in_specs=[pl.BlockSpec(memory_space=pl.ANY)],
        out_specs=pl.BlockSpec(memory_space=pltpu.VMEM),
        scratch_shapes=[
            pltpu.VMEM((ROUNDS,) + shape, jnp.bfloat16),
            pltpu.VMEM((ROUNDS,) + shape, jnp.bfloat16),
            pltpu.VMEM((2,) + shape, terms.dtype),
            pltpu.SemaphoreType.DMA((ROUNDS, 2, PIECES)),
            pltpu.SemaphoreType.DMA((ROUNDS, 2, PIECES)),
            pltpu.SemaphoreType.DMA((ROUNDS, PIECES)),
            pltpu.SemaphoreType.DMA((2,)),
        ],
        compiler_params=pltpu.CompilerParams(
            collective_id=1, has_side_effects=True, vmem_limit_bytes=60 * 1024 * 1024),
    )(terms)


def attention_kernel(skip_ref, first_ref, q_ref, do_ref, win_ref, qstart_ref,
                     o_ref, dq_ref, terms_ref, cache, tops):
    stream = pl.program_id(0)
    first = skip_ref[stream]
    pair = win_ref.shape[3]
    group = q_ref.shape[1] // pair
    span_len, head_dim = q_ref.shape[2:]
    rows = group * span_len
    last = win_ref.shape[0] - 1
    scale = head_dim ** (-0.5)
    heads = range(pair)
    def lanes(ref, h):
        block = ref[0, h * group:(h + 1) * group]
        return jnp.concatenate([block[g] for g in range(group)], axis=1)

    q_ts = [lanes(q_ref, h) for h in heads]
    grad_t_lows = [lanes(do_ref, h) for h in heads]
    grad_ts = [g.astype(jnp.float32) for g in grad_t_lows]
    contract_last = (((1,), (1,)), ((), ()))
    query_start = qstart_ref[0]
    span = first_ref[stream]
    query_pos = lax.broadcasted_iota(jnp.int32, (1, span_len), 1) + span * span_len
    key_offset = lax.broadcasted_iota(jnp.int32, (span_len, span_len), 0)

    def mask(j):
        key_pos = key_offset + (span - last + j) * span_len
        allowed = jnp.logical_and(key_pos >= query_start, key_pos <= query_pos)
        return jnp.tile(allowed, (1, group))

    def scores(j, h, allowed):
        sc = jnp.dot(win_ref[j, 0, 0, h], q_ts[h], preferred_element_type=jnp.float32) * scale
        return jnp.where(allowed, sc, -jnp.inf)

    allowed = mask(last)
    top_list, total_list = [], []
    for h in heads:
        sc = scores(last, h, allowed)
        top = jnp.max(sc, axis=0, keepdims=True)
        expon = jnp.exp(sc - top)
        cache[last, h] = expon
        tops[last, h] = top
        top_list.append(top)
        total_list.append(jnp.sum(expon, axis=0, keepdims=True))

    def stat_step(j, carry):
        top_c, total_c = carry
        allowed = mask(j)
        new_tops, new_totals = [], []
        for h in heads:
            sc = scores(j, h, allowed)
            new_top = jnp.maximum(top_c[h], jnp.max(sc, axis=0, keepdims=True))
            expon = jnp.exp(sc - new_top)
            cache[j, h] = expon
            tops[j, h] = new_top
            new_tops.append(new_top)
            new_totals.append(total_c[h] * jnp.exp(top_c[h] - new_top)
                              + jnp.sum(expon, axis=0, keepdims=True))
        return tuple(new_tops), tuple(new_totals)

    top_list, total_list = lax.fori_loop(first, last, stat_step, (tuple(top_list), tuple(total_list)))
    inverses = [1.0 / t for t in total_list]

    def out_step(j, accs):
        new = []
        for h in heads:
            prob = cache[j, h] * (jnp.exp(tops[j, h] - top_list[h]) * inverses[h])
            cache[j, h] = prob
            value_t = win_ref[j, 0, 1, h].astype(jnp.float32).T.astype(jnp.bfloat16)
            new.append(accs[h] + jnp.dot(value_t, prob.astype(jnp.bfloat16),
                                         preferred_element_type=jnp.float32))
        return tuple(new)

    zero = jnp.zeros((head_dim, rows), jnp.float32)
    accs = out_step(last, tuple(zero for _ in heads))
    accs = lax.fori_loop(first, last, out_step, accs)
    deltas = []
    for h in heads:
        attended_t = accs[h].astype(jnp.bfloat16)
        for g in range(group):
            o_ref[0, h * group + g] = attended_t[:, g * span_len:(g + 1) * span_len]
        deltas.append(jnp.sum(grad_ts[h] * attended_t.astype(jnp.float32), axis=0, keepdims=True))

    def grad_step(j, dqs):
        new = []
        for h in heads:
            prob = cache[j, h]
            low = prob.astype(jnp.bfloat16)
            grad_w = jnp.dot(win_ref[j, 0, 1, h], grad_t_lows[h], preferred_element_type=jnp.float32)
            grad_s = (prob * (grad_w - deltas[h]) * scale).astype(jnp.bfloat16)
            terms_ref[j, 0, 0, h] = lax.dot_general(q_ts[h], grad_s, contract_last,
                                                    preferred_element_type=jnp.float32).astype(terms_ref.dtype)
            terms_ref[j, 0, 1, h] = lax.dot_general(grad_t_lows[h], low, contract_last,
                                                    preferred_element_type=jnp.float32).astype(terms_ref.dtype)
            key_t = win_ref[j, 0, 0, h].astype(jnp.float32).T.astype(jnp.bfloat16)
            new.append(dqs[h] + jnp.dot(key_t, grad_s, preferred_element_type=jnp.float32))
        return tuple(new)

    dqs = grad_step(last, tuple(zero for _ in heads))
    dqs = lax.fori_loop(first, last, grad_step, dqs)
    for h in heads:
        dq_low = dqs[h].astype(jnp.bfloat16)
        for g in range(group):
            dq_ref[0, h * group + g] = dq_low[:, g * span_len:(g + 1) * span_len]

    def clear(j, carry):
        terms_ref[j] = jnp.zeros(terms_ref.shape[1:], terms_ref.dtype)
        return carry

    lax.fori_loop(0, first, clear, 0)


HEAD_PAIR = 4


def attention(skip, span_firsts, q, grad_out, window, query_start, group):
    streams, heads, span_len, head_dim = q.shape
    kv_heads = heads // group
    spans = window.shape[0]
    head_block = pl.BlockSpec((1, group * HEAD_PAIR, span_len, head_dim), lambda s, h, sk, sf: (s, h, 0, 0))
    window_block = pl.BlockSpec((spans, 1, 2, HEAD_PAIR, span_len, head_dim),
                                lambda s, h, sk, sf: (0, s, 0, h, 0, 0))
    return pl.pallas_call(
        attention_kernel,
        out_shape=(
            jax.ShapeDtypeStruct(q.shape, jnp.bfloat16),
            jax.ShapeDtypeStruct(q.shape, jnp.bfloat16),
            jax.ShapeDtypeStruct((spans, streams, 2, kv_heads, span_len, head_dim), jnp.bfloat16),
        ),
        grid_spec=pltpu.PrefetchScalarGridSpec(
            num_scalar_prefetch=2,
            grid=(streams, kv_heads // HEAD_PAIR),
            in_specs=[
                head_block,
                head_block,
                window_block,
                pl.BlockSpec((1, 1, span_len), lambda s, h, sk, sf: (s, 0, 0)),
            ],
            out_specs=[head_block, head_block, window_block],
            scratch_shapes=[pltpu.VMEM((spans, HEAD_PAIR, span_len, group * span_len), jnp.float32),
                            pltpu.VMEM((spans, HEAD_PAIR, 1, group * span_len), jnp.float32)],
        ),
        compiler_params=pltpu.CompilerParams(vmem_limit_bytes=63 * 1024 * 1024),
    )(skip, span_firsts, q, grad_out, window, query_start)


def body(query, keys, values, grad_out, doc_starts):
    shard_count = lax.axis_size("seq")
    device_index = lax.axis_index("seq")
    window = ROUNDS
    span_len = query.shape[2]
    kv_heads = keys.shape[3]
    head_dim = query.shape[4]
    group = query.shape[3] // kv_heads
    q = jnp.transpose(query[:, 0], (0, 2, 3, 1))
    grad_o = jnp.transpose(grad_out[:, 0], (0, 2, 3, 1))
    current = jnp.stack([jnp.transpose(keys[:, 0], (0, 2, 1, 3)),
                         jnp.transpose(values[:, 0], (0, 2, 1, 3))], axis=1)
    flat = current.reshape(2, 2, kv_heads * span_len, head_dim)
    spans = forward_chain(flat, shard_count).reshape((window + 1,) + current.shape)
    span_firsts = jnp.stack([device_index, 2 * shard_count - 1 - device_index]).astype(jnp.int32)
    query_pos = span_firsts[:, None] * span_len + jnp.arange(span_len, dtype=jnp.int32)[None]
    query_start = jnp.max(
        jnp.where(doc_starts[None, None, :] <= query_pos[:, :, None], doc_starts[None, None, :], -1), axis=2)
    span_last = (span_firsts[:, None] - window + jnp.arange(window, dtype=jnp.int32)[None]) * span_len + span_len - 1
    skip = jnp.sum(span_last < query_start[:, :1], axis=1).astype(jnp.int32)
    attended, grad_q, terms = attention(
        skip, span_firsts, q, grad_o, spans, query_start[:, None, :], group)
    term_flat = terms.reshape(window + 1, 2, 2, kv_heads * span_len, head_dim)
    totals = backward_chain(term_flat, shard_count).reshape(current.shape)
    grad_kv = jnp.transpose(totals, (1, 0, 4, 2, 3))[:, :, None]
    return (
        jnp.transpose(attended, (0, 3, 1, 2))[:, None],
        jnp.transpose(grad_q, (0, 3, 1, 2))[:, None],
        grad_kv[0],
        grad_kv[1],
    )


def solution(mesh):
    placed = (
        P("batch", "seq", None, "head", None),
        P("batch", "seq", None, "head", None),
        P("batch", "seq", None, "head", None),
        P("batch", "seq", None, "head", None),
        P("batch"),
    )
    return jax.shard_map(
        body,
        mesh=mesh,
        in_specs=placed,
        out_specs=(
            P("batch", "seq", None, "head", None),
            P("batch", "seq", None, "head", None),
            P("batch", "seq", None, "head", None),
            P("batch", "seq", None, "head", None),
        ),
        check_vma=False,
    )
```

```python
import functools

import jax
import jax.numpy as jnp
from jax import lax
from jax.sharding import PartitionSpec as P

from jax.experimental import pallas as pl
from jax.experimental.pallas import tpu as pltpu

ROUNDS = 16


def greet_neighbours(me, count):
    barrier = pltpu.get_barrier_semaphore()

    @pl.when(me > 0)
    def _():
        pl.semaphore_signal(barrier, 1, device_id={"seq": me - 1})

    @pl.when(me < count - 1)
    def _():
        pl.semaphore_signal(barrier, 1, device_id={"seq": me + 1})

    @pl.when(jnp.logical_and(me > 0, me < count - 1))
    def _():
        pl.semaphore_wait(barrier, 2)

    @pl.when(jnp.logical_or(me == 0, me == count - 1))
    def _():
        pl.semaphore_wait(barrier, 1)


PIECES = 8


def piece_rows(i, total):
    size = total // (PIECES // 2)
    return i // (PIECES // 2), pl.ds((i % (PIECES // 2)) * size, size)


def forward_chain_kernel(count, cur, hist, send_sem, recv_sem, local_sem):
    me = lax.axis_index("seq")
    own = pltpu.make_async_copy(cur, hist.at[ROUNDS], local_sem.at[ROUNDS, 0])
    own.start()
    greet_neighbours(me, count)
    total = cur.shape[2]

    def copies(k, i):
        slot = ROUNDS - k
        kv, rows = piece_rows(i, total)
        src_a = cur.at[0, kv, rows] if k == 1 else hist.at[slot + 1, 0, kv, rows]
        src_b = cur.at[1, kv, rows] if k == 1 else hist.at[slot + 1, 1, kv, rows]
        send_a = pltpu.make_async_remote_copy(
            src_a, hist.at[slot, 0, kv, rows], send_sem.at[slot, 0, i], recv_sem.at[slot, 0, i],
            device_id={"seq": me + 1})
        send_b = pltpu.make_async_remote_copy(
            src_b, hist.at[slot, 1, kv, rows], send_sem.at[slot, 1, i], recv_sem.at[slot, 1, i],
            device_id={"seq": me - 1})
        local_b = pltpu.make_async_copy(src_a, hist.at[slot, 1, kv, rows], local_sem.at[slot, i])
        return send_a, send_b, local_b

    def a_sends(k):
        return jnp.logical_and(me < count - 1, me >= k - 1)

    def receive(k, i):
        send_a, send_b, local_b = copies(k, i)
        pl.when(me >= k)(send_a.wait_recv)
        pl.when(me < count - 1)(send_b.wait_recv)
        pl.when(me == count - 1)(local_b.wait)

    for k in range(1, ROUNDS + 1):
        for i in range(PIECES):
            if k > 1:
                receive(k - 1, i)
            send_a, send_b, local_b = copies(k, i)
            pl.when(a_sends(k))(send_a.start)
            pl.when(me > 0)(send_b.start)
            pl.when(me == count - 1)(local_b.start)

        @pl.when(me < k)
        def _():
            hist[ROUNDS - k, 0] = jnp.zeros(hist.shape[2:], hist.dtype)

    for i in range(PIECES):
        receive(ROUNDS, i)
    for k in range(1, ROUNDS + 1):
        for i in range(PIECES):
            send_a, send_b, _ = copies(k, i)
            pl.when(a_sends(k))(send_a.wait_send)
            pl.when(me > 0)(send_b.wait_send)
    own.wait()


def backward_chain_kernel(count, terms, out, send_buf, recv_buf, staged, send_sem, recv_sem, local_sem,
                          fetch_sem):
    me = lax.axis_index("seq")

    def fetch(t):
        return pltpu.make_async_copy(terms.at[t], staged.at[t % 2], fetch_sem.at[t % 2])

    fetch(0).start()
    greet_neighbours(me, count)
    total = terms.shape[3]

    def copies(t, i):
        slot = t - 1
        kv, rows = piece_rows(i, total)
        send_a = pltpu.make_async_remote_copy(
            send_buf.at[slot, 0, kv, rows], recv_buf.at[slot, 0, kv, rows],
            send_sem.at[slot, 0, i], recv_sem.at[slot, 0, i], device_id={"seq": me - 1})
        send_b = pltpu.make_async_remote_copy(
            send_buf.at[slot, 1, kv, rows], recv_buf.at[slot, 1, kv, rows],
            send_sem.at[slot, 1, i], recv_sem.at[slot, 1, i], device_id={"seq": me + 1})
        local_b = pltpu.make_async_copy(
            send_buf.at[slot, 1, kv, rows], recv_buf.at[slot, 0, kv, rows], local_sem.at[slot, i])
        return send_a, send_b, local_b

    def start(t, i):
        send_a, send_b, local_b = copies(t, i)
        pl.when(me > 0)(send_a.start)
        pl.when(me < count - 1)(send_b.start)
        pl.when(me == count - 1)(local_b.start)

    fetch(0).wait()
    fetch(1).start()
    for i in range(PIECES):
        kv, rows = piece_rows(i, total)
        send_buf[0, :, kv, rows] = staged[0, :, kv, rows].astype(send_buf.dtype)
        start(1, i)
    for t in range(1, ROUNDS + 1):
        slot = t - 1
        fetch(t).wait()
        if t < ROUNDS:
            fetch(t + 1).start()
        for i in range(PIECES):
            kv, rows = piece_rows(i, total)
            send_a, send_b, local_b = copies(t, i)
            pl.when(me < count - 1)(send_a.wait_recv)
            pl.when(me == count - 1)(local_b.wait)
            pl.when(me > 0)(send_b.wait_recv)
            total_a = recv_buf[slot, 0, kv, rows].astype(jnp.float32) + staged[t % 2, 0, kv, rows].astype(jnp.float32)
            if t < ROUNDS:
                send_buf[t, 0, kv, rows] = total_a.astype(send_buf.dtype)
            else:
                out[0, kv, rows] = total_a.astype(out.dtype)

            @pl.when(me > 0)
            def _():
                total_b = recv_buf[slot, 1, kv, rows].astype(jnp.float32) + staged[t % 2, 1, kv, rows].astype(jnp.float32)
                if t < ROUNDS:
                    send_buf[t, 1, kv, rows] = total_b.astype(send_buf.dtype)
                else:
                    out[1, kv, rows] = total_b.astype(out.dtype)

            @pl.when(me == 0)
            def _():
                total_b = staged[t % 2, 1, kv, rows].astype(jnp.float32)
                if t < ROUNDS:
                    send_buf[t, 1, kv, rows] = total_b.astype(send_buf.dtype)
                else:
                    out[1, kv, rows] = total_b.astype(out.dtype)

            if t < ROUNDS:
                start(t + 1, i)
    for t in range(1, ROUNDS + 1):
        for i in range(PIECES):
            send_a, send_b, _ = copies(t, i)
            pl.when(me > 0)(send_a.wait_send)
            pl.when(me < count - 1)(send_b.wait_send)


def forward_chain(current, count):
    shape = current.shape
    return pl.pallas_call(
        functools.partial(forward_chain_kernel, count),
        out_shape=jax.ShapeDtypeStruct((ROUNDS + 1,) + shape, current.dtype),
        in_specs=[pl.BlockSpec(memory_space=pltpu.VMEM)],
        out_specs=pl.BlockSpec(memory_space=pltpu.VMEM),
        scratch_shapes=[
            pltpu.SemaphoreType.DMA((ROUNDS, 2, PIECES)),
            pltpu.SemaphoreType.DMA((ROUNDS, 2, PIECES)),
            pltpu.SemaphoreType.DMA((ROUNDS + 1, PIECES)),
        ],
        compiler_params=pltpu.CompilerParams(
            collective_id=0, has_side_effects=True, vmem_limit_bytes=48 * 1024 * 1024),
    )(current)


def backward_chain(terms, count):
    shape = terms.shape[1:]
    return pl.pallas_call(
        functools.partial(backward_chain_kernel, count),
        out_shape=jax.ShapeDtypeStruct(shape, jnp.bfloat16),
        in_specs=[pl.BlockSpec(memory_space=pl.ANY)],
        out_specs=pl.BlockSpec(memory_space=pltpu.VMEM),
        scratch_shapes=[
            pltpu.VMEM((ROUNDS,) + shape, jnp.bfloat16),
            pltpu.VMEM((ROUNDS,) + shape, jnp.bfloat16),
            pltpu.VMEM((2,) + shape, terms.dtype),
            pltpu.SemaphoreType.DMA((ROUNDS, 2, PIECES)),
            pltpu.SemaphoreType.DMA((ROUNDS, 2, PIECES)),
            pltpu.SemaphoreType.DMA((ROUNDS, PIECES)),
            pltpu.SemaphoreType.DMA((2,)),
        ],
        compiler_params=pltpu.CompilerParams(
            collective_id=1, has_side_effects=True, vmem_limit_bytes=60 * 1024 * 1024),
    )(terms)


def attention_kernel(skip_ref, first_ref, q_ref, do_ref, win_ref, qstart_ref,
                     o_ref, dq_ref, terms_ref, cache, tops):
    stream = pl.program_id(0)
    first = skip_ref[stream]
    pair = win_ref.shape[3]
    group = q_ref.shape[1] // pair
    span_len, head_dim = q_ref.shape[2:]
    rows = group * span_len
    last = win_ref.shape[0] - 1
    scale = head_dim ** (-0.5)
    heads = range(pair)
    def lanes(ref, h):
        block = ref[0, h * group:(h + 1) * group]
        return jnp.concatenate([block[g] for g in range(group)], axis=1)

    q_ts = [lanes(q_ref, h) for h in heads]
    grad_t_lows = [lanes(do_ref, h) for h in heads]
    grad_ts = [g.astype(jnp.float32) for g in grad_t_lows]
    qs = [q.astype(jnp.float32).T.astype(jnp.bfloat16) for q in q_ts]
    grads = [g.T.astype(jnp.bfloat16) for g in grad_ts]
    query_start = qstart_ref[0]
    span = first_ref[stream]
    query_pos = lax.broadcasted_iota(jnp.int32, (1, span_len), 1) + span * span_len
    key_offset = lax.broadcasted_iota(jnp.int32, (span_len, span_len), 0)

    def mask(j):
        key_pos = key_offset + (span - last + j) * span_len
        allowed = jnp.logical_and(key_pos >= query_start, key_pos <= query_pos)
        return jnp.tile(allowed, (1, group))

    def scores(j, h, allowed):
        sc = jnp.dot(win_ref[j, 0, 0, h], q_ts[h], preferred_element_type=jnp.float32) * scale
        return jnp.where(allowed, sc, -jnp.inf)

    allowed = mask(last)
    top_list, total_list = [], []
    for h in heads:
        sc = scores(last, h, allowed)
        top = jnp.max(sc, axis=0, keepdims=True)
        expon = jnp.exp(sc - top)
        cache[last, h] = expon
        tops[last, h] = top
        top_list.append(top)
        total_list.append(jnp.sum(expon, axis=0, keepdims=True))

    def stat_step(j, carry):
        top_c, total_c = carry
        allowed = mask(j)
        new_tops, new_totals = [], []
        for h in heads:
            sc = scores(j, h, allowed)
            new_top = jnp.maximum(top_c[h], jnp.max(sc, axis=0, keepdims=True))
            expon = jnp.exp(sc - new_top)
            cache[j, h] = expon
            tops[j, h] = new_top
            new_tops.append(new_top)
            new_totals.append(total_c[h] * jnp.exp(top_c[h] - new_top)
                              + jnp.sum(expon, axis=0, keepdims=True))
        return tuple(new_tops), tuple(new_totals)

    top_list, total_list = lax.fori_loop(first, last, stat_step, (tuple(top_list), tuple(total_list)))
    inverses = [1.0 / t for t in total_list]

    def out_step(j, accs):
        new = []
        for h in heads:
            prob = cache[j, h] * (jnp.exp(tops[j, h] - top_list[h]) * inverses[h])
            cache[j, h] = prob
            value_t = win_ref[j, 0, 1, h].astype(jnp.float32).T.astype(jnp.bfloat16)
            new.append(accs[h] + jnp.dot(value_t, prob.astype(jnp.bfloat16),
                                         preferred_element_type=jnp.float32))
        return tuple(new)

    zero = jnp.zeros((head_dim, rows), jnp.float32)
    accs = out_step(last, tuple(zero for _ in heads))
    accs = lax.fori_loop(first, last, out_step, accs)
    deltas = []
    for h in heads:
        attended_t = accs[h].astype(jnp.bfloat16)
        o_ref[0, h * group:(h + 1) * group] = attended_t.astype(jnp.float32).T.astype(
            jnp.bfloat16).reshape(group, span_len, head_dim)
        deltas.append(jnp.sum(grad_ts[h] * attended_t.astype(jnp.float32), axis=0, keepdims=True))

    def grad_step(j, dqs):
        new = []
        for h in heads:
            prob = cache[j, h]
            low = prob.astype(jnp.bfloat16)
            grad_w = jnp.dot(win_ref[j, 0, 1, h], grad_t_lows[h], preferred_element_type=jnp.float32)
            grad_s = (prob * (grad_w - deltas[h]) * scale).astype(jnp.bfloat16)
            terms_ref[j, 0, 0, h] = jnp.dot(grad_s, qs[h], preferred_element_type=jnp.float32).astype(
                terms_ref.dtype)
            terms_ref[j, 0, 1, h] = jnp.dot(low, grads[h], preferred_element_type=jnp.float32).astype(
                terms_ref.dtype)
            key_t = win_ref[j, 0, 0, h].astype(jnp.float32).T.astype(jnp.bfloat16)
            new.append(dqs[h] + jnp.dot(key_t, grad_s, preferred_element_type=jnp.float32))
        return tuple(new)

    dqs = grad_step(last, tuple(zero for _ in heads))
    dqs = lax.fori_loop(first, last, grad_step, dqs)
    for h in heads:
        dq_ref[0, h * group:(h + 1) * group] = dqs[h].T.astype(jnp.bfloat16).reshape(
            group, span_len, head_dim)

    def clear(j, carry):
        terms_ref[j] = jnp.zeros(terms_ref.shape[1:], terms_ref.dtype)
        return carry

    lax.fori_loop(0, first, clear, 0)


HEAD_PAIR = 4


def attention(skip, span_firsts, q, grad_out, window, query_start, group):
    streams, heads, span_len, head_dim = q.shape
    kv_heads = heads // group
    spans = window.shape[0]
    head_block = pl.BlockSpec((1, group * HEAD_PAIR, span_len, head_dim), lambda s, h, sk, sf: (s, h, 0, 0))
    window_block = pl.BlockSpec((spans, 1, 2, HEAD_PAIR, span_len, head_dim),
                                lambda s, h, sk, sf: (0, s, 0, h, 0, 0))
    return pl.pallas_call(
        attention_kernel,
        out_shape=(
            jax.ShapeDtypeStruct(q.shape, jnp.bfloat16),
            jax.ShapeDtypeStruct(q.shape, jnp.bfloat16),
            jax.ShapeDtypeStruct((spans, streams, 2, kv_heads, span_len, head_dim), jnp.bfloat16),
        ),
        grid_spec=pltpu.PrefetchScalarGridSpec(
            num_scalar_prefetch=2,
            grid=(streams, kv_heads // HEAD_PAIR),
            in_specs=[
                head_block,
                head_block,
                window_block,
                pl.BlockSpec((1, 1, span_len), lambda s, h, sk, sf: (s, 0, 0)),
            ],
            out_specs=[head_block, head_block, window_block],
            scratch_shapes=[pltpu.VMEM((spans, HEAD_PAIR, span_len, group * span_len), jnp.float32),
                            pltpu.VMEM((spans, HEAD_PAIR, 1, group * span_len), jnp.float32)],
        ),
        compiler_params=pltpu.CompilerParams(vmem_limit_bytes=63 * 1024 * 1024),
    )(skip, span_firsts, q, grad_out, window, query_start)


def body(query, keys, values, grad_out, doc_starts):
    shard_count = lax.axis_size("seq")
    device_index = lax.axis_index("seq")
    window = ROUNDS
    span_len = query.shape[2]
    kv_heads = keys.shape[3]
    head_dim = query.shape[4]
    group = query.shape[3] // kv_heads
    q = jnp.transpose(query[:, 0], (0, 2, 3, 1))
    grad_o = jnp.transpose(grad_out[:, 0], (0, 2, 3, 1))
    current = jnp.stack([jnp.transpose(keys[:, 0], (0, 2, 1, 3)),
                         jnp.transpose(values[:, 0], (0, 2, 1, 3))], axis=1)
    flat = current.reshape(2, 2, kv_heads * span_len, head_dim)
    spans = forward_chain(flat, shard_count).reshape((window + 1,) + current.shape)
    span_firsts = jnp.stack([device_index, 2 * shard_count - 1 - device_index]).astype(jnp.int32)
    query_pos = span_firsts[:, None] * span_len + jnp.arange(span_len, dtype=jnp.int32)[None]
    query_start = jnp.max(
        jnp.where(doc_starts[None, None, :] <= query_pos[:, :, None], doc_starts[None, None, :], -1), axis=2)
    span_last = (span_firsts[:, None] - window + jnp.arange(window, dtype=jnp.int32)[None]) * span_len + span_len - 1
    skip = jnp.sum(span_last < query_start[:, :1], axis=1).astype(jnp.int32)
    attended, grad_q, terms = attention(
        skip, span_firsts, q, grad_o, spans, query_start[:, None, :], group)
    term_flat = terms.reshape(window + 1, 2, 2, kv_heads * span_len, head_dim)
    totals = backward_chain(term_flat, shard_count).reshape(current.shape)
    grad_kv = jnp.transpose(totals, (1, 0, 3, 2, 4))[:, :, None]
    return (
        jnp.transpose(attended, (0, 2, 1, 3))[:, None],
        jnp.transpose(grad_q, (0, 2, 1, 3))[:, None],
        grad_kv[0],
        grad_kv[1],
    )


def solution(mesh):
    placed = (
        P("batch", "seq", None, "head", None),
        P("batch", "seq", None, "head", None),
        P("batch", "seq", None, "head", None),
        P("batch", "seq", None, "head", None),
        P("batch"),
    )
    return jax.shard_map(
        body,
        mesh=mesh,
        in_specs=placed,
        out_specs=(
            P("batch", "seq", None, "head", None),
            P("batch", "seq", None, "head", None),
            P("batch", "seq", None, "head", None),
            P("batch", "seq", None, "head", None),
        ),
        check_vma=False,
    )
```
